32 devices in a mesh: gx: 2 (over y), gy: 4 (over x, core), gz: 4 (over z).
Axes of the slice: x: 2, y: 2, z: 4, core: 2. Of those that a mesh axis runs over, the one named last changes fastest.
Arguments:
- direction: float32 [3, 32, 32, 512], P(None, 'gx', 'gy', 'gz'), may hold values from -6 to 6
- base_flow: bfloat16 [2, 3, 32, 32, 512], P(None, None, 'gx', 'gy', 'gz'), may hold values from -4 to 4
- local_inv: float32 [32, 16], P('gx'), may hold values from -1.5 to 1.5
- couple_in: float32 [4, 16], P('gx'), may hold values from -1.5 to 1.5
- couple_out: float32 [32, 2], P('gx'), may hold values from -4 to 4
- schur_inv: float32 [4, 4], replicated, may hold values from -3 to 3
- plane_x: int32 [8], replicated, may hold values from 0 to 31, as said below
- slot_plane: int32 [8], replicated, may hold values from 0 to 7, each once
- window_inv: float32 [8, 4, 4, 16, 16], P('gx', 'gy', 'gz'), may hold values from -4 to 20
Outputs:
- hess_vec: float32 [3, 32, 32, 512], P(None, 'gx', 'gy', 'gz')
The draws below stay inside these ranges and needn't reach their ends.
Inputs may be any that keep to these rules, and one draw needn't show every extreme that they name: `plane_x`: each plane lies on a streamwise cell of the grid; the planes lie on distinct cells; at most 8 of them lie in the cells of one index d of gx (cells d*16 to d*16 + 15), and some index holds exactly 8.
All inputs are finite; a program needn't handle non-finite values.
Results may differ from the reference program's by a relative error of at most 0.0003.
Values sent between devices are 32-bit elements; how exact they have to be, the bound alone decides.
A program may use at most 64 MiB of HBM per device.

```python
import math
import jax
import jax.numpy as jnp
from jax import lax

CX = 16
CY = 8
WIN = 8
NP = 8
PMAX = 8
NI = 4
CZW = 16
NX = 32
NY = 32
NZ = 512
N_GX = 2
N_GY = 4
N_GZ = 4


def shuffle_cells(device_key):
    return jax.random.permutation(device_key, CX)


def draw_plane_x(key, part):
    start_key, order_key, place_key = jax.random.split(key, 3)
    busiest = jax.random.randint(start_key, (), 0, N_GX)
    plane_order = jax.random.permutation(order_key, NP)
    device_keys = jax.random.split(place_key, N_GX)
    offsets = jax.vmap(shuffle_cells)(device_keys)
    devices = jnp.arange(N_GX, dtype=jnp.int32)[:, None]
    slot_index = jnp.arange(PMAX, dtype=jnp.int32)[None, :]
    shifted = (devices - busiest - 1) % N_GX
    other_rank = PMAX + shifted + slot_index * (N_GX - 1)
    plane_rank = jnp.where(devices == busiest, slot_index, other_rank)
    filled = plane_rank < NP
    plane_id = jnp.where(filled, plane_order[jnp.minimum(plane_rank, NP - 1)], NP)
    cell_x = devices * CX + offsets[:, :PMAX]
    result = jnp.zeros((NP,), jnp.int32)
    return result.at[plane_id.reshape(-1)].set(cell_x.reshape(-1).astype(jnp.int32), mode='drop')


def draw_window_inv(key, part):
    diag_key, rest_key = jax.random.split(key)
    full_shape = (NP, N_GY, N_GZ, CZW, CZW)
    spread_part = jnp.clip(jax.random.normal(rest_key, full_shape, jnp.float32), -4.0, 4.0)
    levels = jnp.exp(jax.random.uniform(diag_key, full_shape, jnp.float32, minval=math.log(4.0), maxval=math.log(16.0)))
    identity_block = jnp.eye(CZW, dtype=jnp.float32)
    return spread_part + identity_block * levels


def shard_levels(stream_key, dims, cuts, low, largest):
    level = 1.0
    for position, shards_of in cuts:
        steps = jax.random.uniform(jax.random.fold_in(jax.random.fold_in(stream_key, 6), position), (shards_of,), jnp.float32, low / len(cuts), largest / len(cuts))
        level = level * jnp.repeat(jnp.exp(steps), dims[position] // shards_of).reshape((-1,) + (1,) * (len(dims) - 1 - position))
    return level


def scatter_about(own_key, extent, width, limit, shards=(), kind=jnp.bfloat16):
    values = width * jax.random.normal(own_key, extent, jnp.float32)
    if shards:
        values = values * shard_levels(own_key, extent, shards, -0.22, 0.18)
    return jnp.clip(values, -limit, limit).astype(kind)


def setup_inputs(seed: int = 0) -> dict:
    splits = jax.random.split(jax.random.key(seed), 10)
    return {
        "direction": scatter_about(splits[0], (3, NX, NY, NZ), 1.0, 6.0, ((1, 2), (2, 4), (3, 4)), jnp.float32),
        "base_flow": scatter_about(splits[1], (2, 3, NX, NY, NZ), 1.0, 4.0, ((2, 2), (3, 4), (4, 4))),
        "local_inv": scatter_about(splits[2], (NX, CX), CX ** -0.5, 1.5, ((0, 2),), jnp.float32),
        "couple_in": scatter_about(splits[3], (NI, CX), CX ** -0.5, 1.5, ((0, 2),), jnp.float32),
        "couple_out": scatter_about(splits[4], (NX, 2), 2 ** -0.5, 4.0, ((0, 2),), jnp.float32),
        "schur_inv": scatter_about(splits[5], (NI, NI), NI ** -0.5, 3.0, (), jnp.float32),
        "plane_x": draw_plane_x(jax.random.fold_in(splits[9], 71), 0),
        "slot_plane": jax.random.permutation(splits[7], NP).astype(jnp.int32),
        "window_inv": draw_window_inv(jax.random.fold_in(splits[9], 71), 0),
    }


time_step = 0.15
high = lax.Precision.HIGHEST


def stencil_x(field):
    length = field.shape[1]
    padded = jnp.pad(field, ((0, 0), (2, 2), (0, 0), (0, 0)))
    near_diff = padded[:, 3:length + 3] - padded[:, 1:length + 1]
    far_diff = padded[:, 4:length + 4] - padded[:, 0:length]
    return (7.0 / 9.0) * near_diff + (1.0 / 36.0) * far_diff


def central_six(field, axis_index):
    def shifted(offset):
        return jnp.roll(field, -offset, axis=axis_index)
    return (45.0 * (shifted(1) - shifted(-1)) - 9.0 * (shifted(2) - shifted(-2)) + (shifted(3) - shifted(-3))) / 60.0


def solve_x(rhs, local_inv, couple_in, couple_out, schur_inv):
    blocks = rhs.reshape(3, N_GX, CX, NY, NZ)
    inverse_blocks = local_inv.reshape(N_GX, CX, CX)
    in_blocks = couple_in.reshape(N_GX, 2, CX)
    out_blocks = couple_out.reshape(N_GX, CX, 2)
    local_part = jnp.einsum('pij,cpjyz->cpiyz', inverse_blocks, blocks, precision=high)
    edge_values = jnp.einsum('pkj,cpjyz->cpkyz', in_blocks, blocks, precision=high).reshape(3, NI, NY, NZ)
    solved = jnp.einsum('mn,cnyz->cmyz', schur_inv, edge_values, precision=high).reshape(3, N_GX, 2, NY, NZ)
    result = local_part + jnp.einsum('pik,cpkyz->cpiyz', out_blocks, solved, precision=high)
    return result.reshape(3, NX, NY, NZ)


def solve_x_adjoint(grad_in, local_inv, couple_in, couple_out, schur_inv):
    blocks = grad_in.reshape(3, N_GX, CX, NY, NZ)
    inverse_blocks = local_inv.reshape(N_GX, CX, CX)
    in_blocks = couple_in.reshape(N_GX, 2, CX)
    out_blocks = couple_out.reshape(N_GX, CX, 2)
    local_part = jnp.einsum('pji,cpjyz->cpiyz', inverse_blocks, blocks, precision=high)
    edge_values = jnp.einsum('pik,cpiyz->cpkyz', out_blocks, blocks, precision=high).reshape(3, NI, NY, NZ)
    solved = jnp.einsum('nm,cnyz->cmyz', schur_inv, edge_values, precision=high).reshape(3, N_GX, 2, NY, NZ)
    result = local_part + jnp.einsum('pki,cpkyz->cpiyz', in_blocks, solved, precision=high)
    return result.reshape(3, NX, NY, NZ)


def observe(state, plane_x, slot_plane, window_inv):
    picked = state[:, plane_x]
    windows = picked.reshape(3, NP, NY, NZ // WIN, WIN).mean(axis=4)
    by_slot = windows[:, slot_plane].reshape(3, NP, N_GY, CY, N_GZ, CZW)
    weighted = jnp.einsum('jgsab,cjgysb->cjgysa', window_inv, by_slot, precision=high).reshape(3, NP, NY, NZ // WIN)
    by_plane = jnp.zeros_like(weighted).at[:, slot_plane].set(weighted)
    expanded = jnp.repeat(by_plane, WIN, axis=3) / WIN
    return jnp.zeros_like(state).at[:, plane_x].add(expanded)


def reference(direction, base_flow, local_inv, couple_in, couple_out, schur_inv, plane_x, slot_plane, window_inv):
    matrices = (local_inv, couple_in, couple_out, schur_inv)

    def tangent(state, step_base):
        velocity = step_base.astype(jnp.float32)
        slope_x = solve_x(stencil_x(state), *matrices)
        slope_y = central_six(state, 2)
        slope_z = central_six(state, 3)
        return state - time_step * (velocity[0] * slope_x + velocity[1] * slope_y + velocity[2] * slope_z)

    def adjoint(state, step_base):
        velocity = step_base.astype(jnp.float32)
        pulled = stencil_x(solve_x_adjoint(velocity[0] * state, *matrices))
        along_y = central_six(velocity[1] * state, 2)
        along_z = central_six(velocity[2] * state, 3)
        return state + time_step * (pulled + along_y + along_z)

    state_one = tangent(direction, base_flow[0])
    state_two = tangent(state_one, base_flow[1])
    adjoint_two = observe(state_two, plane_x, slot_plane, window_inv)
    adjoint_one = adjoint(adjoint_two, base_flow[1]) + observe(state_one, plane_x, slot_plane, window_inv)
    return adjoint(adjoint_one, base_flow[0]) + direction
```

```python
import functools

import jax
import jax.numpy as jnp
from jax import lax
from jax.experimental import pallas as pl
from jax.experimental.pallas import tpu as pltpu
from jax.sharding import PartitionSpec as P

WIN = 8
time_step = 0.15
NEAR = 7.0 / 9.0
FAR = 1.0 / 36.0
C1 = 45.0 / 60.0
C2 = -9.0 / 60.0
C3 = 1.0 / 60.0
MESH = pl.DeviceIdType.MESH
high = lax.Precision.HIGHEST


def weighted(terms):
    chains = [None, None]
    for n, (coef, block) in enumerate(terms):
        part = coef * block
        chains[n % 2] = part if chains[n % 2] is None else chains[n % 2] + part
    return chains[0] if chains[1] is None else chains[0] + chains[1]


def kernel(
    sizes,
    dir_hbm, base_hbm, inv_hbm,
    local_h, in_h, out_h, schur_h, plane_h, slot_h,
    res_ref,
    dir_ref, base_ref, inv_ref, local_s, in_s, out_s, schur_s, plane_s, slot_s, in_v, near_v, near_s, esend, halo, load_sem, table_sem, ts_sem, tr_sem,
    state_one, state_two, force, acc, rhs, obs, prod_y, prod_z, hbuf,
    yside, xrecv, ysend, yrecv, zsend, zrecv, edge, winrecv, lanes_inv, blocks,
    xs_sem, xr_sem, ys_sem, yr_sem, zs_sem, zr_sem, es_sem, er_sem, ws_sem, wr_sem,
):
    n_gx, n_gy, n_gz = sizes
    gx, gy, gz = lax.axis_index("gx"), lax.axis_index("gy"), lax.axis_index("gz")
    comps, cx, cy, cz = dir_ref.shape
    wide = ysend.shape[2]
    loads = [
        pltpu.make_async_copy(src, dst, load_sem.at[n])
        for n, (src, dst) in enumerate((
            (dir_hbm, dir_ref), (in_h, in_s), (schur_h, schur_s), (local_h, local_s),
            (out_h, out_s), (plane_h, plane_s), (slot_h, slot_s),
            (base_hbm, base_ref), (inv_hbm, inv_ref), (in_h, in_v),
        ))
    ]
    owned = inv_ref.shape[0]
    y_next, y_prev = lax.rem(gy + 1, n_gy), lax.rem(gy + n_gy - 1, n_gy)
    z_next, z_prev = lax.rem(gz + 1, n_gz), lax.rem(gz + n_gz - 1, n_gz)

    @pl.when(gx == 0)
    def _():
        xrecv[:, 0] = jnp.zeros(xrecv.shape[:1] + xrecv.shape[2:], jnp.float32)

    @pl.when(gx == n_gx - 1)
    def _():
        xrecv[:, 1] = jnp.zeros(xrecv.shape[:1] + xrecv.shape[2:], jnp.float32)

    barrier = pltpu.get_barrier_semaphore()
    for d in range(1, n_gx):
        pl.semaphore_signal(barrier, device_id={"gx": lax.rem(gx + d, n_gx)}, device_id_type=MESH)
    for q in (y_prev, y_next):
        pl.semaphore_signal(barrier, device_id={"gy": q}, device_id_type=MESH)
    for q in (z_prev, z_next):
        pl.semaphore_signal(barrier, device_id={"gz": q}, device_id_type=MESH)

    for copy in loads:
        copy.start()

    def remote(src, dst, send, recv, where):
        return pltpu.make_async_remote_copy(
            src_ref=src, dst_ref=dst, send_sem=send, recv_sem=recv,
            device_id=where, device_id_type=MESH,
        )

    lane = lax.broadcasted_iota(jnp.int32, (comps, cy, cz), 2)
    sub = lax.broadcasted_iota(jnp.int32, (comps, cy, cz), 1)
    in_group = lane % WIN

    def x_copies(r, src):
        right = remote(src.at[:, cx - 2 : cx], xrecv.at[r, 0], xs_sem.at[r, 0], xr_sem.at[r, 0],
                       {"gx": lax.rem(gx + 1, n_gx)})
        left = remote(src.at[:, 0:2], xrecv.at[r, 1], xs_sem.at[r, 1], xr_sem.at[r, 1],
                      {"gx": lax.rem(gx + n_gx - 1, n_gx)})
        return right, left

    def x_start(copies):
        right, left = copies

        @pl.when(gx < n_gx - 1)
        def _():
            right.start()

        @pl.when(gx > 0)
        def _():
            left.start()

    def x_arrived(copies):
        right, left = copies

        @pl.when(gx > 0)
        def _():
            right.wait_recv()

        @pl.when(gx < n_gx - 1)
        def _():
            left.wait_recv()

    def x_sent(copies):
        right, left = copies

        @pl.when(gx < n_gx - 1)
        def _():
            right.wait_send()

        @pl.when(gx > 0)
        def _():
            left.wait_send()

    def y_copies(r):
        return (
            remote(ysend.at[r, 0], yrecv.at[r, 0], ys_sem.at[r, 0], yr_sem.at[r, 0], {"gy": y_prev}),
            remote(ysend.at[r, 1], yrecv.at[r, 1], ys_sem.at[r, 1], yr_sem.at[r, 1], {"gy": y_next}),
        )

    def z_copies(r):
        return (
            remote(zsend.at[r], zrecv.at[r, 0], zs_sem.at[r, 0], zr_sem.at[r, 0], {"gz": z_prev}),
            remote(zsend.at[r], zrecv.at[r, 1], zs_sem.at[r, 1], zr_sem.at[r, 1], {"gz": z_next}),
        )

    def edge_copies(r):
        return tuple(
            remote(edge.at[r, 0], edge.at[r, d], es_sem.at[r, d], er_sem.at[r, d],
                   {"gx": lax.rem(gx + d, n_gx)})
            for d in range(1, n_gx)
        )

    win_copies = tuple(
        remote(inv_ref, winrecv.at[d - 1], ws_sem.at[d], wr_sem.at[d], {"gx": lax.rem(gx + d, n_gx)})
        for d in range(1, n_gx)
    )

    table_copies = (
        remote(in_v, near_v.at[0], ts_sem.at[0], tr_sem.at[0], {"gx": lax.rem(gx + 1, n_gx)}),
        remote(in_v, near_v.at[1], ts_sem.at[1], tr_sem.at[1], {"gx": lax.rem(gx + n_gx - 1, n_gx)}),
    )
    left_one = jnp.where(gx > 0, 1.0, 0.0)
    right_one = jnp.where(gx < n_gx - 1, 1.0, 0.0)
    left_id, right_id = lax.rem(gx + n_gx - 1, n_gx), lax.rem(gx + 1, n_gx)

    def start(copies):
        for copy in copies:
            copy.start()

    def arrived(copies):
        for copy in copies:
            copy.wait_recv()

    def pack_y(r, src):
        lines = src.reshape(comps * cx * cy, cz)
        for c in range(comps):
            for m in range(wide):
                for side, row in ((0, m), (1, cy - wide + m)):
                    ysend[r, side, m, c] = lines[pl.ds(c * cx * cy + row, cx, stride=cy), :]

    def pack_z(r, src):
        packed = None
        for i in range(cx):
            block = src[:, i]
            turned = block if i == 0 else pltpu.roll(block, WIN * i, 2)
            if packed is None:
                packed = turned
            else:
                packed = jnp.where((lane >= WIN * i - 4) & (lane < WIN * i + 4), turned, packed)
        zsend[r] = packed

    def circular_z(block):
        def diff(k):
            return pltpu.roll(block, cz - k, 2) - pltpu.roll(block, k, 2)

        return C1 * diff(1) + C2 * diff(2) + C3 * diff(3)

    def z_fix(r):
        true = jnp.where(in_group < 4, zrecv[r, 0], zrecv[r, 1])
        delta = true - zsend[r]
        low = jnp.where(in_group >= WIN - 3, delta, 0.0)
        top = jnp.where(in_group < 3, delta, 0.0)
        low_fix = -(C1 * pltpu.roll(low, 1, 2) + C2 * pltpu.roll(low, 2, 2) + C3 * pltpu.roll(low, 3, 2))
        top_fix = (C1 * pltpu.roll(top, cz - 1, 2) + C2 * pltpu.roll(top, cz - 2, 2)
                   + C3 * pltpu.roll(top, cz - 3, 2))
        return jnp.where(in_group < 3, low_fix, 0.0) + jnp.where(in_group >= WIN - 3, top_fix, 0.0)

    def z_fix_of(fix, i):
        turned = fix if i == 0 else pltpu.roll(fix, (cz - WIN * i) % cz, 2)
        return jnp.where((lane < 3) | (lane >= cz - 3), turned, 0.0)

    def fill_sides(r):
        lines = yside.reshape(comps * cx * cy, cz)
        for c in range(comps):
            for m in range(wide):
                for side, row in ((0, m), (1, cy - wide + m)):
                    lines[pl.ds(c * cx * cy + row, cx, stride=cy), :] = yrecv[r, side, m, c]

    def along_y(block, side):
        def diff(k):
            ahead = pltpu.roll(jnp.where(sub < k, side, block), cy - k, 1)
            behind = pltpu.roll(jnp.where(sub >= cy - k, side, block), k, 1)
            return ahead - behind

        return C1 * diff(1) + C2 * diff(2) + C3 * diff(3)

    def stencil_x(src, sides, i):
        def row(n):
            if n < 0:
                return sides[0, :, n + 2]
            if n >= cx:
                return sides[1, :, n - cx]
            return src[:, n]

        return NEAR * (row(i + 1) - row(i - 1)) + FAR * (row(i + 2) - row(i - 2))

    def stencil_inside(src, i):
        total = None
        for offset, coef in ((1, NEAR), (-1, -NEAR), (2, FAR), (-2, -FAR)):
            if 0 <= i + offset < cx:
                part = coef * src[:, i + offset]
                total = part if total is None else total + part
        return total

    def velocity(n, c, i):
        return base_ref[n, c, i].astype(jnp.float32)[None]

    def fold(blocks8):
        level, m = list(blocks8), 1
        while len(level) > 1:
            keep = (lane & m) == 0
            level = [
                jnp.where(keep, a + pltpu.roll(a, cz - m, 2), b + pltpu.roll(b, m, 2))
                for a, b in zip(level[0::2], level[1::2])
            ]
            m *= 2
        return level[0]

    def unfold(block):
        level, m = [block], WIN // 2
        while m >= 1:
            keep = (lane & m) == 0
            wider = []
            for t in level:
                wider.append(jnp.where(keep, t, pltpu.roll(t, m, 2)))
                wider.append(jnp.where(keep, pltpu.roll(t, cz - m, 2), t))
            level = wider
            m //= 2
        return level

    def observe(src, dst):
        for g in range(cx // WIN):
            sums = fold([src[:, g * WIN + k] for k in range(WIN)])
            mixed = lax.dot_general(
                sums.reshape(comps * cy, cz), blocks[g], (((1,), (1,)), ((), ())),
                precision=high, preferred_element_type=jnp.float32,
            ).reshape(comps, cy, cz)
            for k, t in enumerate(unfold(mixed)):
                dst[:, g * WIN + k] = t

    def build_blocks():
        count = inv_ref.shape[2]
        spread = (
            lax.broadcasted_iota(jnp.int32, (count, cz), 1) // WIN
            == lax.broadcasted_iota(jnp.int32, (count, cz), 0)
        ).astype(jnp.float32)
        for d in range(n_gx):
            source = inv_ref[...] if d == 0 else winrecv[d - 1]
            lanes_inv[d * owned : (d + 1) * owned] = jnp.dot(
                source.reshape(owned * count, count), spread,
                precision=high, preferred_element_type=jnp.float32,
            ).reshape(owned, count, cz) * (1.0 / (WIN * WIN))
        blocks[...] = jnp.zeros(blocks.shape, jnp.float32)
        row = lax.broadcasted_iota(jnp.int32, (WIN, cz), 0)
        col = lax.broadcasted_iota(jnp.int32, (WIN, cz), 1) % WIN

        def add_slot(j, carry):
            owner = lax.rem(gx + n_gx - j // owned, n_gx)
            cell = plane_s[slot_s[owner * owned + j % owned]] - gx * cx
            for g in range(cx // WIN):
                here = (row == cell - g * WIN) & (col == cell - g * WIN)
                for s in range(count):
                    line = jnp.broadcast_to(lanes_inv[j, s : s + 1, :], (WIN, cz))
                    blocks[g, s * WIN : (s + 1) * WIN, :] += jnp.where(here, line, 0.0)
            return carry

        lax.fori_loop(0, n_gx * owned, add_slot, 0)

    def interface(r, block, m, transposed):
        terms = []
        for d in range(n_gx):
            owner = lax.rem(gx + n_gx - d, n_gx)
            for k in range(2):
                n, own = 2 * owner + k, 2 * block + m
                coef = schur_s[n, own] if transposed else schur_s[own, n]
                terms.append((coef, edge[r, d, k]))
        return weighted(terms)

    def early_copies(r):
        return tuple(
            remote(esend.at[d], edge.at[r, d], es_sem.at[r, d], er_sem.at[r, d],
                   {"gx": lax.rem(gx + d, n_gx)})
            for d in range(1, n_gx)
        )

    def early_shares(r, src):
        for i in range(cx):
            rhs[:, i] = stencil_inside(src, i)
        below = (NEAR * src[:, 0] + FAR * src[:, 1], FAR * src[:, 0])
        above = (-(NEAR * src[:, cx - 1] + FAR * src[:, cx - 2]), -FAR * src[:, cx - 1])
        parts = []
        for k in range(2):
            parts.append((2 * gx + k, weighted([(in_s[k, j], rhs[:, j]) for j in range(cx)])))
            parts.append((2 * right_id + k, right_one * (
                near_s[1, k, 0] * above[0] + near_s[1, k, 1] * above[1])))
            parts.append((2 * left_id + k, left_one * (
                near_s[0, k, cx - 1] * below[0] + near_s[0, k, cx - 2] * below[1])))
        for d in tuple(range(1, n_gx)) + (0,):
            owner = lax.rem(gx + d, n_gx)
            for m in range(2):
                share = weighted([(schur_s[2 * owner + m, n], part) for n, part in parts])
                if d == 0:
                    edge[r, 0, m] = share
                else:
                    esend[d, m] = share

    sent = []

    def tangent(r, n, src, dst, first, shadow):
        xc, yc, zc = x_copies(r, src), y_copies(r), z_copies(r)
        ec = edge_copies(r) if first else early_copies(r)
        if first:
            loads[0].wait()
        else:
            x_start(xc)
        pack_z(r, src)
        if not first:
            start(zc)
        pack_y(r, src)
        if first:
            pl.semaphore_wait(barrier, n_gx - 1 + 4)
            x_start(xc)
            start(zc)
        start(yc)
        if not first:
            early_shares(r, src)
            start(ec)
        sent.append((xc, yc + zc + ec))
        if first:
            for copy in loads[1:]:
                copy.wait()
            start(table_copies)
        for i in range(cx):
            block = src[:, i]
            acc[:, i] = block - time_step * (velocity(n, 2, i) * circular_z(block))
        x_arrived(xc)
        for i in range(cx) if first else (0, 1, cx - 2, cx - 1):
            rhs[:, i] = stencil_x(src, xrecv.at[r], i)
        if first:
            for k in range(2):
                edge[r, 0, k] = weighted([(in_s[k, j], rhs[:, j]) for j in range(cx)])
            start(ec)
            start(win_copies)
        for i in range(cx):
            solved = weighted([(local_s[i, j], rhs[:, j]) for j in range(cx)])
            acc[:, i] -= time_step * (velocity(n, 0, i) * solved)
        if first:
            arrived(table_copies)
            table = pltpu.make_async_copy(near_v, near_s, table_sem.at[0])
            table.start()
            table.wait()
        shadow()
        arrived(yc)
        fill_sides(r)
        for i in range(cx):
            acc[:, i] -= time_step * (velocity(n, 1, i) * along_y(src[:, i], yside[:, i]))
        arrived(zc)
        fix = z_fix(r)
        arrived(ec)
        if first:
            values = [interface(r, gx, m, False) for m in range(2)]
        else:
            values = [weighted([(1.0, edge[r, d, m]) for d in range(n_gx)]) for m in range(2)]
        for i in range(cx):
            pulled = out_s[0, i] * values[0] + out_s[1, i] * values[1]
            dst[:, i] = acc[:, i] - time_step * (
                velocity(n, 0, i) * pulled + velocity(n, 2, i) * z_fix_of(fix, i)
            )

    def adjoint(r, n, src, dst, extra):
        xc, yc, zc, ec = x_copies(r, hbuf.at[r - 2]), y_copies(r), z_copies(r), edge_copies(r)
        sent.append((xc, yc + zc + ec))
        held = hbuf.at[r - 2]
        for i in range(cx):
            prod_z[:, i] = velocity(n, 2, i) * src[:, i]
        pack_z(r, prod_z)
        start(zc)
        for i in range(cx):
            prod_y[:, i] = velocity(n, 1, i) * src[:, i]
        pack_y(r, prod_y)
        start(yc)
        for i in range(cx):
            rhs[:, i] = velocity(n, 0, i) * src[:, i]
        for k in range(2):
            edge[r, 0, k] = weighted([(out_s[k, i], rhs[:, i]) for i in range(cx)])
        start(ec)
        order = (0, 1, cx - 2, cx - 1) + tuple(range(2, cx - 2))
        for place, i in enumerate(order):
            held[:, i] = weighted([(local_s[j, i], rhs[:, j]) for j in range(cx)])
            if place == 3:
                x_start(xc)
        for i in range(cx):
            total = src[:, i] + time_step * circular_z(prod_z[:, i])
            acc[:, i] = total if extra is None else total + extra[:, i]
        arrived(ec)
        values = [interface(r, gx, m, True) for m in range(2)]
        lower = [left_one * interface(r, left_id, m, True) for m in range(2)]
        upper = [right_one * interface(r, right_id, m, True) for m in range(2)]
        for i in range(cx):
            rhs[:, i] = held[:, i] + (in_s[0, i] * values[0] + in_s[1, i] * values[1])
        for i in range(2, cx - 2):
            acc[:, i] += time_step * stencil_x(rhs, halo, i)
        x_arrived(xc)
        for n in range(2):
            halo[0, :, n] = xrecv[r, 0, :, n] + (
                near_s[0, 0, cx - 2 + n] * lower[0] + near_s[0, 1, cx - 2 + n] * lower[1])
            halo[1, :, n] = xrecv[r, 1, :, n] + (
                near_s[1, 0, n] * upper[0] + near_s[1, 1, n] * upper[1])
        for i in (0, 1, cx - 2, cx - 1):
            acc[:, i] += time_step * stencil_x(rhs, halo, i)
        arrived(yc)
        fill_sides(r)
        for i in range(cx):
            acc[:, i] += time_step * along_y(prod_y[:, i], yside[:, i])
        arrived(zc)
        fix = z_fix(r)
        for i in range(cx):
            dst[:, i] = acc[:, i] + time_step * z_fix_of(fix, i)

    def nothing():
        pass

    def observe_one():
        arrived(win_copies)
        build_blocks()
        observe(state_one, obs)

    tangent(0, 0, dir_ref, state_one, True, nothing)
    tangent(1, 1, state_one, state_two, False, observe_one)
    observe(state_two, force)
    adjoint(2, 1, force, state_two, obs)
    adjoint(3, 0, state_two, res_ref, None)
    for xc, rest in sent:
        x_sent(xc)
        for copy in rest:
            copy.wait_send()
    for copy in win_copies + table_copies:
        copy.wait_send()


def pair_kernel(
    sizes,
    dir_hbm, base_hbm, inv_hbm,
    local_h, in_h, out_h, schur_h, plane_h, slot_h,
    res_ref,
    dir_ref, base_ref, inv_ref, local_s, in_s, out_s, schur_s, plane_s, slot_s, in_v, near_v, near_s,
    state_one, state_two, force, acc, rhs, obs, prod, held, yside, vel, uz_pack,
    xsend, xrecv, ysend, yrecv, zsend, zrecv, winrecv, lanes_inv, blocks,
    load_sem, side_sem, xs_sem, xr_sem, ys_sem, yr_sem, zs_sem, zr_sem,
):
    n_gx, n_gy, n_gz = sizes
    gx, gy, gz = lax.axis_index("gx"), lax.axis_index("gy"), lax.axis_index("gz")
    comps, cx, cy, cz = dir_ref.shape
    wide = ysend.shape[2]
    owned = inv_ref.shape[0]
    other = 1 - gx
    y_next, y_prev = lax.rem(gy + 1, n_gy), lax.rem(gy + n_gy - 1, n_gy)
    z_next, z_prev = lax.rem(gz + 1, n_gz), lax.rem(gz + n_gz - 1, n_gz)
    first = gx == 0
    near_row = jnp.where(first, cx - 2, 0)
    their_row = jnp.where(first, 0, cx - 2)

    barrier = pltpu.get_barrier_semaphore()
    for q in (z_prev, z_next):
        pl.semaphore_signal(barrier, device_id={"gz": q}, device_id_type=MESH)
    pl.semaphore_signal(barrier, device_id={"gx": other}, device_id_type=MESH)
    for q in (y_prev, y_next):
        pl.semaphore_signal(barrier, device_id={"gy": q}, device_id_type=MESH)

    loads = [
        pltpu.make_async_copy(src, dst, load_sem.at[n])
        for n, (src, dst) in enumerate((
            (dir_hbm, dir_ref), (in_h, in_s), (in_h, in_v), (base_hbm, base_ref), (local_h, local_s),
            (schur_h, schur_s), (out_h, out_s), (plane_h, plane_s), (slot_h, slot_s), (inv_hbm, inv_ref),
        ))
    ]
    for copy in loads:
        copy.start()

    def remote(src, dst, send, recv, where):
        return pltpu.make_async_remote_copy(
            src_ref=src, dst_ref=dst, send_sem=send, recv_sem=recv,
            device_id=where, device_id_type=MESH,
        )

    def x_copy(r):
        return remote(xsend.at[r], xrecv.at[r], xs_sem.at[r % 2], xr_sem.at[r % 2], {"gx": other})

    def y_copies(r):
        return tuple(
            remote(ysend.at[r, d], yrecv.at[r, d], ys_sem.at[r % 2], yr_sem.at[r % 2], {"gy": q})
            for d, q in enumerate((y_prev, y_next))
        )

    def z_copies(r):
        return tuple(
            remote(zsend.at[r], zrecv.at[r, d], zs_sem.at[r % 2], zr_sem.at[r % 2], {"gz": q})
            for d, q in enumerate((z_prev, z_next))
        )

    def y_both(r):
        return remote(yrecv.at[r], yrecv.at[r], ys_sem.at[r % 2], yr_sem.at[r % 2], {"gy": y_next})

    def z_both(r):
        return remote(zrecv.at[r], zrecv.at[r], zs_sem.at[r % 2], zr_sem.at[r % 2], {"gz": z_next})

    def settle(r):
        if r >= 0:
            x_copy(r).wait_send()
            y_both(r).wait_send()
            z_both(r).wait_send()

    win_copy = remote(inv_ref, winrecv, side_sem.at[0], side_sem.at[1], {"gx": other})
    table_copy = remote(in_v, near_v, side_sem.at[2], side_sem.at[3], {"gx": other})

    lane = lax.broadcasted_iota(jnp.int32, (cy, cz), 1)
    in_group = lane % WIN
    cell_of = ((lane + WIN // 2) // WIN) % cx
    near_edge = (lane < 3) | (lane >= cz - 3)
    left, right = in_group < 3, in_group >= WIN - 3
    ahead = in_group < WIN // 2

    def packed(block_of):
        total = None
        for i in range(cx):
            block = block_of(i)
            turned = block if i == 0 else pltpu.roll(block, WIN * i, block.ndim - 1)
            total = turned if total is None else jnp.where(cell_of == i, turned, total)
        return total

    def unpacked(block, i):
        turned = block if i == 0 else pltpu.roll(block, (cz - WIN * i) % cz, 2)
        return jnp.where(near_edge, turned, 0.0)

    def pack_y(r, src):
        lines = src.reshape(comps * cx * cy, cz)
        for side, start in ((0, 0), (1, cy - wide)):
            for m in range(wide):
                for c in range(comps):
                    ysend[r, side, m, c] = lines[pl.ds(c * cx * cy + start + m, cx, stride=cy), :]

    def circular(block, axis):
        size = block.shape[axis]

        def diff(k):
            return pltpu.roll(block, size - k, axis) - pltpu.roll(block, k, axis)

        return C1 * diff(1) + C2 * diff(2) + C3 * diff(3)

    def z_fix(r):
        delta = jnp.where(ahead, zrecv[r, 0], zrecv[r, 1]) - zsend[r]
        low = jnp.where(right, delta, 0.0)
        top = jnp.where(left, delta, 0.0)
        low_fix = -(C1 * pltpu.roll(low, 1, 2) + C2 * pltpu.roll(low, 2, 2) + C3 * pltpu.roll(low, 3, 2))
        top_fix = (C1 * pltpu.roll(top, cz - 1, 2) + C2 * pltpu.roll(top, cz - 2, 2)
                   + C3 * pltpu.roll(top, cz - 3, 2))
        return jnp.where(left, low_fix, jnp.where(right, top_fix, 0.0))

    def y_fix(r):
        lines = yside.reshape(comps * cx * cy, cz)
        for c in range(comps):
            def put(row, value):
                lines[pl.ds(c * cx * cy + row, cx, stride=cy), :] = value

            d0, d1, d2 = (yrecv[r, 0, m, c] - ysend[r, 0, m, c] for m in range(3))
            put(cy - 1, C1 * d0 + C2 * d1 + C3 * d2)
            put(cy - 2, C2 * d0 + C3 * d1)
            put(cy - 3, C3 * d0)
            d0, d1, d2 = (yrecv[r, 1, m, c] - ysend[r, 1, m, c] for m in range(3))
            put(0, -(C1 * d2 + C2 * d1 + C3 * d0))
            put(1, -(C2 * d2 + C3 * d1))
            put(2, -(C3 * d2))

    def stencil_inside(row, i):
        total = None
        for step, coef in ((1, NEAR), (2, FAR)):
            up, down = i + step < cx, i - step >= 0
            if up and down:
                part = coef * (row(i + step) - row(i - step))
            elif up:
                part = coef * row(i + step)
            elif down:
                part = -coef * row(i - step)
            else:
                continue
            total = part if total is None else total + part
        return total

    def rows_of(ref):
        return lambda i: ref[:, i]

    def across(pair, to_first):
        low, high = pair
        upper = (FAR * low, NEAR * low + FAR * high)
        lower = (-(NEAR * high + FAR * low), -FAR * high)
        return tuple(jnp.where(to_first, u, d) for u, d in zip(upper, lower))

    def fold(blocks8):
        level, m = list(blocks8), 1
        while len(level) > 1:
            keep = (lane & m) == 0
            level = [
                jnp.where(keep, a + pltpu.roll(a, cz - m, 2), b + pltpu.roll(b, m, 2))
                for a, b in zip(level[0::2], level[1::2])
            ]
            m *= 2
        return level[0]

    def unfold(block):
        level, m = [block], WIN // 2
        while m >= 1:
            keep = (lane & m) == 0
            wider = []
            for t in level:
                wider.append(jnp.where(keep, t, pltpu.roll(t, m, 2)))
                wider.append(jnp.where(keep, pltpu.roll(t, cz - m, 2), t))
            level = wider
            m //= 2
        return level

    def observe(src, dst):
        for g in range(cx // WIN):
            sums = fold([src[:, g * WIN + k] for k in range(WIN)])
            mixed = lax.dot_general(
                sums.reshape(comps * cy, cz), blocks[g], (((1,), (1,)), ((), ())),
                precision=high, preferred_element_type=jnp.float32,
            ).reshape(comps, cy, cz)
            for k, t in enumerate(unfold(mixed)):
                dst[:, g * WIN + k] = t

    def build_blocks():
        count = inv_ref.shape[2]
        spread = (
            lax.broadcasted_iota(jnp.int32, (count, cz), 1) // WIN
            == lax.broadcasted_iota(jnp.int32, (count, cz), 0)
        ).astype(jnp.float32)
        for d, source in enumerate((inv_ref, winrecv)):
            lanes_inv[d * owned : (d + 1) * owned] = jnp.dot(
                source[...].reshape(owned * count, count), spread,
                precision=high, preferred_element_type=jnp.float32,
            ).reshape(owned, count, cz) * (1.0 / (WIN * WIN))
        blocks[...] = jnp.zeros(blocks.shape, jnp.float32)
        row = lax.broadcasted_iota(jnp.int32, (WIN, cz), 0)
        col = lax.broadcasted_iota(jnp.int32, (WIN, cz), 1) % WIN

        def add_slot(j, carry):
            owner = jnp.where(j < owned, gx, other)
            cell = plane_s[slot_s[owner * owned + j % owned]] - gx * cx
            for g in range(cx // WIN):
                here = (row == cell - g * WIN) & (col == cell - g * WIN)
                for s in range(count):
                    line = jnp.broadcast_to(lanes_inv[j, s : s + 1, :], (WIN, cz))
                    blocks[g, s * WIN : (s + 1) * WIN, :] += jnp.where(here, line, 0.0)
            return carry

        lax.fori_loop(0, n_gx * owned, add_slot, 0)

    def start(copies):
        for copy in copies:
            copy.start()

    def tangent(r, n, src, dst, edge, shadow):
        settle(r - 2)
        zsend[r] = edge
        if r:
            start(z_copies(r))
        pack_y(r, src)
        if not r:
            pl.semaphore_wait(barrier, n_gx - 1 + 4)
            start(z_copies(r))
        start(y_copies(r))
        ours = src[:, pl.ds(near_row, 2)]
        for k in range(2):
            xsend[r, k] = ours[:, k]
        if not r:
            loads[2].wait()
            table_copy.start()
            loads[1].wait()
        for i in range(cx):
            rhs[:, i] = stencil_inside(rows_of(src), i)
        for k in range(2):
            xsend[r, 2 + k] = weighted([(in_s[k, j], rhs[:, j]) for j in range(cx)])
        x_copy(r).start()
        if not r:
            for copy in loads[3:]:
                copy.wait()
            win_copy.start()
            for m in range(2):
                for c in range(comps):
                    for i in range(cx):
                        vel[m, c, i] = time_step * base_ref[m, c, i].astype(jnp.float32)
                uz_pack[m] = packed(lambda i: vel[m, 2, i])
            yside[...] = jnp.zeros(yside.shape, jnp.float32)
        for i in range(cx):
            block = src[:, i]
            solved = weighted([(local_s[i, j], rhs[:, j]) for j in range(cx)])
            acc[:, i] = block - (
                vel[n, 2, i] * circular(block, 2) + vel[n, 1, i] * circular(block, 1) + vel[n, 0, i] * solved)
        shadow()
        x_copy(r).wait_recv()
        pair = xrecv[r, 0], xrecv[r, 1]
        halo = across(pair, first)
        own = [
            xsend[r, 2 + k] + in_s[k, near_row] * halo[0] + in_s[k, near_row + 1] * halo[1] for k in range(2)
        ]
        away = across((xsend[r, 0], xsend[r, 1]), gx != 0)
        theirs = [
            xrecv[r, 2 + k] + near_s[k, their_row] * away[0] + near_s[k, their_row + 1] * away[1]
            for k in range(2)
        ]
        values = [
            weighted([(schur_s[2 * gx + m, 2 * gx + k], own[k]) for k in range(2)]
                     + [(schur_s[2 * gx + m, 2 * other + k], theirs[k]) for k in range(2)])
            for m in range(2)
        ]
        for i in range(cx):
            acc[:, i] -= vel[n, 0, i] * weighted([
                (local_s[i, near_row], halo[0]), (local_s[i, near_row + 1], halo[1]),
                (out_s[0, i], values[0]), (out_s[1, i], values[1])])
        y_both(r).wait_recv()
        y_fix(r)
        for i in range(cx):
            acc[:, i] -= vel[n, 1, i] * yside[:, i]
        before = packed(rows_of(acc))
        z_both(r).wait_recv()
        fix = uz_pack[n] * z_fix(r)
        after = before - fix

        def finish():
            for i in range(cx):
                dst[:, i] = acc[:, i] - unpacked(fix, i)

        return after, finish

    def adjoint(r, n, src, dst, edge, finish_src, extra):
        settle(r - 2)
        zsend[r] = uz_pack[n] * edge
        start(z_copies(r))
        finish_src()
        for i in range(cx):
            prod[:, i] = vel[n, 1, i] * src[:, i]
        pack_y(r, prod)
        start(y_copies(r))
        for i in range(cx):
            rhs[:, i] = vel[n, 0, i] * src[:, i]
        for k in range(2):
            xsend[r, k] = weighted([(local_s[j, near_row + k], rhs[:, j]) for j in range(cx)])
            xsend[r, 2 + k] = weighted([(out_s[k, j], rhs[:, j]) for j in range(cx)])
        x_copy(r).start()
        for i in range(cx):
            held[:, i] = weighted([(local_s[j, i], rhs[:, j]) for j in range(cx)])
        for i in range(cx):
            total = src[:, i] + circular(vel[n, 2, i] * src[:, i], 2) + circular(prod[:, i], 1)
            if extra is not None:
                total = total + extra[:, i]
            acc[:, i] = total + stencil_inside(rows_of(held), i)
        x_copy(r).wait_recv()

        def solved(block):
            return [
                weighted([(schur_s[2 * gx + k, 2 * block + m], xsend[r, 2 + k]) for k in range(2)]
                         + [(schur_s[2 * other + k, 2 * block + m], xrecv[r, 2 + k]) for k in range(2)])
                for m in range(2)
            ]

        own, theirs = solved(gx), solved(other)
        halo = across([
            xrecv[r, k] + near_s[0, their_row + k] * theirs[0] + near_s[1, their_row + k] * theirs[1]
            for k in range(2)
        ], first)
        for i in range(cx):
            acc[:, i] += weighted([
                (stencil_inside(lambda j, m=m: in_s[m, j], i), own[m]) for m in range(2)])
        for k in range(2):
            acc[:, near_row + k] += halo[k]
        y_both(r).wait_recv()
        y_fix(r)
        for i in range(cx):
            acc[:, i] += yside[:, i]
        before = packed(rows_of(acc))
        z_both(r).wait_recv()
        fix = z_fix(r)
        after = before + fix

        def finish():
            for i in range(cx):
                dst[:, i] = acc[:, i] + unpacked(fix, i)

        return after, finish

    def table():
        table_copy.wait_recv()
        copy = pltpu.make_async_copy(near_v, near_s, load_sem.at[0])
        copy.start()
        copy.wait()

    def observe_one():
        win_copy.wait_recv()
        build_blocks()
        observe(state_one, obs)

    loads[0].wait()
    edge, finish = tangent(0, 0, dir_ref, state_one, packed(rows_of(dir_ref)), table)
    finish()
    edge, finish = tangent(1, 1, state_one, state_two, edge, observe_one)
    finish()
    observe(state_two, force)
    edge, finish = adjoint(2, 1, force, state_two, packed(rows_of(force)), lambda: None, obs)
    edge, finish = adjoint(3, 0, state_two, res_ref, edge, finish, None)
    finish()
    settle(2)
    settle(3)
    win_copy.wait_send()
    table_copy.wait_send()


def solution(mesh):
    sizes = tuple(mesh.shape[name] for name in ("gx", "gy", "gz"))

    def local(direction, base_flow, local_inv, couple_in, couple_out, schur_inv,
              plane_x, slot_plane, window_inv):
        n_gx = sizes[0]
        comps, cx, cy, cz = direction.shape
        owned, count = window_inv.shape[0], window_inv.shape[3]
        wide = 3
        field = pltpu.VMEM(direction.shape, jnp.float32)

        def held(*shape):
            return pltpu.VMEM(shape, jnp.float32)

        sems = pltpu.SemaphoreType.DMA
        vmem = pl.BlockSpec(memory_space=pltpu.VMEM)
        kept = functools.partial(pltpu.with_memory_space_constraint, memory_space=pltpu.HBM)
        hbm = pl.BlockSpec(memory_space=pltpu.HBM)
        tables = (local_inv, couple_in, couple_out.T, schur_inv, plane_x, slot_plane)
        operands = tuple(map(kept, (direction, base_flow, window_inv.reshape(owned, count, count)) + tables))
        call = functools.partial(
            pl.pallas_call,
            out_shape=jax.ShapeDtypeStruct(direction.shape, jnp.float32),
            in_specs=[hbm] * 9,
            out_specs=vmem,
            compiler_params=pltpu.CompilerParams(collective_id=0, has_side_effects=True, vmem_limit_bytes=16 * 2**20),
        )
        loaded = [
            field, pltpu.VMEM(base_flow.shape, base_flow.dtype), held(owned, count, count),
        ] + [pltpu.SMEM(t.shape, t.dtype) for t in tables]
        if n_gx == 2:
            pulled = call(
                functools.partial(pair_kernel, sizes),
                scratch_shapes=loaded + [
                    held(2, cx), held(2, cx), pltpu.SMEM((2, cx), jnp.float32),
                ] + [field] * 9 + [
                    held(*base_flow.shape), held(2, cy, cz),
                    held(4, 4, comps, cy, cz), held(4, 4, comps, cy, cz),
                    held(4, 2, wide, comps, cx, cz), held(4, 2, wide, comps, cx, cz),
                    held(4, comps, cy, cz), held(4, 2, comps, cy, cz),
                    held(owned, count, count), held(n_gx * owned, count, cz), held(cx // WIN, count * WIN, cz),
                    sems((10,)), sems((4,)),
                ] + [sems((2,))] * 6,
            )(*operands)
            return pulled + direction
        pulled = call(
            functools.partial(kernel, sizes),
            scratch_shapes=loaded + [
                held(2, cx), held(2, 2, cx), pltpu.SMEM((2, 2, cx), jnp.float32),
                held(n_gx, 2, comps, cy, cz), held(2, comps, 2, cy, cz),
                sems((10,)), sems((1,)), sems((2,)), sems((2,)),
            ] + [field] * 8 + [
                held(2, comps, cx, cy, cz),
                field,
                held(4, 2, comps, 2, cy, cz),
                held(4, 2, wide, comps, cx, cz),
                held(4, 2, wide, comps, cx, cz),
                held(4, comps, cy, cz),
                held(4, 2, comps, cy, cz),
                held(4, n_gx, 2, comps, cy, cz),
                held(n_gx - 1, owned, count, count),
                held(n_gx * owned, count, cz),
                held(cx // WIN, count * WIN, cz),
                sems((4, 2)), sems((4, 2)), sems((4, 2)), sems((4, 2)), sems((4, 2)), sems((4, 2)),
                sems((4, n_gx)), sems((4, n_gx)), sems((n_gx,)), sems((n_gx,)),
            ],
        )(*operands)
        return pulled + direction

    return jax.shard_map(
        local,
        mesh=mesh,
        in_specs=(
            P(None, "gx", "gy", "gz"),
            P(None, None, "gx", "gy", "gz"),
            P("gx", None),
            P("gx", None),
            P("gx", None),
            P(),
            P(),
            P(),
            P("gx", "gy", "gz", None, None),
        ),
        out_specs=P(None, "gx", "gy", "gz"),
        check_vma=False,
    )
```

```python
import functools

import jax
import jax.numpy as jnp
from jax import lax
from jax.experimental import pallas as pl
from jax.experimental.pallas import tpu as pltpu
from jax.sharding import PartitionSpec as P

WIN = 8
time_step = 0.15
NEAR = 7.0 / 9.0
FAR = 1.0 / 36.0
C1 = 45.0 / 60.0
C2 = -9.0 / 60.0
C3 = 1.0 / 60.0
MESH = pl.DeviceIdType.MESH
high = lax.Precision.HIGHEST


def weighted(terms):
    chains = [None, None]
    for n, (coef, block) in enumerate(terms):
        part = coef * block
        chains[n % 2] = part if chains[n % 2] is None else chains[n % 2] + part
    return chains[0] if chains[1] is None else chains[0] + chains[1]


def kernel(
    sizes,
    dir_hbm, base_hbm, inv_hbm,
    local_h, in_h, out_h, schur_h, plane_h, slot_h,
    res_ref,
    dir_ref, base_ref, inv_ref, local_s, in_s, out_s, schur_s, plane_s, slot_s, in_v, near_v, near_s, esend, halo, load_sem, table_sem, ts_sem, tr_sem,
    state_one, state_two, force, acc, rhs, obs, prod_y, prod_z, hbuf,
    yside, xrecv, ysend, yrecv, zsend, zrecv, edge, winrecv, lanes_inv, blocks,
    xs_sem, xr_sem, ys_sem, yr_sem, zs_sem, zr_sem, es_sem, er_sem, ws_sem, wr_sem,
):
    n_gx, n_gy, n_gz = sizes
    gx, gy, gz = lax.axis_index("gx"), lax.axis_index("gy"), lax.axis_index("gz")
    comps, cx, cy, cz = dir_ref.shape
    wide = ysend.shape[2]
    loads = [
        pltpu.make_async_copy(src, dst, load_sem.at[n])
        for n, (src, dst) in enumerate((
            (dir_hbm, dir_ref), (in_h, in_s), (schur_h, schur_s), (local_h, local_s),
            (out_h, out_s), (plane_h, plane_s), (slot_h, slot_s),
            (base_hbm, base_ref), (inv_hbm, inv_ref), (in_h, in_v),
        ))
    ]
    owned = inv_ref.shape[0]
    y_next, y_prev = lax.rem(gy + 1, n_gy), lax.rem(gy + n_gy - 1, n_gy)
    z_next, z_prev = lax.rem(gz + 1, n_gz), lax.rem(gz + n_gz - 1, n_gz)

    @pl.when(gx == 0)
    def _():
        xrecv[:, 0] = jnp.zeros(xrecv.shape[:1] + xrecv.shape[2:], jnp.float32)

    @pl.when(gx == n_gx - 1)
    def _():
        xrecv[:, 1] = jnp.zeros(xrecv.shape[:1] + xrecv.shape[2:], jnp.float32)

    barrier = pltpu.get_barrier_semaphore()
    for d in range(1, n_gx):
        pl.semaphore_signal(barrier, device_id={"gx": lax.rem(gx + d, n_gx)}, device_id_type=MESH)
    for q in (y_prev, y_next):
        pl.semaphore_signal(barrier, device_id={"gy": q}, device_id_type=MESH)
    for q in (z_prev, z_next):
        pl.semaphore_signal(barrier, device_id={"gz": q}, device_id_type=MESH)

    for copy in loads:
        copy.start()

    def remote(src, dst, send, recv, where):
        return pltpu.make_async_remote_copy(
            src_ref=src, dst_ref=dst, send_sem=send, recv_sem=recv,
            device_id=where, device_id_type=MESH,
        )

    lane = lax.broadcasted_iota(jnp.int32, (comps, cy, cz), 2)
    sub = lax.broadcasted_iota(jnp.int32, (comps, cy, cz), 1)
    in_group = lane % WIN

    def x_copies(r, src):
        right = remote(src.at[:, cx - 2 : cx], xrecv.at[r, 0], xs_sem.at[r, 0], xr_sem.at[r, 0],
                       {"gx": lax.rem(gx + 1, n_gx)})
        left = remote(src.at[:, 0:2], xrecv.at[r, 1], xs_sem.at[r, 1], xr_sem.at[r, 1],
                      {"gx": lax.rem(gx + n_gx - 1, n_gx)})
        return right, left

    def x_start(copies):
        right, left = copies

        @pl.when(gx < n_gx - 1)
        def _():
            right.start()

        @pl.when(gx > 0)
        def _():
            left.start()

    def x_arrived(copies):
        right, left = copies

        @pl.when(gx > 0)
        def _():
            right.wait_recv()

        @pl.when(gx < n_gx - 1)
        def _():
            left.wait_recv()

    def x_sent(copies):
        right, left = copies

        @pl.when(gx < n_gx - 1)
        def _():
            right.wait_send()

        @pl.when(gx > 0)
        def _():
            left.wait_send()

    def y_copies(r):
        return (
            remote(ysend.at[r, 0], yrecv.at[r, 0], ys_sem.at[r, 0], yr_sem.at[r, 0], {"gy": y_prev}),
            remote(ysend.at[r, 1], yrecv.at[r, 1], ys_sem.at[r, 1], yr_sem.at[r, 1], {"gy": y_next}),
        )

    def z_copies(r):
        return (
            remote(zsend.at[r], zrecv.at[r, 0], zs_sem.at[r, 0], zr_sem.at[r, 0], {"gz": z_prev}),
            remote(zsend.at[r], zrecv.at[r, 1], zs_sem.at[r, 1], zr_sem.at[r, 1], {"gz": z_next}),
        )

    def edge_copies(r):
        return tuple(
            remote(edge.at[r, 0], edge.at[r, d], es_sem.at[r, d], er_sem.at[r, d],
                   {"gx": lax.rem(gx + d, n_gx)})
            for d in range(1, n_gx)
        )

    win_copies = tuple(
        remote(inv_ref, winrecv.at[d - 1], ws_sem.at[d], wr_sem.at[d], {"gx": lax.rem(gx + d, n_gx)})
        for d in range(1, n_gx)
    )

    table_copies = (
        remote(in_v, near_v.at[0], ts_sem.at[0], tr_sem.at[0], {"gx": lax.rem(gx + 1, n_gx)}),
        remote(in_v, near_v.at[1], ts_sem.at[1], tr_sem.at[1], {"gx": lax.rem(gx + n_gx - 1, n_gx)}),
    )
    left_one = jnp.where(gx > 0, 1.0, 0.0)
    right_one = jnp.where(gx < n_gx - 1, 1.0, 0.0)
    left_id, right_id = lax.rem(gx + n_gx - 1, n_gx), lax.rem(gx + 1, n_gx)

    def start(copies):
        for copy in copies:
            copy.start()

    def arrived(copies):
        for copy in copies:
            copy.wait_recv()

    def pack_y(r, src):
        lines = src.reshape(comps * cx * cy, cz)
        for c in range(comps):
            for m in range(wide):
                for side, row in ((0, m), (1, cy - wide + m)):
                    ysend[r, side, m, c] = lines[pl.ds(c * cx * cy + row, cx, stride=cy), :]

    def pack_z(r, src):
        packed = None
        for i in range(cx):
            block = src[:, i]
            turned = block if i == 0 else pltpu.roll(block, WIN * i, 2)
            if packed is None:
                packed = turned
            else:
                packed = jnp.where((lane >= WIN * i - 4) & (lane < WIN * i + 4), turned, packed)
        zsend[r] = packed

    def circular_z(block):
        def diff(k):
            return pltpu.roll(block, cz - k, 2) - pltpu.roll(block, k, 2)

        return C1 * diff(1) + C2 * diff(2) + C3 * diff(3)

    def z_fix(r):
        true = jnp.where(in_group < 4, zrecv[r, 0], zrecv[r, 1])
        delta = true - zsend[r]
        low = jnp.where(in_group >= WIN - 3, delta, 0.0)
        top = jnp.where(in_group < 3, delta, 0.0)
        low_fix = -(C1 * pltpu.roll(low, 1, 2) + C2 * pltpu.roll(low, 2, 2) + C3 * pltpu.roll(low, 3, 2))
        top_fix = (C1 * pltpu.roll(top, cz - 1, 2) + C2 * pltpu.roll(top, cz - 2, 2)
                   + C3 * pltpu.roll(top, cz - 3, 2))
        return jnp.where(in_group < 3, low_fix, 0.0) + jnp.where(in_group >= WIN - 3, top_fix, 0.0)

    def z_fix_of(fix, i):
        turned = fix if i == 0 else pltpu.roll(fix, (cz - WIN * i) % cz, 2)
        return jnp.where((lane < 3) | (lane >= cz - 3), turned, 0.0)

    def fill_sides(r):
        lines = yside.reshape(comps * cx * cy, cz)
        for c in range(comps):
            for m in range(wide):
                for side, row in ((0, m), (1, cy - wide + m)):
                    lines[pl.ds(c * cx * cy + row, cx, stride=cy), :] = yrecv[r, side, m, c]

    def along_y(block, side):
        def diff(k):
            ahead = pltpu.roll(jnp.where(sub < k, side, block), cy - k, 1)
            behind = pltpu.roll(jnp.where(sub >= cy - k, side, block), k, 1)
            return ahead - behind

        return C1 * diff(1) + C2 * diff(2) + C3 * diff(3)

    def stencil_x(src, sides, i):
        def row(n):
            if n < 0:
                return sides[0, :, n + 2]
            if n >= cx:
                return sides[1, :, n - cx]
            return src[:, n]

        return NEAR * (row(i + 1) - row(i - 1)) + FAR * (row(i + 2) - row(i - 2))

    def stencil_inside(src, i):
        total = None
        for offset, coef in ((1, NEAR), (-1, -NEAR), (2, FAR), (-2, -FAR)):
            if 0 <= i + offset < cx:
                part = coef * src[:, i + offset]
                total = part if total is None else total + part
        return total

    def velocity(n, c, i):
        return base_ref[n, c, i].astype(jnp.float32)[None]

    def fold(blocks8):
        level, m = list(blocks8), 1
        while len(level) > 1:
            keep = (lane & m) == 0
            level = [
                jnp.where(keep, a + pltpu.roll(a, cz - m, 2), b + pltpu.roll(b, m, 2))
                for a, b in zip(level[0::2], level[1::2])
            ]
            m *= 2
        return level[0]

    def unfold(block):
        level, m = [block], WIN // 2
        while m >= 1:
            keep = (lane & m) == 0
            wider = []
            for t in level:
                wider.append(jnp.where(keep, t, pltpu.roll(t, m, 2)))
                wider.append(jnp.where(keep, pltpu.roll(t, cz - m, 2), t))
            level = wider
            m //= 2
        return level

    def observe(src, dst):
        for g in range(cx // WIN):
            sums = fold([src[:, g * WIN + k] for k in range(WIN)])
            mixed = lax.dot_general(
                sums.reshape(comps * cy, cz), blocks[g], (((1,), (1,)), ((), ())),
                precision=high, preferred_element_type=jnp.float32,
            ).reshape(comps, cy, cz)
            for k, t in enumerate(unfold(mixed)):
                dst[:, g * WIN + k] = t

    def build_blocks():
        count = inv_ref.shape[2]
        spread = (
            lax.broadcasted_iota(jnp.int32, (count, cz), 1) // WIN
            == lax.broadcasted_iota(jnp.int32, (count, cz), 0)
        ).astype(jnp.float32)
        for d in range(n_gx):
            source = inv_ref[...] if d == 0 else winrecv[d - 1]
            lanes_inv[d * owned : (d + 1) * owned] = jnp.dot(
                source.reshape(owned * count, count), spread,
                precision=high, preferred_element_type=jnp.float32,
            ).reshape(owned, count, cz) * (1.0 / (WIN * WIN))
        blocks[...] = jnp.zeros(blocks.shape, jnp.float32)
        row = lax.broadcasted_iota(jnp.int32, (WIN, cz), 0)
        col = lax.broadcasted_iota(jnp.int32, (WIN, cz), 1) % WIN

        def add_slot(j, carry):
            owner = lax.rem(gx + n_gx - j // owned, n_gx)
            cell = plane_s[slot_s[owner * owned + j % owned]] - gx * cx
            for g in range(cx // WIN):
                here = (row == cell - g * WIN) & (col == cell - g * WIN)
                for s in range(count):
                    line = jnp.broadcast_to(lanes_inv[j, s : s + 1, :], (WIN, cz))
                    blocks[g, s * WIN : (s + 1) * WIN, :] += jnp.where(here, line, 0.0)
            return carry

        lax.fori_loop(0, n_gx * owned, add_slot, 0)

    def interface(r, block, m, transposed):
        terms = []
        for d in range(n_gx):
            owner = lax.rem(gx + n_gx - d, n_gx)
            for k in range(2):
                n, own = 2 * owner + k, 2 * block + m
                coef = schur_s[n, own] if transposed else schur_s[own, n]
                terms.append((coef, edge[r, d, k]))
        return weighted(terms)

    def early_copies(r):
        return tuple(
            remote(esend.at[d], edge.at[r, d], es_sem.at[r, d], er_sem.at[r, d],
                   {"gx": lax.rem(gx + d, n_gx)})
            for d in range(1, n_gx)
        )

    def early_shares(r, src):
        for i in range(cx):
            rhs[:, i] = stencil_inside(src, i)
        below = (NEAR * src[:, 0] + FAR * src[:, 1], FAR * src[:, 0])
        above = (-(NEAR * src[:, cx - 1] + FAR * src[:, cx - 2]), -FAR * src[:, cx - 1])
        parts = []
        for k in range(2):
            parts.append((2 * gx + k, weighted([(in_s[k, j], rhs[:, j]) for j in range(cx)])))
            parts.append((2 * right_id + k, right_one * (
                near_s[1, k, 0] * above[0] + near_s[1, k, 1] * above[1])))
            parts.append((2 * left_id + k, left_one * (
                near_s[0, k, cx - 1] * below[0] + near_s[0, k, cx - 2] * below[1])))
        for d in tuple(range(1, n_gx)) + (0,):
            owner = lax.rem(gx + d, n_gx)
            for m in range(2):
                share = weighted([(schur_s[2 * owner + m, n], part) for n, part in parts])
                if d == 0:
                    edge[r, 0, m] = share
                else:
                    esend[d, m] = share

    sent = []

    def tangent(r, n, src, dst, first, shadow):
        xc, yc, zc = x_copies(r, src), y_copies(r), z_copies(r)
        ec = edge_copies(r) if first else early_copies(r)
        if first:
            loads[0].wait()
        else:
            x_start(xc)
        pack_z(r, src)
        if not first:
            start(zc)
        pack_y(r, src)
        if first:
            pl.semaphore_wait(barrier, n_gx - 1 + 4)
            x_start(xc)
            start(zc)
        start(yc)
        if not first:
            early_shares(r, src)
            start(ec)
        sent.append((xc, yc + zc + ec))
        if first:
            for copy in loads[1:]:
                copy.wait()
            start(table_copies)
        for i in range(cx):
            block = src[:, i]
            acc[:, i] = block - time_step * (velocity(n, 2, i) * circular_z(block))
        x_arrived(xc)
        for i in range(cx) if first else (0, 1, cx - 2, cx - 1):
            rhs[:, i] = stencil_x(src, xrecv.at[r], i)
        if first:
            for k in range(2):
                edge[r, 0, k] = weighted([(in_s[k, j], rhs[:, j]) for j in range(cx)])
            start(ec)
            start(win_copies)
        for i in range(cx):
            solved = weighted([(local_s[i, j], rhs[:, j]) for j in range(cx)])
            acc[:, i] -= time_step * (velocity(n, 0, i) * solved)
        if first:
            arrived(table_copies)
            table = pltpu.make_async_copy(near_v, near_s, table_sem.at[0])
            table.start()
            table.wait()
        shadow()
        arrived(yc)
        fill_sides(r)
        for i in range(cx):
            acc[:, i] -= time_step * (velocity(n, 1, i) * along_y(src[:, i], yside[:, i]))
        arrived(zc)
        fix = z_fix(r)
        arrived(ec)
        if first:
            values = [interface(r, gx, m, False) for m in range(2)]
        else:
            values = [weighted([(1.0, edge[r, d, m]) for d in range(n_gx)]) for m in range(2)]
        for i in range(cx):
            pulled = out_s[0, i] * values[0] + out_s[1, i] * values[1]
            dst[:, i] = acc[:, i] - time_step * (
                velocity(n, 0, i) * pulled + velocity(n, 2, i) * z_fix_of(fix, i)
            )

    def adjoint(r, n, src, dst, extra):
        xc, yc, zc, ec = x_copies(r, hbuf.at[r - 2]), y_copies(r), z_copies(r), edge_copies(r)
        sent.append((xc, yc + zc + ec))
        held = hbuf.at[r - 2]
        for i in range(cx):
            prod_z[:, i] = velocity(n, 2, i) * src[:, i]
        pack_z(r, prod_z)
        start(zc)
        for i in range(cx):
            prod_y[:, i] = velocity(n, 1, i) * src[:, i]
        pack_y(r, prod_y)
        start(yc)
        for i in range(cx):
            rhs[:, i] = velocity(n, 0, i) * src[:, i]
        for k in range(2):
            edge[r, 0, k] = weighted([(out_s[k, i], rhs[:, i]) for i in range(cx)])
        start(ec)
        order = (0, 1, cx - 2, cx - 1) + tuple(range(2, cx - 2))
        for place, i in enumerate(order):
            held[:, i] = weighted([(local_s[j, i], rhs[:, j]) for j in range(cx)])
            if place == 3:
                x_start(xc)
        for i in range(cx):
            total = src[:, i] + time_step * circular_z(prod_z[:, i])
            acc[:, i] = total if extra is None else total + extra[:, i]
        arrived(ec)
        values = [interface(r, gx, m, True) for m in range(2)]
        lower = [left_one * interface(r, left_id, m, True) for m in range(2)]
        upper = [right_one * interface(r, right_id, m, True) for m in range(2)]
        for i in range(cx):
            rhs[:, i] = held[:, i] + (in_s[0, i] * values[0] + in_s[1, i] * values[1])
        for i in range(2, cx - 2):
            acc[:, i] += time_step * stencil_x(rhs, halo, i)
        x_arrived(xc)
        for n in range(2):
            halo[0, :, n] = xrecv[r, 0, :, n] + (
                near_s[0, 0, cx - 2 + n] * lower[0] + near_s[0, 1, cx - 2 + n] * lower[1])
            halo[1, :, n] = xrecv[r, 1, :, n] + (
                near_s[1, 0, n] * upper[0] + near_s[1, 1, n] * upper[1])
        for i in (0, 1, cx - 2, cx - 1):
            acc[:, i] += time_step * stencil_x(rhs, halo, i)
        arrived(yc)
        fill_sides(r)
        for i in range(cx):
            acc[:, i] += time_step * along_y(prod_y[:, i], yside[:, i])
        arrived(zc)
        fix = z_fix(r)
        for i in range(cx):
            dst[:, i] = acc[:, i] + time_step * z_fix_of(fix, i)

    def nothing():
        pass

    def observe_one():
        arrived(win_copies)
        build_blocks()
        observe(state_one, obs)

    tangent(0, 0, dir_ref, state_one, True, nothing)
    tangent(1, 1, state_one, state_two, False, observe_one)
    observe(state_two, force)
    adjoint(2, 1, force, state_two, obs)
    adjoint(3, 0, state_two, res_ref, None)
    for xc, rest in sent:
        x_sent(xc)
        for copy in rest:
            copy.wait_send()
    for copy in win_copies + table_copies:
        copy.wait_send()


def pair_kernel(
    sizes,
    dir_hbm, base_hbm, inv_hbm,
    local_h, in_h, out_h, schur_h, plane_h, slot_h,
    res_ref,
    dir_ref, base_ref, inv_ref, local_s, in_s, out_s, schur_s, plane_s, slot_s, in_v, near_v, near_s,
    state_one, costate, force, acc, rhs, obs, prod, held, yside, vel, uz_pack,
    xsend, xrecv, ysend, yrecv, zsend, zrecv, winrecv, lanes_inv, blocks, seen_w, fix_rows, fix_edge, mixed,
    load_sem, side_sem, xs_sem, xr_sem, ys_sem, yr_sem, zs_sem, zr_sem,
):
    n_gx, n_gy, n_gz = sizes
    gx, gy, gz = lax.axis_index("gx"), lax.axis_index("gy"), lax.axis_index("gz")
    comps, cx, cy, cz = dir_ref.shape
    wide = ysend.shape[2]
    owned = inv_ref.shape[0]
    other = 1 - gx
    y_next, y_prev = lax.rem(gy + 1, n_gy), lax.rem(gy + n_gy - 1, n_gy)
    z_next, z_prev = lax.rem(gz + 1, n_gz), lax.rem(gz + n_gz - 1, n_gz)
    first = gx == 0
    near_row = jnp.where(first, cx - 2, 0)
    their_row = jnp.where(first, 0, cx - 2)

    barrier = pltpu.get_barrier_semaphore()
    for q in (z_prev, z_next):
        pl.semaphore_signal(barrier, device_id={"gz": q}, device_id_type=MESH)
    pl.semaphore_signal(barrier, device_id={"gx": other}, device_id_type=MESH)
    for q in (y_prev, y_next):
        pl.semaphore_signal(barrier, device_id={"gy": q}, device_id_type=MESH)

    loads = [
        pltpu.make_async_copy(src, dst, load_sem.at[n])
        for n, (src, dst) in enumerate((
            (dir_hbm, dir_ref), (in_h, in_s), (in_h, in_v), (base_hbm, base_ref), (local_h, local_s),
            (schur_h, schur_s), (out_h, out_s), (plane_h, plane_s), (slot_h, slot_s), (inv_hbm, inv_ref),
        ))
    ]
    for copy in loads:
        copy.start()

    def remote(src, dst, send, recv, where):
        return pltpu.make_async_remote_copy(
            src_ref=src, dst_ref=dst, send_sem=send, recv_sem=recv,
            device_id=where, device_id_type=MESH,
        )

    def x_copy(r):
        return remote(xsend.at[r], xrecv.at[r], xs_sem.at[r % 2], xr_sem.at[r % 2], {"gx": other})

    def y_copies(r):
        return tuple(
            remote(ysend.at[r, d], yrecv.at[r, d], ys_sem.at[r % 2], yr_sem.at[r % 2], {"gy": q})
            for d, q in enumerate((y_prev, y_next))
        )

    def z_copies(r):
        return tuple(
            remote(zsend.at[r], zrecv.at[r, d], zs_sem.at[r % 2], zr_sem.at[r % 2], {"gz": q})
            for d, q in enumerate((z_prev, z_next))
        )

    def y_both(r):
        return remote(yrecv.at[r], yrecv.at[r], ys_sem.at[r % 2], yr_sem.at[r % 2], {"gy": y_next})

    def z_both(r):
        return remote(zrecv.at[r], zrecv.at[r], zs_sem.at[r % 2], zr_sem.at[r % 2], {"gz": z_next})

    def settle(r):
        if r >= 0:
            x_copy(r).wait_send()
            y_both(r).wait_send()
            z_both(r).wait_send()

    win_copy = remote(inv_ref, winrecv, side_sem.at[0], side_sem.at[1], {"gx": other})
    table_copy = remote(in_v, near_v, side_sem.at[2], side_sem.at[3], {"gx": other})

    lane = lax.broadcasted_iota(jnp.int32, (cy, cz), 1)
    in_group = lane % WIN
    cell_of = ((lane + WIN // 2) // WIN) % cx
    near_edge = (lane < 3) | (lane >= cz - 3)
    left, right = in_group < 3, in_group >= WIN - 3
    ahead = in_group < WIN // 2

    def packed(block_of):
        total = None
        for i in range(cx):
            block = block_of(i)
            turned = block if i == 0 else pltpu.roll(block, WIN * i, block.ndim - 1)
            total = turned if total is None else jnp.where(cell_of == i, turned, total)
        return total

    def unpacked(block, i):
        turned = block if i == 0 else pltpu.roll(block, (cz - WIN * i) % cz, 2)
        return jnp.where(near_edge, turned, 0.0)

    def pack_y(r, src):
        lines = src.reshape(comps * cx * cy, cz)
        for side, start in ((0, 0), (1, cy - wide)):
            for m in range(wide):
                for c in range(comps):
                    ysend[r, side, m, c] = lines[pl.ds(c * cx * cy + start + m, cx, stride=cy), :]

    def circular(block, axis):
        size = block.shape[axis]

        def diff(k):
            return pltpu.roll(block, size - k, axis) - pltpu.roll(block, k, axis)

        return C1 * diff(1) + C2 * diff(2) + C3 * diff(3)

    def z_fix(r):
        delta = jnp.where(ahead, zrecv[r, 0], zrecv[r, 1]) - zsend[r]
        low = jnp.where(right, delta, 0.0)
        top = jnp.where(left, delta, 0.0)
        low_fix = -(C1 * pltpu.roll(low, 1, 2) + C2 * pltpu.roll(low, 2, 2) + C3 * pltpu.roll(low, 3, 2))
        top_fix = (C1 * pltpu.roll(top, cz - 1, 2) + C2 * pltpu.roll(top, cz - 2, 2)
                   + C3 * pltpu.roll(top, cz - 3, 2))
        return jnp.where(left, low_fix, jnp.where(right, top_fix, 0.0))

    def y_fix(r):
        lines = yside.reshape(comps * cx * cy, cz)
        for c in range(comps):
            def put(row, value):
                lines[pl.ds(c * cx * cy + row, cx, stride=cy), :] = value

            d0, d1, d2 = (yrecv[r, 0, m, c] - ysend[r, 0, m, c] for m in range(3))
            put(cy - 1, C1 * d0 + C2 * d1 + C3 * d2)
            put(cy - 2, C2 * d0 + C3 * d1)
            put(cy - 3, C3 * d0)
            d0, d1, d2 = (yrecv[r, 1, m, c] - ysend[r, 1, m, c] for m in range(3))
            put(0, -(C1 * d2 + C2 * d1 + C3 * d0))
            put(1, -(C2 * d2 + C3 * d1))
            put(2, -(C3 * d2))

    def stencil_inside(row, i):
        total = None
        for step, coef in ((1, NEAR), (2, FAR)):
            up, down = i + step < cx, i - step >= 0
            if up and down:
                part = coef * (row(i + step) - row(i - step))
            elif up:
                part = coef * row(i + step)
            elif down:
                part = -coef * row(i - step)
            else:
                continue
            total = part if total is None else total + part
        return total

    def rows_of(ref):
        return lambda i: ref[:, i]

    def across(pair, to_first):
        low, high = pair
        upper = (FAR * low, NEAR * low + FAR * high)
        lower = (-(NEAR * high + FAR * low), -FAR * high)
        return tuple(jnp.where(to_first, u, d) for u, d in zip(upper, lower))

    def fold(blocks8):
        level, m = list(blocks8), 1
        while len(level) > 1:
            keep = (lane & m) == 0
            level = [
                jnp.where(keep, a + pltpu.roll(a, cz - m, 2), b + pltpu.roll(b, m, 2))
                for a, b in zip(level[0::2], level[1::2])
            ]
            m *= 2
        return level[0]

    def unfold(block):
        level, m = [block], WIN // 2
        while m >= 1:
            keep = (lane & m) == 0
            wider = []
            for t in level:
                wider.append(jnp.where(keep, t, pltpu.roll(t, m, 2)))
                wider.append(jnp.where(keep, pltpu.roll(t, cz - m, 2), t))
            level = wider
            m //= 2
        return level

    def product(a, b, side):
        return lax.dot_general(
            a, b, (((1,), (side,)), ((), ())), precision=high, preferred_element_type=jnp.float32)

    def parts(a):
        high_part = a.astype(jnp.bfloat16)
        return high_part, (a - high_part.astype(jnp.float32)).astype(jnp.bfloat16)

    def weights(a):
        one, two = parts(a)
        return jnp.concatenate([one, two, one], axis=0)

    def apply(a, stacked):
        one, two = parts(a)
        return jnp.dot(
            jnp.concatenate([one, one, two], axis=1), stacked, preferred_element_type=jnp.float32)

    def build_edges():
        count = inv_ref.shape[2]
        place = lax.broadcasted_iota(jnp.int32, (cz, cz), 0)
        column = lax.broadcasted_iota(jnp.int32, (cz, cz), 1)
        cell = ((place + WIN // 2) // WIN) % cx
        target = cell % WIN + jnp.where(place % WIN < WIN // 2, 0, (count - 1) * WIN)
        total = None
        for g in range(cx // WIN):
            chosen = ((cell // WIN == g) & (column == target)).astype(jnp.float32)
            turned = blocks[g].T
            onto_edge = product(turned, chosen, 1)
            seen_w[g, :, :cz] = weights(turned)
            seen_w[g, :, cz:] = weights(onto_edge)
            fix_rows[g] = weights(product(chosen, turned, 0))
            part = product(chosen, onto_edge, 0)
            total = part if total is None else total + part
        fix_edge[...] = weights(total)

    def observe(src, dst):
        for g in range(cx // WIN):
            sums = fold([src[:, g * WIN + k] for k in range(WIN)])
            total = apply(sums.reshape(comps * cy, cz), seen_w[g, :, :cz]).reshape(comps, cy, cz)
            for k, t in enumerate(unfold(total)):
                dst[:, g * WIN + k] = t

    def build_blocks():
        count = inv_ref.shape[2]
        spread = (
            lax.broadcasted_iota(jnp.int32, (count, cz), 1) // WIN
            == lax.broadcasted_iota(jnp.int32, (count, cz), 0)
        ).astype(jnp.float32)
        for d, source in enumerate((inv_ref, winrecv)):
            lanes_inv[d * owned : (d + 1) * owned] = jnp.dot(
                source[...].reshape(owned * count, count), spread,
                precision=high, preferred_element_type=jnp.float32,
            ).reshape(owned, count, cz) * (1.0 / (WIN * WIN))
        blocks[...] = jnp.zeros(blocks.shape, jnp.float32)
        row = lax.broadcasted_iota(jnp.int32, (WIN, cz), 0)
        col = lax.broadcasted_iota(jnp.int32, (WIN, cz), 1) % WIN

        def add_slot(j, carry):
            owner = jnp.where(j < owned, gx, other)
            cell = plane_s[slot_s[owner * owned + j % owned]] - gx * cx
            for g in range(cx // WIN):
                here = (row == cell - g * WIN) & (col == cell - g * WIN)
                for s in range(count):
                    line = jnp.broadcast_to(lanes_inv[j, s : s + 1, :], (WIN, cz))
                    blocks[g, s * WIN : (s + 1) * WIN, :] += jnp.where(here, line, 0.0)
            return carry

        lax.fori_loop(0, n_gx * owned, add_slot, 0)

    def start(copies):
        for copy in copies:
            copy.start()

    def tangent(r, n, src, edge, finish_src, shadow, close):
        zsend[r] = edge
        if not r:
            pl.semaphore_wait(barrier, n_gx - 1 + 4)
        start(z_copies(r))
        finish_src()
        pack_y(r, src)
        start(y_copies(r))
        ours = src[:, pl.ds(near_row, 2)]
        for k in range(2):
            xsend[r, k] = ours[:, k]
        if not r:
            loads[2].wait()
            table_copy.start()
            loads[1].wait()
        for i in range(cx):
            rhs[:, i] = stencil_inside(rows_of(src), i)
        for k in range(2):
            xsend[r, 2 + k] = weighted([(in_s[k, j], rhs[:, j]) for j in range(cx)])
        x_copy(r).start()
        if not r:
            for copy in loads[3:]:
                copy.wait()
            win_copy.start()
            for m in range(2):
                for c in range(comps):
                    for i in range(cx):
                        vel[m, c, i] = time_step * base_ref[m, c, i].astype(jnp.float32)
                uz_pack[m] = packed(lambda i: vel[m, 2, i])
            yside[...] = jnp.zeros(yside.shape, jnp.float32)
        for i in range(cx):
            block = src[:, i]
            solved = weighted([(local_s[i, j], rhs[:, j]) for j in range(cx)])
            acc[:, i] = block - (
                vel[n, 2, i] * circular(block, 2) + vel[n, 1, i] * circular(block, 1) + vel[n, 0, i] * solved)
        shadow()
        x_copy(r).wait_recv()
        pair = xrecv[r, 0], xrecv[r, 1]
        halo = across(pair, first)
        own = [
            xsend[r, 2 + k] + in_s[k, near_row] * halo[0] + in_s[k, near_row + 1] * halo[1] for k in range(2)
        ]
        away = across((xsend[r, 0], xsend[r, 1]), gx != 0)
        theirs = [
            xrecv[r, 2 + k] + near_s[k, their_row] * away[0] + near_s[k, their_row + 1] * away[1]
            for k in range(2)
        ]
        values = [
            weighted([(schur_s[2 * gx + m, 2 * gx + k], own[k]) for k in range(2)]
                     + [(schur_s[2 * gx + m, 2 * other + k], theirs[k]) for k in range(2)])
            for m in range(2)
        ]
        for i in range(cx):
            acc[:, i] -= vel[n, 0, i] * weighted([
                (local_s[i, near_row], halo[0]), (local_s[i, near_row + 1], halo[1]),
                (out_s[0, i], values[0]), (out_s[1, i], values[1])])
        y_both(r).wait_recv()
        y_fix(r)
        for i in range(cx):
            acc[:, i] -= vel[n, 1, i] * yside[:, i]
        closing = close()
        settle(r - 1)
        z_both(r).wait_recv()
        return closing(uz_pack[n] * z_fix(r))

    def close_state():
        before = packed(rows_of(acc))

        def closing(fix):
            def finish():
                for i in range(cx):
                    state_one[:, i] = acc[:, i] - unpacked(fix, i)

            return before - fix, finish

        return closing

    def close_observed():
        groups = range(cx // WIN)
        before = None
        for g in groups:
            sums = fold([acc[:, g * WIN + k] for k in range(WIN)]).reshape(comps * cy, cz)
            both = apply(sums, seen_w[g])
            mixed[g] = both[:, :cz]
            before = both[:, cz:] if before is None else before + both[:, cz:]

        def closing(fix):
            flat = fix.reshape(comps * cy, cz)

            def finish():
                for g in groups:
                    total = (mixed[g] - apply(flat, fix_rows[g])).reshape(comps, cy, cz)
                    for k, t in enumerate(unfold(total)):
                        force[:, g * WIN + k] = t

            return (before - apply(flat, fix_edge[...])).reshape(comps, cy, cz), finish

        return closing

    def adjoint(r, n, src, dst, edge, finish_src, shadow, extra):
        zsend[r] = uz_pack[n] * edge
        start(z_copies(r))
        finish_src()
        for i in range(cx):
            prod[:, i] = vel[n, 1, i] * src[:, i]
        pack_y(r, prod)
        start(y_copies(r))
        for i in range(cx):
            rhs[:, i] = vel[n, 0, i] * src[:, i]
        for k in range(2):
            xsend[r, k] = weighted([(local_s[j, near_row + k], rhs[:, j]) for j in range(cx)])
            xsend[r, 2 + k] = weighted([(out_s[k, j], rhs[:, j]) for j in range(cx)])
        x_copy(r).start()
        shadow()
        for i in range(cx):
            held[:, i] = weighted([(local_s[j, i], rhs[:, j]) for j in range(cx)])
        for i in range(cx):
            total = src[:, i] + circular(vel[n, 2, i] * src[:, i], 2) + circular(prod[:, i], 1)
            if extra is not None:
                total = total + extra[:, i]
            acc[:, i] = total + stencil_inside(rows_of(held), i)
        x_copy(r).wait_recv()

        def solved(block):
            return [
                weighted([(schur_s[2 * gx + k, 2 * block + m], xsend[r, 2 + k]) for k in range(2)]
                         + [(schur_s[2 * other + k, 2 * block + m], xrecv[r, 2 + k]) for k in range(2)])
                for m in range(2)
            ]

        own, theirs = solved(gx), solved(other)
        halo = across([
            xrecv[r, k] + near_s[0, their_row + k] * theirs[0] + near_s[1, their_row + k] * theirs[1]
            for k in range(2)
        ], first)
        for i in range(cx):
            acc[:, i] += weighted([
                (stencil_inside(lambda j, m=m: in_s[m, j], i), own[m]) for m in range(2)])
        for k in range(2):
            acc[:, near_row + k] += halo[k]
        y_both(r).wait_recv()
        y_fix(r)
        for i in range(cx):
            acc[:, i] += yside[:, i]
        before = packed(rows_of(acc))
        settle(r - 1)
        z_both(r).wait_recv()
        fix = z_fix(r)
        after = before + fix

        def finish():
            for i in range(cx):
                dst[:, i] = acc[:, i] + unpacked(fix, i)

        return after, finish

    def table():
        table_copy.wait_recv()
        copy = pltpu.make_async_copy(near_v, near_s, load_sem.at[0])
        copy.start()
        copy.wait()

    def observe_one():
        observe(state_one, obs)

    def tables():
        win_copy.wait_recv()
        build_blocks()
        build_edges()

    def nothing():
        pass

    loads[0].wait()
    edge, finish = tangent(0, 0, dir_ref, packed(rows_of(dir_ref)), nothing, table, close_state)
    edge, finish = tangent(1, 1, state_one, edge, finish, tables, close_observed)
    edge, finish = adjoint(2, 1, force, costate, edge, finish, observe_one, obs)
    edge, finish = adjoint(3, 0, costate, res_ref, edge, finish, nothing, None)
    finish()
    settle(3)
    win_copy.wait_send()
    table_copy.wait_send()


def solution(mesh):
    sizes = tuple(mesh.shape[name] for name in ("gx", "gy", "gz"))

    def local(direction, base_flow, local_inv, couple_in, couple_out, schur_inv,
              plane_x, slot_plane, window_inv):
        n_gx = sizes[0]
        comps, cx, cy, cz = direction.shape
        owned, count = window_inv.shape[0], window_inv.shape[3]
        wide = 3
        field = pltpu.VMEM(direction.shape, jnp.float32)

        def held(*shape):
            return pltpu.VMEM(shape, jnp.float32)

        sems = pltpu.SemaphoreType.DMA
        vmem = pl.BlockSpec(memory_space=pltpu.VMEM)
        kept = functools.partial(pltpu.with_memory_space_constraint, memory_space=pltpu.HBM)
        hbm = pl.BlockSpec(memory_space=pltpu.HBM)
        tables = (local_inv, couple_in, couple_out.T, schur_inv, plane_x, slot_plane)
        operands = tuple(map(kept, (direction, base_flow, window_inv.reshape(owned, count, count)) + tables))
        call = functools.partial(
            pl.pallas_call,
            out_shape=jax.ShapeDtypeStruct(direction.shape, jnp.float32),
            in_specs=[hbm] * 9,
            out_specs=vmem,
            compiler_params=pltpu.CompilerParams(collective_id=0, has_side_effects=True, vmem_limit_bytes=16 * 2**20),
        )
        loaded = [
            field, pltpu.VMEM(base_flow.shape, base_flow.dtype), held(owned, count, count),
        ] + [pltpu.SMEM(t.shape, t.dtype) for t in tables]
        if n_gx == 2:
            pulled = call(
                functools.partial(pair_kernel, sizes),
                scratch_shapes=loaded + [
                    held(2, cx), held(2, cx), pltpu.SMEM((2, cx), jnp.float32),
                ] + [field] * 9 + [
                    held(*base_flow.shape), held(2, cy, cz),
                    held(4, 4, comps, cy, cz), held(4, 4, comps, cy, cz),
                    held(4, 2, wide, comps, cx, cz), held(4, 2, wide, comps, cx, cz),
                    held(4, comps, cy, cz), held(4, 2, comps, cy, cz),
                    held(owned, count, count), held(n_gx * owned, count, cz), held(cx // WIN, count * WIN, cz),
                    pltpu.VMEM((cx // WIN, 3 * cz, 2 * cz), jnp.bfloat16),
                    pltpu.VMEM((cx // WIN, 3 * cz, cz), jnp.bfloat16), pltpu.VMEM((3 * cz, cz), jnp.bfloat16),
                    held(cx // WIN, comps * cy, cz),
                    sems((10,)), sems((4,)),
                ] + [sems((2,))] * 6,
            )(*operands)
            return pulled + direction
        pulled = call(
            functools.partial(kernel, sizes),
            scratch_shapes=loaded + [
                held(2, cx), held(2, 2, cx), pltpu.SMEM((2, 2, cx), jnp.float32),
                held(n_gx, 2, comps, cy, cz), held(2, comps, 2, cy, cz),
                sems((10,)), sems((1,)), sems((2,)), sems((2,)),
            ] + [field] * 8 + [
                held(2, comps, cx, cy, cz),
                field,
                held(4, 2, comps, 2, cy, cz),
                held(4, 2, wide, comps, cx, cz),
                held(4, 2, wide, comps, cx, cz),
                held(4, comps, cy, cz),
                held(4, 2, comps, cy, cz),
                held(4, n_gx, 2, comps, cy, cz),
                held(n_gx - 1, owned, count, count),
                held(n_gx * owned, count, cz),
                held(cx // WIN, count * WIN, cz),
                sems((4, 2)), sems((4, 2)), sems((4, 2)), sems((4, 2)), sems((4, 2)), sems((4, 2)),
                sems((4, n_gx)), sems((4, n_gx)), sems((n_gx,)), sems((n_gx,)),
            ],
        )(*operands)
        return pulled + direction

    return jax.shard_map(
        local,
        mesh=mesh,
        in_specs=(
            P(None, "gx", "gy", "gz"),
            P(None, None, "gx", "gy", "gz"),
            P("gx", None),
            P("gx", None),
            P("gx", None),
            P(),
            P(),
            P(),
            P("gx", "gy", "gz", None, None),
        ),
        out_specs=P(None, "gx", "gy", "gz"),
        check_vma=False,
    )
```

```python
import functools

import jax
import jax.numpy as jnp
from jax import lax
from jax.experimental import pallas as pl
from jax.experimental.pallas import tpu as pltpu
from jax.sharding import PartitionSpec as P

WIN = 8
time_step = 0.15
NEAR = 7.0 / 9.0
FAR = 1.0 / 36.0
C1 = 45.0 / 60.0
C2 = -9.0 / 60.0
C3 = 1.0 / 60.0
MESH = pl.DeviceIdType.MESH
high = lax.Precision.HIGHEST


def weighted(terms):
    chains = [None, None]
    for n, (coef, block) in enumerate(terms):
        part = coef * block
        chains[n % 2] = part if chains[n % 2] is None else chains[n % 2] + part
    return chains[0] if chains[1] is None else chains[0] + chains[1]


def kernel(
    sizes,
    dir_hbm, base_hbm, inv_hbm,
    local_h, in_h, out_h, schur_h, plane_h, slot_h,
    res_ref,
    dir_ref, base_ref, inv_ref, local_s, in_s, out_s, schur_s, plane_s, slot_s, in_v, near_v, near_s, esend, halo, load_sem, table_sem, ts_sem, tr_sem,
    state_one, state_two, force, acc, rhs, obs, prod_y, prod_z, hbuf,
    yside, xrecv, ysend, yrecv, zsend, zrecv, edge, winrecv, lanes_inv, blocks,
    xs_sem, xr_sem, ys_sem, yr_sem, zs_sem, zr_sem, es_sem, er_sem, ws_sem, wr_sem,
):
    n_gx, n_gy, n_gz = sizes
    gx, gy, gz = lax.axis_index("gx"), lax.axis_index("gy"), lax.axis_index("gz")
    comps, cx, cy, cz = dir_ref.shape
    wide = ysend.shape[2]
    loads = [
        pltpu.make_async_copy(src, dst, load_sem.at[n])
        for n, (src, dst) in enumerate((
            (dir_hbm, dir_ref), (in_h, in_s), (schur_h, schur_s), (local_h, local_s),
            (out_h, out_s), (plane_h, plane_s), (slot_h, slot_s),
            (base_hbm, base_ref), (inv_hbm, inv_ref), (in_h, in_v),
        ))
    ]
    owned = inv_ref.shape[0]
    y_next, y_prev = lax.rem(gy + 1, n_gy), lax.rem(gy + n_gy - 1, n_gy)
    z_next, z_prev = lax.rem(gz + 1, n_gz), lax.rem(gz + n_gz - 1, n_gz)

    @pl.when(gx == 0)
    def _():
        xrecv[:, 0] = jnp.zeros(xrecv.shape[:1] + xrecv.shape[2:], jnp.float32)

    @pl.when(gx == n_gx - 1)
    def _():
        xrecv[:, 1] = jnp.zeros(xrecv.shape[:1] + xrecv.shape[2:], jnp.float32)

    barrier = pltpu.get_barrier_semaphore()
    for d in range(1, n_gx):
        pl.semaphore_signal(barrier, device_id={"gx": lax.rem(gx + d, n_gx)}, device_id_type=MESH)
    for q in (y_prev, y_next):
        pl.semaphore_signal(barrier, device_id={"gy": q}, device_id_type=MESH)
    for q in (z_prev, z_next):
        pl.semaphore_signal(barrier, device_id={"gz": q}, device_id_type=MESH)

    for copy in loads:
        copy.start()

    def remote(src, dst, send, recv, where):
        return pltpu.make_async_remote_copy(
            src_ref=src, dst_ref=dst, send_sem=send, recv_sem=recv,
            device_id=where, device_id_type=MESH,
        )

    lane = lax.broadcasted_iota(jnp.int32, (comps, cy, cz), 2)
    sub = lax.broadcasted_iota(jnp.int32, (comps, cy, cz), 1)
    in_group = lane % WIN

    def x_copies(r, src):
        right = remote(src.at[:, cx - 2 : cx], xrecv.at[r, 0], xs_sem.at[r, 0], xr_sem.at[r, 0],
                       {"gx": lax.rem(gx + 1, n_gx)})
        left = remote(src.at[:, 0:2], xrecv.at[r, 1], xs_sem.at[r, 1], xr_sem.at[r, 1],
                      {"gx": lax.rem(gx + n_gx - 1, n_gx)})
        return right, left

    def x_start(copies):
        right, left = copies

        @pl.when(gx < n_gx - 1)
        def _():
            right.start()

        @pl.when(gx > 0)
        def _():
            left.start()

    def x_arrived(copies):
        right, left = copies

        @pl.when(gx > 0)
        def _():
            right.wait_recv()

        @pl.when(gx < n_gx - 1)
        def _():
            left.wait_recv()

    def x_sent(copies):
        right, left = copies

        @pl.when(gx < n_gx - 1)
        def _():
            right.wait_send()

        @pl.when(gx > 0)
        def _():
            left.wait_send()

    def y_copies(r):
        return (
            remote(ysend.at[r, 0], yrecv.at[r, 0], ys_sem.at[r, 0], yr_sem.at[r, 0], {"gy": y_prev}),
            remote(ysend.at[r, 1], yrecv.at[r, 1], ys_sem.at[r, 1], yr_sem.at[r, 1], {"gy": y_next}),
        )

    def z_copies(r):
        return (
            remote(zsend.at[r], zrecv.at[r, 0], zs_sem.at[r, 0], zr_sem.at[r, 0], {"gz": z_prev}),
            remote(zsend.at[r], zrecv.at[r, 1], zs_sem.at[r, 1], zr_sem.at[r, 1], {"gz": z_next}),
        )

    def edge_copies(r):
        return tuple(
            remote(edge.at[r, 0], edge.at[r, d], es_sem.at[r, d], er_sem.at[r, d],
                   {"gx": lax.rem(gx + d, n_gx)})
            for d in range(1, n_gx)
        )

    win_copies = tuple(
        remote(inv_ref, winrecv.at[d - 1], ws_sem.at[d], wr_sem.at[d], {"gx": lax.rem(gx + d, n_gx)})
        for d in range(1, n_gx)
    )

    table_copies = (
        remote(in_v, near_v.at[0], ts_sem.at[0], tr_sem.at[0], {"gx": lax.rem(gx + 1, n_gx)}),
        remote(in_v, near_v.at[1], ts_sem.at[1], tr_sem.at[1], {"gx": lax.rem(gx + n_gx - 1, n_gx)}),
    )
    left_one = jnp.where(gx > 0, 1.0, 0.0)
    right_one = jnp.where(gx < n_gx - 1, 1.0, 0.0)
    left_id, right_id = lax.rem(gx + n_gx - 1, n_gx), lax.rem(gx + 1, n_gx)

    def start(copies):
        for copy in copies:
            copy.start()

    def arrived(copies):
        for copy in copies:
            copy.wait_recv()

    def pack_y(r, src):
        lines = src.reshape(comps * cx * cy, cz)
        for c in range(comps):
            for m in range(wide):
                for side, row in ((0, m), (1, cy - wide + m)):
                    ysend[r, side, m, c] = lines[pl.ds(c * cx * cy + row, cx, stride=cy), :]

    def pack_z(r, src):
        packed = None
        for i in range(cx):
            block = src[:, i]
            turned = block if i == 0 else pltpu.roll(block, WIN * i, 2)
            if packed is None:
                packed = turned
            else:
                packed = jnp.where((lane >= WIN * i - 4) & (lane < WIN * i + 4), turned, packed)
        zsend[r] = packed

    def circular_z(block):
        def diff(k):
            return pltpu.roll(block, cz - k, 2) - pltpu.roll(block, k, 2)

        return C1 * diff(1) + C2 * diff(2) + C3 * diff(3)

    def z_fix(r):
        true = jnp.where(in_group < 4, zrecv[r, 0], zrecv[r, 1])
        delta = true - zsend[r]
        low = jnp.where(in_group >= WIN - 3, delta, 0.0)
        top = jnp.where(in_group < 3, delta, 0.0)
        low_fix = -(C1 * pltpu.roll(low, 1, 2) + C2 * pltpu.roll(low, 2, 2) + C3 * pltpu.roll(low, 3, 2))
        top_fix = (C1 * pltpu.roll(top, cz - 1, 2) + C2 * pltpu.roll(top, cz - 2, 2)
                   + C3 * pltpu.roll(top, cz - 3, 2))
        return jnp.where(in_group < 3, low_fix, 0.0) + jnp.where(in_group >= WIN - 3, top_fix, 0.0)

    def z_fix_of(fix, i):
        turned = fix if i == 0 else pltpu.roll(fix, (cz - WIN * i) % cz, 2)
        return jnp.where((lane < 3) | (lane >= cz - 3), turned, 0.0)

    def fill_sides(r):
        lines = yside.reshape(comps * cx * cy, cz)
        for c in range(comps):
            for m in range(wide):
                for side, row in ((0, m), (1, cy - wide + m)):
                    lines[pl.ds(c * cx * cy + row, cx, stride=cy), :] = yrecv[r, side, m, c]

    def along_y(block, side):
        def diff(k):
            ahead = pltpu.roll(jnp.where(sub < k, side, block), cy - k, 1)
            behind = pltpu.roll(jnp.where(sub >= cy - k, side, block), k, 1)
            return ahead - behind

        return C1 * diff(1) + C2 * diff(2) + C3 * diff(3)

    def stencil_x(src, sides, i):
        def row(n):
            if n < 0:
                return sides[0, :, n + 2]
            if n >= cx:
                return sides[1, :, n - cx]
            return src[:, n]

        return NEAR * (row(i + 1) - row(i - 1)) + FAR * (row(i + 2) - row(i - 2))

    def stencil_inside(src, i):
        total = None
        for offset, coef in ((1, NEAR), (-1, -NEAR), (2, FAR), (-2, -FAR)):
            if 0 <= i + offset < cx:
                part = coef * src[:, i + offset]
                total = part if total is None else total + part
        return total

    def velocity(n, c, i):
        return base_ref[n, c, i].astype(jnp.float32)[None]

    def fold(blocks8):
        level, m = list(blocks8), 1
        while len(level) > 1:
            keep = (lane & m) == 0
            level = [
                jnp.where(keep, a + pltpu.roll(a, cz - m, 2), b + pltpu.roll(b, m, 2))
                for a, b in zip(level[0::2], level[1::2])
            ]
            m *= 2
        return level[0]

    def unfold(block):
        level, m = [block], WIN // 2
        while m >= 1:
            keep = (lane & m) == 0
            wider = []
            for t in level:
                wider.append(jnp.where(keep, t, pltpu.roll(t, m, 2)))
                wider.append(jnp.where(keep, pltpu.roll(t, cz - m, 2), t))
            level = wider
            m //= 2
        return level

    def observe(src, dst):
        for g in range(cx // WIN):
            sums = fold([src[:, g * WIN + k] for k in range(WIN)])
            mixed = lax.dot_general(
                sums.reshape(comps * cy, cz), blocks[g], (((1,), (1,)), ((), ())),
                precision=high, preferred_element_type=jnp.float32,
            ).reshape(comps, cy, cz)
            for k, t in enumerate(unfold(mixed)):
                dst[:, g * WIN + k] = t

    def build_blocks():
        count = inv_ref.shape[2]
        spread = (
            lax.broadcasted_iota(jnp.int32, (count, cz), 1) // WIN
            == lax.broadcasted_iota(jnp.int32, (count, cz), 0)
        ).astype(jnp.float32)
        for d in range(n_gx):
            source = inv_ref[...] if d == 0 else winrecv[d - 1]
            lanes_inv[d * owned : (d + 1) * owned] = jnp.dot(
                source.reshape(owned * count, count), spread,
                precision=high, preferred_element_type=jnp.float32,
            ).reshape(owned, count, cz) * (1.0 / (WIN * WIN))
        blocks[...] = jnp.zeros(blocks.shape, jnp.float32)
        row = lax.broadcasted_iota(jnp.int32, (WIN, cz), 0)
        col = lax.broadcasted_iota(jnp.int32, (WIN, cz), 1) % WIN

        def add_slot(j, carry):
            owner = lax.rem(gx + n_gx - j // owned, n_gx)
            cell = plane_s[slot_s[owner * owned + j % owned]] - gx * cx
            for g in range(cx // WIN):
                here = (row == cell - g * WIN) & (col == cell - g * WIN)
                for s in range(count):
                    line = jnp.broadcast_to(lanes_inv[j, s : s + 1, :], (WIN, cz))
                    blocks[g, s * WIN : (s + 1) * WIN, :] += jnp.where(here, line, 0.0)
            return carry

        lax.fori_loop(0, n_gx * owned, add_slot, 0)

    def interface(r, block, m, transposed):
        terms = []
        for d in range(n_gx):
            owner = lax.rem(gx + n_gx - d, n_gx)
            for k in range(2):
                n, own = 2 * owner + k, 2 * block + m
                coef = schur_s[n, own] if transposed else schur_s[own, n]
                terms.append((coef, edge[r, d, k]))
        return weighted(terms)

    def early_copies(r):
        return tuple(
            remote(esend.at[d], edge.at[r, d], es_sem.at[r, d], er_sem.at[r, d],
                   {"gx": lax.rem(gx + d, n_gx)})
            for d in range(1, n_gx)
        )

    def early_shares(r, src):
        for i in range(cx):
            rhs[:, i] = stencil_inside(src, i)
        below = (NEAR * src[:, 0] + FAR * src[:, 1], FAR * src[:, 0])
        above = (-(NEAR * src[:, cx - 1] + FAR * src[:, cx - 2]), -FAR * src[:, cx - 1])
        parts = []
        for k in range(2):
            parts.append((2 * gx + k, weighted([(in_s[k, j], rhs[:, j]) for j in range(cx)])))
            parts.append((2 * right_id + k, right_one * (
                near_s[1, k, 0] * above[0] + near_s[1, k, 1] * above[1])))
            parts.append((2 * left_id + k, left_one * (
                near_s[0, k, cx - 1] * below[0] + near_s[0, k, cx - 2] * below[1])))
        for d in tuple(range(1, n_gx)) + (0,):
            owner = lax.rem(gx + d, n_gx)
            for m in range(2):
                share = weighted([(schur_s[2 * owner + m, n], part) for n, part in parts])
                if d == 0:
                    edge[r, 0, m] = share
                else:
                    esend[d, m] = share

    sent = []

    def tangent(r, n, src, dst, first, shadow):
        xc, yc, zc = x_copies(r, src), y_copies(r), z_copies(r)
        ec = edge_copies(r) if first else early_copies(r)
        if first:
            loads[0].wait()
        else:
            x_start(xc)
        pack_z(r, src)
        if not first:
            start(zc)
        pack_y(r, src)
        if first:
            pl.semaphore_wait(barrier, n_gx - 1 + 4)
            x_start(xc)
            start(zc)
        start(yc)
        if not first:
            early_shares(r, src)
            start(ec)
        sent.append((xc, yc + zc + ec))
        if first:
            for copy in loads[1:]:
                copy.wait()
            start(table_copies)
        for i in range(cx):
            block = src[:, i]
            acc[:, i] = block - time_step * (velocity(n, 2, i) * circular_z(block))
        x_arrived(xc)
        for i in range(cx) if first else (0, 1, cx - 2, cx - 1):
            rhs[:, i] = stencil_x(src, xrecv.at[r], i)
        if first:
            for k in range(2):
                edge[r, 0, k] = weighted([(in_s[k, j], rhs[:, j]) for j in range(cx)])
            start(ec)
            start(win_copies)
        for i in range(cx):
            solved = weighted([(local_s[i, j], rhs[:, j]) for j in range(cx)])
            acc[:, i] -= time_step * (velocity(n, 0, i) * solved)
        if first:
            arrived(table_copies)
            table = pltpu.make_async_copy(near_v, near_s, table_sem.at[0])
            table.start()
            table.wait()
        shadow()
        arrived(yc)
        fill_sides(r)
        for i in range(cx):
            acc[:, i] -= time_step * (velocity(n, 1, i) * along_y(src[:, i], yside[:, i]))
        arrived(zc)
        fix = z_fix(r)
        arrived(ec)
        if first:
            values = [interface(r, gx, m, False) for m in range(2)]
        else:
            values = [weighted([(1.0, edge[r, d, m]) for d in range(n_gx)]) for m in range(2)]
        for i in range(cx):
            pulled = out_s[0, i] * values[0] + out_s[1, i] * values[1]
            dst[:, i] = acc[:, i] - time_step * (
                velocity(n, 0, i) * pulled + velocity(n, 2, i) * z_fix_of(fix, i)
            )

    def adjoint(r, n, src, dst, extra):
        xc, yc, zc, ec = x_copies(r, hbuf.at[r - 2]), y_copies(r), z_copies(r), edge_copies(r)
        sent.append((xc, yc + zc + ec))
        held = hbuf.at[r - 2]
        for i in range(cx):
            prod_z[:, i] = velocity(n, 2, i) * src[:, i]
        pack_z(r, prod_z)
        start(zc)
        for i in range(cx):
            prod_y[:, i] = velocity(n, 1, i) * src[:, i]
        pack_y(r, prod_y)
        start(yc)
        for i in range(cx):
            rhs[:, i] = velocity(n, 0, i) * src[:, i]
        for k in range(2):
            edge[r, 0, k] = weighted([(out_s[k, i], rhs[:, i]) for i in range(cx)])
        start(ec)
        order = (0, 1, cx - 2, cx - 1) + tuple(range(2, cx - 2))
        for place, i in enumerate(order):
            held[:, i] = weighted([(local_s[j, i], rhs[:, j]) for j in range(cx)])
            if place == 3:
                x_start(xc)
        for i in range(cx):
            total = src[:, i] + time_step * circular_z(prod_z[:, i])
            acc[:, i] = total if extra is None else total + extra[:, i]
        arrived(ec)
        values = [interface(r, gx, m, True) for m in range(2)]
        lower = [left_one * interface(r, left_id, m, True) for m in range(2)]
        upper = [right_one * interface(r, right_id, m, True) for m in range(2)]
        for i in range(cx):
            rhs[:, i] = held[:, i] + (in_s[0, i] * values[0] + in_s[1, i] * values[1])
        for i in range(2, cx - 2):
            acc[:, i] += time_step * stencil_x(rhs, halo, i)
        x_arrived(xc)
        for n in range(2):
            halo[0, :, n] = xrecv[r, 0, :, n] + (
                near_s[0, 0, cx - 2 + n] * lower[0] + near_s[0, 1, cx - 2 + n] * lower[1])
            halo[1, :, n] = xrecv[r, 1, :, n] + (
                near_s[1, 0, n] * upper[0] + near_s[1, 1, n] * upper[1])
        for i in (0, 1, cx - 2, cx - 1):
            acc[:, i] += time_step * stencil_x(rhs, halo, i)
        arrived(yc)
        fill_sides(r)
        for i in range(cx):
            acc[:, i] += time_step * along_y(prod_y[:, i], yside[:, i])
        arrived(zc)
        fix = z_fix(r)
        for i in range(cx):
            dst[:, i] = acc[:, i] + time_step * z_fix_of(fix, i)

    def nothing():
        pass

    def observe_one():
        arrived(win_copies)
        build_blocks()
        observe(state_one, obs)

    tangent(0, 0, dir_ref, state_one, True, nothing)
    tangent(1, 1, state_one, state_two, False, observe_one)
    observe(state_two, force)
    adjoint(2, 1, force, state_two, obs)
    adjoint(3, 0, state_two, res_ref, None)
    for xc, rest in sent:
        x_sent(xc)
        for copy in rest:
            copy.wait_send()
    for copy in win_copies + table_copies:
        copy.wait_send()


def pair_kernel(
    sizes,
    dir_hbm, base_hbm, inv_hbm,
    local_h, in_h, out_h, schur_h, plane_h, slot_h,
    res_ref,
    dir_ref, base_ref, inv_ref, local_s, in_s, out_s, schur_s, plane_s, slot_s, in_v, near_v, near_s,
    state_one, costate, force, acc, rhs, obs, prod, held, yside, vel, uz_pack,
    xsend, xrecv, ysend, yrecv, zsend, zrecv, winrecv, lanes_inv, blocks, seen_w, fix_rows, fix_edge, mixed, uz_near,
    own_side, fix_sent, fix_near, across_x, across_w, uxy_pack,
    load_sem, sent_sem, side_sem, xr_sem, yr_sem, zr_sem,
):
    n_gx, n_gy, n_gz = sizes
    gx, gy, gz = lax.axis_index("gx"), lax.axis_index("gy"), lax.axis_index("gz")
    comps, cx, cy, cz = dir_ref.shape
    wide = ysend.shape[3]
    owned = inv_ref.shape[0]
    other = 1 - gx
    y_next, y_prev = lax.rem(gy + 1, n_gy), lax.rem(gy + n_gy - 1, n_gy)
    z_next, z_prev = lax.rem(gz + 1, n_gz), lax.rem(gz + n_gz - 1, n_gz)
    first = gx == 0
    near_row = jnp.where(first, cx - 2, 0)
    their_row = jnp.where(first, 0, cx - 2)

    barrier = pltpu.get_barrier_semaphore()
    for q in (z_prev, z_next):
        pl.semaphore_signal(barrier, device_id={"gz": q}, device_id_type=MESH)
    pl.semaphore_signal(barrier, device_id={"gx": other}, device_id_type=MESH)
    for q in (y_prev, y_next):
        pl.semaphore_signal(barrier, device_id={"gy": q}, device_id_type=MESH)

    loads = [
        pltpu.make_async_copy(src, dst, load_sem.at[n])
        for n, (src, dst) in enumerate((
            (dir_hbm, dir_ref), (in_h, in_s), (in_h, in_v), (base_hbm, base_ref), (local_h, local_s),
            (schur_h, schur_s), (out_h, out_s), (plane_h, plane_s), (slot_h, slot_s), (inv_hbm, inv_ref),
        ))
    ]
    for copy in loads:
        copy.start()

    def remote(src, dst, send, recv, where):
        return pltpu.make_async_remote_copy(
            src_ref=src, dst_ref=dst, send_sem=send, recv_sem=recv,
            device_id=where, device_id_type=MESH,
        )

    x_sent = [load_sem.at[n] for n in (1, 7, 1, 7)]
    y_sent = [sent_sem.at[0], load_sem.at[6]] * 2
    z_sent = [load_sem.at[n] for n in (0, 5, 0, 8)]

    def x_copy(r):
        return remote(xsend.at[r], xrecv.at[r], x_sent[r], xr_sem.at[r % 2], {"gx": other})

    def y_copies(r, c):
        return tuple(
            remote(ysend.at[r, c, d], yrecv.at[r, c, d], y_sent[r], yr_sem.at[r % 2, c], {"gy": q})
            for d, q in enumerate((y_prev, y_next))
        )

    def z_copies(r):
        return tuple(
            remote(zsend.at[r], zrecv.at[r, d], z_sent[r], zr_sem.at[r], {"gz": q})
            for d, q in enumerate((z_prev, z_next))
        )

    uz_copies = tuple(
        remote(uz_pack.at[0], uz_near.at[d], load_sem.at[4], side_sem.at[2], {"gz": q})
        for d, q in enumerate((z_prev, z_next))
    )
    uz_both = remote(uz_near, uz_near, load_sem.at[4], side_sem.at[2], {"gz": z_next})

    fix_copies = tuple(
        remote(fix_sent, fix_near.at[d], load_sem.at[9], side_sem.at[3], where)
        for d, where in enumerate(({"gy": y_prev}, {"gy": y_next}, {"gx": other}))
    )
    fix_all = remote(fix_near, fix_near, load_sem.at[9], side_sem.at[3], {"gx": other})

    def y_both(r, c):
        return remote(yrecv.at[r, c], yrecv.at[r, c], y_sent[r], yr_sem.at[r % 2, c], {"gy": y_next})

    def y_all(r):
        return remote(yrecv.at[r], yrecv.at[r], y_sent[r], yr_sem.at[r % 2, 0], {"gy": y_next})

    def z_both(r):
        return remote(zrecv.at[r], zrecv.at[r], z_sent[r], zr_sem.at[r], {"gz": z_next})

    def settle(r):
        if r >= 0:
            x_copy(r).wait_send()
            y_all(r).wait_send()
            z_both(r).wait_send()

    win_copy = remote(inv_ref, winrecv, load_sem.at[3], side_sem.at[0], {"gx": other})
    table_copy = remote(in_v, near_v, load_sem.at[2], side_sem.at[1], {"gx": other})

    lane = lax.broadcasted_iota(jnp.int32, (cy, cz), 1)
    in_group = lane % WIN
    cell_of = ((lane + WIN // 2) // WIN) % cx
    sub = lax.broadcasted_iota(jnp.int32, (cy, cz), 0)
    near_edge = (lane < 3) | (lane >= cz - 3)
    left, right = in_group < 3, in_group >= WIN - 3
    ahead = in_group < WIN // 2

    def packed(block_of):
        total = None
        for i in range(cx):
            block = block_of(i)
            turned = block if i == 0 else pltpu.roll(block, WIN * i, block.ndim - 1)
            total = turned if total is None else jnp.where(cell_of == i, turned, total)
        return total

    def unpacked(block, i):
        turned = block if i == 0 else pltpu.roll(block, (cz - WIN * i) % cz, 2)
        return jnp.where(near_edge, turned, 0.0)

    def send_y(r, src):
        lines = src.reshape(comps * cx * cy, cz)
        for c in range(comps):
            for side, begin in ((0, 0), (1, cy - wide)):
                for m in range(wide):
                    ysend[r, c, side, m] = lines[pl.ds(c * cx * cy + begin + m, cx, stride=cy), :]
            start(y_copies(r, c))

    def circular(block, axis):
        size = block.shape[axis]

        def diff(k):
            return pltpu.roll(block, size - k, axis) - pltpu.roll(block, k, axis)

        return C1 * diff(1) + C2 * diff(2) + C3 * diff(3)

    def lateral(edge):
        low = jnp.where(right, edge, 0.0)
        top = jnp.where(left, edge, 0.0)
        low_fix = -(C1 * pltpu.roll(low, 1, 2) + C2 * pltpu.roll(low, 2, 2) + C3 * pltpu.roll(low, 3, 2))
        top_fix = (C1 * pltpu.roll(top, cz - 1, 2) + C2 * pltpu.roll(top, cz - 2, 2)
                   + C3 * pltpu.roll(top, cz - 3, 2))
        return jnp.where(left, low_fix, jnp.where(right, top_fix, 0.0))

    def facing(pair):
        return jnp.where(ahead, pair[0], pair[1])

    def y_fix(r, c):
        y_both(r, c).wait_recv()
        lines = yside.reshape(comps * cx * cy, cz)

        def put(row, value):
            lines[pl.ds(c * cx * cy + row, cx, stride=cy), :] = value

        d0, d1, d2 = (yrecv[r, c, 0, m] - ysend[r, c, 0, m] for m in range(3))
        put(cy - 1, C1 * d0 + C2 * d1 + C3 * d2)
        put(cy - 2, C2 * d0 + C3 * d1)
        put(cy - 3, C3 * d0)
        d0, d1, d2 = (yrecv[r, c, 1, m] - ysend[r, c, 1, m] for m in range(3))
        put(0, -(C1 * d2 + C2 * d1 + C3 * d0))
        put(1, -(C2 * d2 + C3 * d1))
        put(2, -(C3 * d2))

    def stencil_inside(row, i):
        total = None
        for step, coef in ((1, NEAR), (2, FAR)):
            up, down = i + step < cx, i - step >= 0
            if up and down:
                part = coef * (row(i + step) - row(i - step))
            elif up:
                part = coef * row(i + step)
            elif down:
                part = -coef * row(i - step)
            else:
                continue
            total = part if total is None else total + part
        return total

    def rows_of(ref):
        return lambda i: ref[:, i]

    def across(pair, to_first):
        low, high = pair
        upper = (FAR * low, NEAR * low + FAR * high)
        lower = (-(NEAR * high + FAR * low), -FAR * high)
        return tuple(jnp.where(to_first, u, d) for u, d in zip(upper, lower))

    def fold(blocks8):
        level, m = list(blocks8), 1
        while len(level) > 1:
            keep = (lane & m) == 0
            level = [
                jnp.where(keep, a + pltpu.roll(a, cz - m, 2), b + pltpu.roll(b, m, 2))
                for a, b in zip(level[0::2], level[1::2])
            ]
            m *= 2
        return level[0]

    def unfold(block):
        level, m = [block], WIN // 2
        while m >= 1:
            keep = (lane & m) == 0
            wider = []
            for t in level:
                wider.append(jnp.where(keep, t, pltpu.roll(t, m, 2)))
                wider.append(jnp.where(keep, pltpu.roll(t, cz - m, 2), t))
            level = wider
            m //= 2
        return level

    def product(a, b, side):
        return lax.dot_general(
            a, b, (((1,), (side,)), ((), ())), precision=high, preferred_element_type=jnp.float32)

    def parts(a):
        high_part = a.astype(jnp.bfloat16)
        return high_part, (a - high_part.astype(jnp.float32)).astype(jnp.bfloat16)

    def weights(a):
        one, two = parts(a)
        return jnp.concatenate([one, two, one], axis=0)

    def apply(a, stacked):
        one, two = parts(a)
        return jnp.dot(
            jnp.concatenate([one, one, two], axis=1), stacked, preferred_element_type=jnp.float32)

    def build_edges():
        count = inv_ref.shape[2]
        place = lax.broadcasted_iota(jnp.int32, (cz, cz), 0)
        column = lax.broadcasted_iota(jnp.int32, (cz, cz), 1)
        cell = ((place + WIN // 2) // WIN) % cx
        target = cell % WIN + jnp.where(place % WIN < WIN // 2, 0, (count - 1) * WIN)
        total = None
        for g in range(cx // WIN):
            chosen = ((cell // WIN == g) & (column == target)).astype(jnp.float32)
            turned = blocks[g].T
            onto_edge = product(turned, chosen, 1)
            seen_w[g, :, :cz] = weights(turned)
            seen_w[g, :, cz:] = weights(onto_edge)
            fix_rows[g] = weights(product(chosen, turned, 0))
            part = product(chosen, onto_edge, 0)
            total = part if total is None else total + part
        fix_edge[...] = weights(total)

    def observe(src, dst):
        for g in range(cx // WIN):
            sums = fold([src[:, g * WIN + k] for k in range(WIN)])
            total = apply(sums.reshape(comps * cy, cz), seen_w[g, :, :cz]).reshape(comps, cy, cz)
            for k, t in enumerate(unfold(total)):
                dst[:, g * WIN + k] = t

    def build_blocks():
        count = inv_ref.shape[2]
        spread = (
            lax.broadcasted_iota(jnp.int32, (count, cz), 1) // WIN
            == lax.broadcasted_iota(jnp.int32, (count, cz), 0)
        ).astype(jnp.float32)
        for d, source in enumerate((inv_ref, winrecv)):
            lanes_inv[d * owned : (d + 1) * owned] = jnp.dot(
                source[...].reshape(owned * count, count), spread,
                precision=high, preferred_element_type=jnp.float32,
            ).reshape(owned, count, cz) * (1.0 / (WIN * WIN))
        blocks[...] = jnp.zeros(blocks.shape, jnp.float32)
        row = lax.broadcasted_iota(jnp.int32, (WIN, cz), 0)
        col = lax.broadcasted_iota(jnp.int32, (WIN, cz), 1) % WIN

        def add_slot(j, carry):
            owner = jnp.where(j < owned, gx, other)
            cell = plane_s[slot_s[owner * owned + j % owned]] - gx * cx
            for g in range(cx // WIN):
                here = (row == cell - g * WIN) & (col == cell - g * WIN)
                for s in range(count):
                    line = jnp.broadcast_to(lanes_inv[j, s : s + 1, :], (WIN, cz))
                    blocks[g, s * WIN : (s + 1) * WIN, :] += jnp.where(here, line, 0.0)
            return carry

        lax.fori_loop(0, n_gx * owned, add_slot, 0)

    def start(copies):
        for copy in copies:
            copy.start()

    def send_sides(r, src):
        ours = src[:, pl.ds(near_row, 2)]
        for k in range(2):
            xsend[r, k] = ours[:, k]
        for i in range(cx):
            rhs[:, i] = stencil_inside(rows_of(src), i)
        for k in range(2):
            xsend[r, 2 + k] = weighted([(in_s[k, j], rhs[:, j]) for j in range(cx)])
        x_copy(r).start()

    def build_across():
        def spot(j):
            return jnp.where(cell_of == j, 1.0, 0.0)

        corner = across((spot(their_row), spot(their_row + 1)), first)
        inner = [stencil_inside(spot, j) for j in range(cx)]
        own = [in_s[k, near_row] * corner[0] + in_s[k, near_row + 1] * corner[1] for k in range(2)]
        theirs = [weighted([(near_s[k, j], inner[j]) for j in range(cx)]) for k in range(2)]
        values = [
            weighted([(schur_s[2 * gx + m, 2 * gx + k], own[k]) for k in range(2)]
                     + [(schur_s[2 * gx + m, 2 * other + k], theirs[k]) for k in range(2)])
            for m in range(2)
        ]
        lines = [
            weighted([(local_s[i, near_row], corner[0]), (local_s[i, near_row + 1], corner[1]),
                      (out_s[0, i], values[0]), (out_s[1, i], values[1])])
            for i in range(cx)
        ]
        for i in range(cx):
            line = jnp.where(sub < WIN // 2, lines[i], lines[(i + 1) % cx])
            across_x[i * WIN : (i + 1) * WIN] = jnp.where(in_group == sub, line, 0.0)
        across_w[...] = weights(across_x[...].T)

    def side_fix():
        fix_all.wait_recv()
        along_x = apply(fix_near[2].reshape(comps * cy, cz), across_w[...]).reshape(comps, cy, cz)
        after_y, before_y = fix_near[0] - fix_sent[...], fix_near[1] - fix_sent[...]
        along_y = weighted([
            (coef, pltpu.roll(jnp.where(sub < k, after_y, 0.0), cy - k, 1)
             - pltpu.roll(jnp.where(sub >= cy - k, before_y, 0.0), k, 1))
            for k, coef in ((1, C1), (2, C2), (3, C3))
        ])
        return uxy_pack[0] * along_x + uxy_pack[1] * along_y

    def tangent(r, n, src, edge, before_face, finish_src, shadow, close):
        if not r:
            zsend[r] = edge
            pl.semaphore_wait(barrier, n_gx - 1 + 4)
            start(z_copies(r))
            send_y(r, src)
            loads[2].wait()
            table_copy.start()
            loads[1].wait()
            send_sides(r, src)
            for copy in loads[3:]:
                copy.wait()
            win_copy.start()
            for m in range(2):
                for c in range(comps):
                    for i in range(cx):
                        vel[m, c, i] = time_step * base_ref[m, c, i].astype(jnp.float32)
                uz_pack[m] = packed(lambda i: vel[m, 2, i])
                if not m:
                    start(uz_copies)
            yside[...] = jnp.zeros(yside.shape, jnp.float32)
            ends = xsend[r, 0], xsend[r, 1]
            sides = [xsend.at[r, 2 + k] for k in range(2)]
        else:
            finish_src()
            for i in range(cx):
                rhs[:, i] = stencil_inside(rows_of(src), i)
            for k in range(2):
                own_side[k] = weighted([(in_s[k, j], rhs[:, j]) for j in range(cx)])
            ours = src[:, pl.ds(near_row, 2)]
            ends = ours[:, 0], ours[:, 1]
            sides = [own_side.at[k] for k in range(2)]
        for i in range(cx):
            block = src[:, i]
            solved = weighted([(local_s[i, j], rhs[:, j]) for j in range(cx)])
            acc[:, i] = block - (
                vel[n, 2, i] * circular(block, 2) + vel[n, 1, i] * circular(block, 1) + vel[n, 0, i] * solved)
        shadow()
        away = across(ends, gx != 0)
        face = lateral(edge)
        def add_y(c):
            y_fix(r, c)
            for i in range(cx):
                acc[c, i] -= vel[n, 1, i] * yside[c, i]

        for c in range(comps - 1):
            add_y(c)
        x_copy(r).wait_recv()
        halo = across((xrecv[r, 0], xrecv[r, 1]), first)
        own = [
            sides[k][...] + in_s[k, near_row] * halo[0] + in_s[k, near_row + 1] * halo[1] for k in range(2)
        ]
        theirs = [
            xrecv[r, 2 + k] + near_s[k, their_row] * away[0] + near_s[k, their_row + 1] * away[1]
            for k in range(2)
        ]
        values = [
            weighted([(schur_s[2 * gx + m, 2 * gx + k], own[k]) for k in range(2)]
                     + [(schur_s[2 * gx + m, 2 * other + k], theirs[k]) for k in range(2)])
            for m in range(2)
        ]
        for i in range(cx):
            acc[:, i] -= vel[n, 0, i] * weighted([
                (local_s[i, near_row], halo[0]), (local_s[i, near_row + 1], halo[1]),
                (out_s[0, i], values[0]), (out_s[1, i], values[1])])
        add_y(comps - 1)
        closing = close(face)
        if r:
            uz_both.wait_recv()
            missing = facing(uz_near) * before_face
        z_both(r).wait_recv()
        theirs = facing(zrecv.at[r])
        return closing(lateral(theirs - missing if r else theirs)), face

    def close_state(face):
        before = packed(rows_of(acc)) + uz_pack[0] * face
        zsend[1] = before
        start(z_copies(1))
        send_y(1, acc)
        send_sides(1, acc)

        def closing(late):
            fix = uz_pack[0] * (late - face)
            fix_sent[...] = fix
            start(fix_copies)

            def finish():
                for i in range(cx):
                    state_one[:, i] = acc[:, i] - unpacked(fix, i)

            return before - uz_pack[0] * late, finish

        return closing

    def close_observed(face):
        groups = range(cx // WIN)
        before = None
        for g in groups:
            sums = fold([acc[:, g * WIN + k] for k in range(WIN)]).reshape(comps * cy, cz)
            both = apply(sums, seen_w[g])
            mixed[g] = both[:, :cz]
            before = both[:, cz:] if before is None else before + both[:, cz:]

        settle(0)

        def closing(late):
            flat = (uz_pack[1] * (late - face) - side_fix()).reshape(comps * cy, cz)

            def finish():
                for g in groups:
                    total = (mixed[g] - apply(flat, fix_rows[g])).reshape(comps, cy, cz)
                    for k, t in enumerate(unfold(total)):
                        force[:, g * WIN + k] = t

            return (before - apply(flat, fix_edge[...])).reshape(comps, cy, cz), finish

        return closing

    def adjoint(r, n, src, dst, edge, before_face, finish_src, shadow, extra):
        edge = uz_pack[n] * edge
        if before_face is None:
            zsend[r] = edge
            start(z_copies(r))
        finish_src()
        for i in range(cx):
            prod[:, i] = vel[n, 1, i] * src[:, i]
        send_y(r, prod)
        for i in range(cx):
            rhs[:, i] = vel[n, 0, i] * src[:, i]
        for k in range(2):
            xsend[r, k] = weighted([(local_s[j, near_row + k], rhs[:, j]) for j in range(cx)])
            xsend[r, 2 + k] = weighted([(out_s[k, j], rhs[:, j]) for j in range(cx)])
        x_copy(r).start()
        shadow()
        for i in range(cx):
            held[:, i] = weighted([(local_s[j, i], rhs[:, j]) for j in range(cx)])
        for i in range(cx):
            total = src[:, i] + circular(vel[n, 2, i] * src[:, i], 2) + circular(prod[:, i], 1)
            if extra is not None:
                total = total + extra[:, i]
            acc[:, i] = total + stencil_inside(rows_of(held), i)

        def add_y(c):
            y_fix(r, c)
            for i in range(cx):
                acc[c, i] += yside[c, i]

        for c in range(comps - 1):
            add_y(c)
        x_copy(r).wait_recv()

        def solved(block):
            return [
                weighted([(schur_s[2 * gx + k, 2 * block + m], xsend[r, 2 + k]) for k in range(2)]
                         + [(schur_s[2 * other + k, 2 * block + m], xrecv[r, 2 + k]) for k in range(2)])
                for m in range(2)
            ]

        own, theirs = solved(gx), solved(other)
        halo = across([
            xrecv[r, k] + near_s[0, their_row + k] * theirs[0] + near_s[1, their_row + k] * theirs[1]
            for k in range(2)
        ], first)
        for i in range(cx):
            acc[:, i] += weighted([
                (stencil_inside(lambda j, m=m: in_s[m, j], i), own[m]) for m in range(2)])
        for k in range(2):
            acc[:, near_row + k] += halo[k]
        add_y(comps - 1)
        face = lateral(edge)
        if before_face is None:
            before = packed(rows_of(acc)) - face
            zsend[r + 1] = uz_pack[n - 1] * before
            start(z_copies(r + 1))
        else:
            missing = facing(uz_near) * before_face
        settle(r - 1)
        z_both(r).wait_recv()
        theirs = facing(zrecv.at[r])
        late = lateral(theirs if before_face is None else theirs + missing)
        fix = late - face
        after = before + late if before_face is None else None

        def finish():
            for i in range(cx):
                dst[:, i] = acc[:, i] + unpacked(fix, i)

        return after, face, finish

    def table():
        table_copy.wait_recv()
        copy = pltpu.make_async_copy(near_v, near_s, load_sem.at[8])
        copy.start()
        copy.wait()

    def observe_one():
        observe(state_one, obs)

    def tables():
        win_copy.wait_recv()
        build_blocks()
        build_edges()
        build_across()
        for c in range(2):
            uxy_pack[c] = packed(lambda i: vel[1, c, i])

    def nothing():
        pass

    loads[0].wait()
    (edge, finish), face = tangent(
        0, 0, dir_ref, packed(rows_of(dir_ref)), None, nothing, table, close_state)
    (edge, finish), face = tangent(1, 1, state_one, edge, face, finish, tables, close_observed)
    edge, face, finish = adjoint(2, 1, force, costate, edge, None, finish, observe_one, obs)
    edge, face, finish = adjoint(3, 0, costate, res_ref, edge, face, finish, nothing, dir_ref)
    finish()
    settle(3)
    win_copy.wait_send()
    uz_both.wait_send()
    fix_all.wait_send()
    table_copy.wait_send()


def solution(mesh):
    sizes = tuple(mesh.shape[name] for name in ("gx", "gy", "gz"))

    def local(direction, base_flow, local_inv, couple_in, couple_out, schur_inv,
              plane_x, slot_plane, window_inv):
        n_gx = sizes[0]
        comps, cx, cy, cz = direction.shape
        owned, count = window_inv.shape[0], window_inv.shape[3]
        wide = 3
        field = pltpu.VMEM(direction.shape, jnp.float32)

        def held(*shape):
            return pltpu.VMEM(shape, jnp.float32)

        sems = pltpu.SemaphoreType.DMA
        vmem = pl.BlockSpec(memory_space=pltpu.VMEM)
        kept = functools.partial(pltpu.with_memory_space_constraint, memory_space=pltpu.HBM)
        hbm = pl.BlockSpec(memory_space=pltpu.HBM)
        tables = (local_inv, couple_in, couple_out.T, schur_inv, plane_x, slot_plane)
        operands = tuple(map(kept, (direction, base_flow, window_inv.reshape(owned, count, count)) + tables))
        call = functools.partial(
            pl.pallas_call,
            out_shape=jax.ShapeDtypeStruct(direction.shape, jnp.float32),
            in_specs=[hbm] * 9,
            out_specs=vmem,
            compiler_params=pltpu.CompilerParams(collective_id=0, has_side_effects=True, vmem_limit_bytes=16 * 2**20),
        )
        loaded = [
            field, pltpu.VMEM(base_flow.shape, base_flow.dtype), held(owned, count, count),
        ] + [pltpu.SMEM(t.shape, t.dtype) for t in tables]
        if n_gx == 2:
            pulled = call(
                functools.partial(pair_kernel, sizes),
                scratch_shapes=loaded + [
                    held(2, cx), held(2, cx), pltpu.SMEM((2, cx), jnp.float32),
                ] + [field] * 9 + [
                    held(*base_flow.shape), held(2, cy, cz),
                    held(4, 4, comps, cy, cz), held(4, 4, comps, cy, cz),
                    held(4, comps, 2, wide, cx, cz), held(4, comps, 2, wide, cx, cz),
                    held(4, comps, cy, cz), held(4, 2, comps, cy, cz),
                    held(owned, count, count), held(n_gx * owned, count, cz), held(cx // WIN, count * WIN, cz),
                    pltpu.VMEM((cx // WIN, 3 * cz, 2 * cz), jnp.bfloat16),
                    pltpu.VMEM((cx // WIN, 3 * cz, cz), jnp.bfloat16), pltpu.VMEM((3 * cz, cz), jnp.bfloat16),
                    held(cx // WIN, comps * cy, cz), held(2, cy, cz),
                    held(2, comps, cy, cz), held(comps, cy, cz), held(3, comps, cy, cz),
                    held(cz, cz), pltpu.VMEM((3 * cz, cz), jnp.bfloat16), held(2, cy, cz),
                    sems((10,)), sems((1,)), sems((4,)), sems((2,)), sems((2, comps)), sems((4,)),
                ],
            )(*operands)
            return pulled
        pulled = call(
            functools.partial(kernel, sizes),
            scratch_shapes=loaded + [
                held(2, cx), held(2, 2, cx), pltpu.SMEM((2, 2, cx), jnp.float32),
                held(n_gx, 2, comps, cy, cz), held(2, comps, 2, cy, cz),
                sems((10,)), sems((1,)), sems((2,)), sems((2,)),
            ] + [field] * 8 + [
                held(2, comps, cx, cy, cz),
                field,
                held(4, 2, comps, 2, cy, cz),
                held(4, 2, wide, comps, cx, cz),
                held(4, 2, wide, comps, cx, cz),
                held(4, comps, cy, cz),
                held(4, 2, comps, cy, cz),
                held(4, n_gx, 2, comps, cy, cz),
                held(n_gx - 1, owned, count, count),
                held(n_gx * owned, count, cz),
                held(cx // WIN, count * WIN, cz),
                sems((4, 2)), sems((4, 2)), sems((4, 2)), sems((4, 2)), sems((4, 2)), sems((4, 2)),
                sems((4, n_gx)), sems((4, n_gx)), sems((n_gx,)), sems((n_gx,)),
            ],
        )(*operands)
        return pulled + direction

    return jax.shard_map(
        local,
        mesh=mesh,
        in_specs=(
            P(None, "gx", "gy", "gz"),
            P(None, None, "gx", "gy", "gz"),
            P("gx", None),
            P("gx", None),
            P("gx", None),
            P(),
            P(),
            P(),
            P("gx", "gy", "gz", None, None),
        ),
        out_specs=P(None, "gx", "gy", "gz"),
        check_vma=False,
    )
```

```python
import functools

import jax
import jax.numpy as jnp
from jax import lax
from jax.experimental import pallas as pl
from jax.experimental.pallas import tpu as pltpu
from jax.sharding import PartitionSpec as P

WIN = 8
time_step = 0.15
NEAR = 7.0 / 9.0
FAR = 1.0 / 36.0
C1 = 45.0 / 60.0
C2 = -9.0 / 60.0
C3 = 1.0 / 60.0
MESH = pl.DeviceIdType.MESH
high = lax.Precision.HIGHEST


def weighted(terms):
    chains = [None, None]
    for n, (coef, block) in enumerate(terms):
        part = coef * block
        chains[n % 2] = part if chains[n % 2] is None else chains[n % 2] + part
    return chains[0] if chains[1] is None else chains[0] + chains[1]


def kernel(
    sizes,
    dir_hbm, base_hbm, inv_hbm,
    local_h, in_h, out_h, schur_h, plane_h, slot_h,
    res_ref,
    dir_ref, base_ref, inv_ref, local_s, in_s, out_s, schur_s, plane_s, slot_s, in_v, near_v, near_s, esend, halo, load_sem, table_sem, ts_sem, tr_sem,
    state_one, state_two, force, acc, rhs, obs, prod_y, prod_z, hbuf,
    yside, xrecv, ysend, yrecv, zsend, zrecv, edge, winrecv, lanes_inv, blocks,
    xs_sem, xr_sem, ys_sem, yr_sem, zs_sem, zr_sem, es_sem, er_sem, ws_sem, wr_sem,
):
    n_gx, n_gy, n_gz = sizes
    gx, gy, gz = lax.axis_index("gx"), lax.axis_index("gy"), lax.axis_index("gz")
    comps, cx, cy, cz = dir_ref.shape
    wide = ysend.shape[2]
    loads = [
        pltpu.make_async_copy(src, dst, load_sem.at[n])
        for n, (src, dst) in enumerate((
            (dir_hbm, dir_ref), (in_h, in_s), (schur_h, schur_s), (local_h, local_s),
            (out_h, out_s), (plane_h, plane_s), (slot_h, slot_s),
            (base_hbm, base_ref), (inv_hbm, inv_ref), (in_h, in_v),
        ))
    ]
    owned = inv_ref.shape[0]
    y_next, y_prev = lax.rem(gy + 1, n_gy), lax.rem(gy + n_gy - 1, n_gy)
    z_next, z_prev = lax.rem(gz + 1, n_gz), lax.rem(gz + n_gz - 1, n_gz)

    @pl.when(gx == 0)
    def _():
        xrecv[:, 0] = jnp.zeros(xrecv.shape[:1] + xrecv.shape[2:], jnp.float32)

    @pl.when(gx == n_gx - 1)
    def _():
        xrecv[:, 1] = jnp.zeros(xrecv.shape[:1] + xrecv.shape[2:], jnp.float32)

    barrier = pltpu.get_barrier_semaphore()
    for d in range(1, n_gx):
        pl.semaphore_signal(barrier, device_id={"gx": lax.rem(gx + d, n_gx)}, device_id_type=MESH)
    for q in (y_prev, y_next):
        pl.semaphore_signal(barrier, device_id={"gy": q}, device_id_type=MESH)
    for q in (z_prev, z_next):
        pl.semaphore_signal(barrier, device_id={"gz": q}, device_id_type=MESH)

    for copy in loads:
        copy.start()

    def remote(src, dst, send, recv, where):
        return pltpu.make_async_remote_copy(
            src_ref=src, dst_ref=dst, send_sem=send, recv_sem=recv,
            device_id=where, device_id_type=MESH,
        )

    lane = lax.broadcasted_iota(jnp.int32, (comps, cy, cz), 2)
    sub = lax.broadcasted_iota(jnp.int32, (comps, cy, cz), 1)
    in_group = lane % WIN

    def x_copies(r, src):
        right = remote(src.at[:, cx - 2 : cx], xrecv.at[r, 0], xs_sem.at[r, 0], xr_sem.at[r, 0],
                       {"gx": lax.rem(gx + 1, n_gx)})
        left = remote(src.at[:, 0:2], xrecv.at[r, 1], xs_sem.at[r, 1], xr_sem.at[r, 1],
                      {"gx": lax.rem(gx + n_gx - 1, n_gx)})
        return right, left

    def x_start(copies):
        right, left = copies

        @pl.when(gx < n_gx - 1)
        def _():
            right.start()

        @pl.when(gx > 0)
        def _():
            left.start()

    def x_arrived(copies):
        right, left = copies

        @pl.when(gx > 0)
        def _():
            right.wait_recv()

        @pl.when(gx < n_gx - 1)
        def _():
            left.wait_recv()

    def x_sent(copies):
        right, left = copies

        @pl.when(gx < n_gx - 1)
        def _():
            right.wait_send()

        @pl.when(gx > 0)
        def _():
            left.wait_send()

    def y_copies(r):
        return (
            remote(ysend.at[r, 0], yrecv.at[r, 0], ys_sem.at[r, 0], yr_sem.at[r, 0], {"gy": y_prev}),
            remote(ysend.at[r, 1], yrecv.at[r, 1], ys_sem.at[r, 1], yr_sem.at[r, 1], {"gy": y_next}),
        )

    def z_copies(r):
        return (
            remote(zsend.at[r], zrecv.at[r, 0], zs_sem.at[r, 0], zr_sem.at[r, 0], {"gz": z_prev}),
            remote(zsend.at[r], zrecv.at[r, 1], zs_sem.at[r, 1], zr_sem.at[r, 1], {"gz": z_next}),
        )

    def edge_copies(r):
        return tuple(
            remote(edge.at[r, 0], edge.at[r, d], es_sem.at[r, d], er_sem.at[r, d],
                   {"gx": lax.rem(gx + d, n_gx)})
            for d in range(1, n_gx)
        )

    win_copies = tuple(
        remote(inv_ref, winrecv.at[d - 1], ws_sem.at[d], wr_sem.at[d], {"gx": lax.rem(gx + d, n_gx)})
        for d in range(1, n_gx)
    )

    table_copies = (
        remote(in_v, near_v.at[0], ts_sem.at[0], tr_sem.at[0], {"gx": lax.rem(gx + 1, n_gx)}),
        remote(in_v, near_v.at[1], ts_sem.at[1], tr_sem.at[1], {"gx": lax.rem(gx + n_gx - 1, n_gx)}),
    )
    left_one = jnp.where(gx > 0, 1.0, 0.0)
    right_one = jnp.where(gx < n_gx - 1, 1.0, 0.0)
    left_id, right_id = lax.rem(gx + n_gx - 1, n_gx), lax.rem(gx + 1, n_gx)

    def start(copies):
        for copy in copies:
            copy.start()

    def arrived(copies):
        for copy in copies:
            copy.wait_recv()

    def pack_y(r, src):
        lines = src.reshape(comps * cx * cy, cz)
        for c in range(comps):
            for m in range(wide):
                for side, row in ((0, m), (1, cy - wide + m)):
                    ysend[r, side, m, c] = lines[pl.ds(c * cx * cy + row, cx, stride=cy), :]

    def pack_z(r, src):
        packed = None
        for i in range(cx):
            block = src[:, i]
            turned = block if i == 0 else pltpu.roll(block, WIN * i, 2)
            if packed is None:
                packed = turned
            else:
                packed = jnp.where((lane >= WIN * i - 4) & (lane < WIN * i + 4), turned, packed)
        zsend[r] = packed

    def circular_z(block):
        def diff(k):
            return pltpu.roll(block, cz - k, 2) - pltpu.roll(block, k, 2)

        return C1 * diff(1) + C2 * diff(2) + C3 * diff(3)

    def z_fix(r):
        true = jnp.where(in_group < 4, zrecv[r, 0], zrecv[r, 1])
        delta = true - zsend[r]
        low = jnp.where(in_group >= WIN - 3, delta, 0.0)
        top = jnp.where(in_group < 3, delta, 0.0)
        low_fix = -(C1 * pltpu.roll(low, 1, 2) + C2 * pltpu.roll(low, 2, 2) + C3 * pltpu.roll(low, 3, 2))
        top_fix = (C1 * pltpu.roll(top, cz - 1, 2) + C2 * pltpu.roll(top, cz - 2, 2)
                   + C3 * pltpu.roll(top, cz - 3, 2))
        return jnp.where(in_group < 3, low_fix, 0.0) + jnp.where(in_group >= WIN - 3, top_fix, 0.0)

    def z_fix_of(fix, i):
        turned = fix if i == 0 else pltpu.roll(fix, (cz - WIN * i) % cz, 2)
        return jnp.where((lane < 3) | (lane >= cz - 3), turned, 0.0)

    def fill_sides(r):
        lines = yside.reshape(comps * cx * cy, cz)
        for c in range(comps):
            for m in range(wide):
                for side, row in ((0, m), (1, cy - wide + m)):
                    lines[pl.ds(c * cx * cy + row, cx, stride=cy), :] = yrecv[r, side, m, c]

    def along_y(block, side):
        def diff(k):
            ahead = pltpu.roll(jnp.where(sub < k, side, block), cy - k, 1)
            behind = pltpu.roll(jnp.where(sub >= cy - k, side, block), k, 1)
            return ahead - behind

        return C1 * diff(1) + C2 * diff(2) + C3 * diff(3)

    def stencil_x(src, sides, i):
        def row(n):
            if n < 0:
                return sides[0, :, n + 2]
            if n >= cx:
                return sides[1, :, n - cx]
            return src[:, n]

        return NEAR * (row(i + 1) - row(i - 1)) + FAR * (row(i + 2) - row(i - 2))

    def stencil_inside(src, i):
        total = None
        for offset, coef in ((1, NEAR), (-1, -NEAR), (2, FAR), (-2, -FAR)):
            if 0 <= i + offset < cx:
                part = coef * src[:, i + offset]
                total = part if total is None else total + part
        return total

    def velocity(n, c, i):
        return base_ref[n, c, i].astype(jnp.float32)[None]

    def fold(blocks8):
        level, m = list(blocks8), 1
        while len(level) > 1:
            keep = (lane & m) == 0
            level = [
                jnp.where(keep, a + pltpu.roll(a, cz - m, 2), b + pltpu.roll(b, m, 2))
                for a, b in zip(level[0::2], level[1::2])
            ]
            m *= 2
        return level[0]

    def unfold(block):
        level, m = [block], WIN // 2
        while m >= 1:
            keep = (lane & m) == 0
            wider = []
            for t in level:
                wider.append(jnp.where(keep, t, pltpu.roll(t, m, 2)))
                wider.append(jnp.where(keep, pltpu.roll(t, cz - m, 2), t))
            level = wider
            m //= 2
        return level

    def observe(src, dst):
        for g in range(cx // WIN):
            sums = fold([src[:, g * WIN + k] for k in range(WIN)])
            mixed = lax.dot_general(
                sums.reshape(comps * cy, cz), blocks[g], (((1,), (1,)), ((), ())),
                precision=high, preferred_element_type=jnp.float32,
            ).reshape(comps, cy, cz)
            for k, t in enumerate(unfold(mixed)):
                dst[:, g * WIN + k] = t

    def build_blocks():
        count = inv_ref.shape[2]
        spread = (
            lax.broadcasted_iota(jnp.int32, (count, cz), 1) // WIN
            == lax.broadcasted_iota(jnp.int32, (count, cz), 0)
        ).astype(jnp.float32)
        for d in range(n_gx):
            source = inv_ref[...] if d == 0 else winrecv[d - 1]
            lanes_inv[d * owned : (d + 1) * owned] = jnp.dot(
                source.reshape(owned * count, count), spread,
                precision=high, preferred_element_type=jnp.float32,
            ).reshape(owned, count, cz) * (1.0 / (WIN * WIN))
        blocks[...] = jnp.zeros(blocks.shape, jnp.float32)
        row = lax.broadcasted_iota(jnp.int32, (WIN, cz), 0)
        col = lax.broadcasted_iota(jnp.int32, (WIN, cz), 1) % WIN

        def add_slot(j, carry):
            owner = lax.rem(gx + n_gx - j // owned, n_gx)
            cell = plane_s[slot_s[owner * owned + j % owned]] - gx * cx
            for g in range(cx // WIN):
                here = (row == cell - g * WIN) & (col == cell - g * WIN)
                for s in range(count):
                    line = jnp.broadcast_to(lanes_inv[j, s : s + 1, :], (WIN, cz))
                    blocks[g, s * WIN : (s + 1) * WIN, :] += jnp.where(here, line, 0.0)
            return carry

        lax.fori_loop(0, n_gx * owned, add_slot, 0)

    def interface(r, block, m, transposed):
        terms = []
        for d in range(n_gx):
            owner = lax.rem(gx + n_gx - d, n_gx)
            for k in range(2):
                n, own = 2 * owner + k, 2 * block + m
                coef = schur_s[n, own] if transposed else schur_s[own, n]
                terms.append((coef, edge[r, d, k]))
        return weighted(terms)

    def early_copies(r):
        return tuple(
            remote(esend.at[d], edge.at[r, d], es_sem.at[r, d], er_sem.at[r, d],
                   {"gx": lax.rem(gx + d, n_gx)})
            for d in range(1, n_gx)
        )

    def early_shares(r, src):
        for i in range(cx):
            rhs[:, i] = stencil_inside(src, i)
        below = (NEAR * src[:, 0] + FAR * src[:, 1], FAR * src[:, 0])
        above = (-(NEAR * src[:, cx - 1] + FAR * src[:, cx - 2]), -FAR * src[:, cx - 1])
        parts = []
        for k in range(2):
            parts.append((2 * gx + k, weighted([(in_s[k, j], rhs[:, j]) for j in range(cx)])))
            parts.append((2 * right_id + k, right_one * (
                near_s[1, k, 0] * above[0] + near_s[1, k, 1] * above[1])))
            parts.append((2 * left_id + k, left_one * (
                near_s[0, k, cx - 1] * below[0] + near_s[0, k, cx - 2] * below[1])))
        for d in tuple(range(1, n_gx)) + (0,):
            owner = lax.rem(gx + d, n_gx)
            for m in range(2):
                share = weighted([(schur_s[2 * owner + m, n], part) for n, part in parts])
                if d == 0:
                    edge[r, 0, m] = share
                else:
                    esend[d, m] = share

    sent = []

    def tangent(r, n, src, dst, first, shadow):
        xc, yc, zc = x_copies(r, src), y_copies(r), z_copies(r)
        ec = edge_copies(r) if first else early_copies(r)
        if first:
            loads[0].wait()
        else:
            x_start(xc)
        pack_z(r, src)
        if not first:
            start(zc)
        pack_y(r, src)
        if first:
            pl.semaphore_wait(barrier, n_gx - 1 + 4)
            x_start(xc)
            start(zc)
        start(yc)
        if not first:
            early_shares(r, src)
            start(ec)
        sent.append((xc, yc + zc + ec))
        if first:
            for copy in loads[1:]:
                copy.wait()
            start(table_copies)
        for i in range(cx):
            block = src[:, i]
            acc[:, i] = block - time_step * (velocity(n, 2, i) * circular_z(block))
        x_arrived(xc)
        for i in range(cx) if first else (0, 1, cx - 2, cx - 1):
            rhs[:, i] = stencil_x(src, xrecv.at[r], i)
        if first:
            for k in range(2):
                edge[r, 0, k] = weighted([(in_s[k, j], rhs[:, j]) for j in range(cx)])
            start(ec)
            start(win_copies)
        for i in range(cx):
            solved = weighted([(local_s[i, j], rhs[:, j]) for j in range(cx)])
            acc[:, i] -= time_step * (velocity(n, 0, i) * solved)
        if first:
            arrived(table_copies)
            table = pltpu.make_async_copy(near_v, near_s, table_sem.at[0])
            table.start()
            table.wait()
        shadow()
        arrived(yc)
        fill_sides(r)
        for i in range(cx):
            acc[:, i] -= time_step * (velocity(n, 1, i) * along_y(src[:, i], yside[:, i]))
        arrived(zc)
        fix = z_fix(r)
        arrived(ec)
        if first:
            values = [interface(r, gx, m, False) for m in range(2)]
        else:
            values = [weighted([(1.0, edge[r, d, m]) for d in range(n_gx)]) for m in range(2)]
        for i in range(cx):
            pulled = out_s[0, i] * values[0] + out_s[1, i] * values[1]
            dst[:, i] = acc[:, i] - time_step * (
                velocity(n, 0, i) * pulled + velocity(n, 2, i) * z_fix_of(fix, i)
            )

    def adjoint(r, n, src, dst, extra):
        xc, yc, zc, ec = x_copies(r, hbuf.at[r - 2]), y_copies(r), z_copies(r), edge_copies(r)
        sent.append((xc, yc + zc + ec))
        held = hbuf.at[r - 2]
        for i in range(cx):
            prod_z[:, i] = velocity(n, 2, i) * src[:, i]
        pack_z(r, prod_z)
        start(zc)
        for i in range(cx):
            prod_y[:, i] = velocity(n, 1, i) * src[:, i]
        pack_y(r, prod_y)
        start(yc)
        for i in range(cx):
            rhs[:, i] = velocity(n, 0, i) * src[:, i]
        for k in range(2):
            edge[r, 0, k] = weighted([(out_s[k, i], rhs[:, i]) for i in range(cx)])
        start(ec)
        order = (0, 1, cx - 2, cx - 1) + tuple(range(2, cx - 2))
        for place, i in enumerate(order):
            held[:, i] = weighted([(local_s[j, i], rhs[:, j]) for j in range(cx)])
            if place == 3:
                x_start(xc)
        for i in range(cx):
            total = src[:, i] + time_step * circular_z(prod_z[:, i])
            acc[:, i] = total if extra is None else total + extra[:, i]
        arrived(ec)
        values = [interface(r, gx, m, True) for m in range(2)]
        lower = [left_one * interface(r, left_id, m, True) for m in range(2)]
        upper = [right_one * interface(r, right_id, m, True) for m in range(2)]
        for i in range(cx):
            rhs[:, i] = held[:, i] + (in_s[0, i] * values[0] + in_s[1, i] * values[1])
        for i in range(2, cx - 2):
            acc[:, i] += time_step * stencil_x(rhs, halo, i)
        x_arrived(xc)
        for n in range(2):
            halo[0, :, n] = xrecv[r, 0, :, n] + (
                near_s[0, 0, cx - 2 + n] * lower[0] + near_s[0, 1, cx - 2 + n] * lower[1])
            halo[1, :, n] = xrecv[r, 1, :, n] + (
                near_s[1, 0, n] * upper[0] + near_s[1, 1, n] * upper[1])
        for i in (0, 1, cx - 2, cx - 1):
            acc[:, i] += time_step * stencil_x(rhs, halo, i)
        arrived(yc)
        fill_sides(r)
        for i in range(cx):
            acc[:, i] += time_step * along_y(prod_y[:, i], yside[:, i])
        arrived(zc)
        fix = z_fix(r)
        for i in range(cx):
            dst[:, i] = acc[:, i] + time_step * z_fix_of(fix, i)

    def nothing():
        pass

    def observe_one():
        arrived(win_copies)
        build_blocks()
        observe(state_one, obs)

    tangent(0, 0, dir_ref, state_one, True, nothing)
    tangent(1, 1, state_one, state_two, False, observe_one)
    observe(state_two, force)
    adjoint(2, 1, force, state_two, obs)
    adjoint(3, 0, state_two, res_ref, None)
    for xc, rest in sent:
        x_sent(xc)
        for copy in rest:
            copy.wait_send()
    for copy in win_copies + table_copies:
        copy.wait_send()


def pair_kernel(
    sizes,
    dir_hbm, base_hbm, inv_hbm,
    local_h, in_h, out_h, schur_h, plane_h, slot_h,
    res_ref,
    dir_ref, base_ref, inv_ref, local_s, in_s, out_s, schur_s, plane_s, slot_s, in_v, near_v, near_s, slope_s,
    state_one, costate, force, acc, rhs, obs, prod, held, yside, vel, uz_pack,
    xsend, xrecv, ysend, yrecv, zsend, zrecv, winrecv, lanes_inv, blocks, seen_w, fix_rows, fix_edge, mixed, uz_near,
    own_side, fix_sent, fix_near, across_x, across_w, uxy_pack,
    load_sem, sent_sem, side_sem, xr_sem, yr_sem, zr_sem,
):
    n_gx, n_gy, n_gz = sizes
    gx, gy, gz = lax.axis_index("gx"), lax.axis_index("gy"), lax.axis_index("gz")
    comps, cx, cy, cz = dir_ref.shape
    wide = ysend.shape[3]
    owned = inv_ref.shape[0]
    other = 1 - gx
    y_next, y_prev = lax.rem(gy + 1, n_gy), lax.rem(gy + n_gy - 1, n_gy)
    z_next, z_prev = lax.rem(gz + 1, n_gz), lax.rem(gz + n_gz - 1, n_gz)
    first = gx == 0
    near_row = jnp.where(first, cx - 2, 0)
    their_row = jnp.where(first, 0, cx - 2)

    barrier = pltpu.get_barrier_semaphore()
    for q in (z_prev, z_next):
        pl.semaphore_signal(barrier, device_id={"gz": q}, device_id_type=MESH)
    pl.semaphore_signal(barrier, device_id={"gx": other}, device_id_type=MESH)
    for q in (y_prev, y_next):
        pl.semaphore_signal(barrier, device_id={"gy": q}, device_id_type=MESH)

    loads = [
        pltpu.make_async_copy(src, dst, load_sem.at[n])
        for n, (src, dst) in enumerate((
            (dir_hbm, dir_ref), (in_h, in_s), (in_h, in_v), (base_hbm, base_ref), (local_h, local_s),
            (schur_h, schur_s), (out_h, out_s), (plane_h, plane_s), (slot_h, slot_s), (inv_hbm, inv_ref),
        ))
    ]
    for copy in loads:
        copy.start()

    def remote(src, dst, send, recv, where):
        return pltpu.make_async_remote_copy(
            src_ref=src, dst_ref=dst, send_sem=send, recv_sem=recv,
            device_id=where, device_id_type=MESH,
        )

    x_sent = [load_sem.at[n] for n in (1, 7, 1, 7)]
    y_sent = [sent_sem.at[0], load_sem.at[6]] * 2
    z_sent = [load_sem.at[n] for n in (0, 5, 0, 8)]

    def x_copy(r, c):
        return remote(xsend.at[r, c], xrecv.at[r, c], x_sent[r], xr_sem.at[r % 2, c], {"gx": other})

    def x_all(r):
        return remote(xsend.at[r], xrecv.at[r], x_sent[r], xr_sem.at[r % 2, 0], {"gx": other})

    def y_copies(r, c):
        return tuple(
            remote(ysend.at[r, c, d], yrecv.at[r, c, d], y_sent[r], yr_sem.at[r % 2, c], {"gy": q})
            for d, q in enumerate((y_prev, y_next))
        )

    def z_copies(r):
        return tuple(
            remote(zsend.at[r], zrecv.at[r, d], z_sent[r], zr_sem.at[r], {"gz": q})
            for d, q in enumerate((z_prev, z_next))
        )

    uz_copies = tuple(
        remote(uz_pack.at[0], uz_near.at[d], load_sem.at[4], side_sem.at[2], {"gz": q})
        for d, q in enumerate((z_prev, z_next))
    )
    uz_both = remote(uz_near, uz_near, load_sem.at[4], side_sem.at[2], {"gz": z_next})

    fix_copies = tuple(
        remote(fix_sent, fix_near.at[d], load_sem.at[9], side_sem.at[3], where)
        for d, where in enumerate(({"gy": y_prev}, {"gy": y_next}, {"gx": other}))
    )
    fix_all = remote(fix_near, fix_near, load_sem.at[9], side_sem.at[3], {"gx": other})

    def y_both(r, c):
        return remote(yrecv.at[r, c], yrecv.at[r, c], y_sent[r], yr_sem.at[r % 2, c], {"gy": y_next})

    def y_all(r):
        return remote(yrecv.at[r], yrecv.at[r], y_sent[r], yr_sem.at[r % 2, 0], {"gy": y_next})

    def z_both(r):
        return remote(zrecv.at[r], zrecv.at[r], z_sent[r], zr_sem.at[r], {"gz": z_next})

    def settle(r):
        if r >= 0:
            x_all(r).wait_send()
            y_all(r).wait_send()
            z_both(r).wait_send()

    win_copy = remote(inv_ref, winrecv, load_sem.at[3], side_sem.at[0], {"gx": other})
    table_copy = remote(in_v, near_v, load_sem.at[2], side_sem.at[1], {"gx": other})

    lane = lax.broadcasted_iota(jnp.int32, (cy, cz), 1)
    in_group = lane % WIN
    cell_of = ((lane + WIN // 2) // WIN) % cx
    sub = lax.broadcasted_iota(jnp.int32, (cy, cz), 0)
    near_edge = (lane < 3) | (lane >= cz - 3)
    left, right = in_group < 3, in_group >= WIN - 3
    ahead = in_group < WIN // 2

    def packed(block_of):
        total = None
        for i in range(cx):
            block = block_of(i)
            turned = block if i == 0 else pltpu.roll(block, WIN * i, block.ndim - 1)
            total = turned if total is None else jnp.where(cell_of == i, turned, total)
        return total

    def unpacked(block, i):
        turned = block if i == 0 else pltpu.roll(block, (cz - WIN * i) % cz, 2)
        return jnp.where(near_edge, turned, 0.0)

    def send_y(r, c, src):
        lines = src.reshape(comps * cx * cy, cz)
        for side, begin in ((0, 0), (1, cy - wide)):
            for m in range(wide):
                ysend[r, c, side, m] = lines[pl.ds(c * cx * cy + begin + m, cx, stride=cy), :]
        start(y_copies(r, c))

    def circular(block, axis):
        size = block.shape[axis]

        def diff(k):
            return pltpu.roll(block, size - k, axis) - pltpu.roll(block, k, axis)

        return C1 * diff(1) + C2 * diff(2) + C3 * diff(3)

    def lateral(edge):
        low = jnp.where(right, edge, 0.0)
        top = jnp.where(left, edge, 0.0)
        low_fix = -(C1 * pltpu.roll(low, 1, 2) + C2 * pltpu.roll(low, 2, 2) + C3 * pltpu.roll(low, 3, 2))
        top_fix = (C1 * pltpu.roll(top, cz - 1, 2) + C2 * pltpu.roll(top, cz - 2, 2)
                   + C3 * pltpu.roll(top, cz - 3, 2))
        return jnp.where(left, low_fix, jnp.where(right, top_fix, 0.0))

    def facing(pair):
        return jnp.where(ahead, pair[0], pair[1])

    def y_fix(r, c):
        y_both(r, c).wait_recv()
        lines = yside.reshape(comps * cx * cy, cz)

        def put(row, value):
            lines[pl.ds(c * cx * cy + row, cx, stride=cy), :] = value

        d0, d1, d2 = (yrecv[r, c, 0, m] - ysend[r, c, 0, m] for m in range(3))
        put(cy - 1, C1 * d0 + C2 * d1 + C3 * d2)
        put(cy - 2, C2 * d0 + C3 * d1)
        put(cy - 3, C3 * d0)
        d0, d1, d2 = (yrecv[r, c, 1, m] - ysend[r, c, 1, m] for m in range(3))
        put(0, -(C1 * d2 + C2 * d1 + C3 * d0))
        put(1, -(C2 * d2 + C3 * d1))
        put(2, -(C3 * d2))

    def stencil_inside(row, i):
        total = None
        for step, coef in ((1, NEAR), (2, FAR)):
            up, down = i + step < cx, i - step >= 0
            if up and down:
                part = coef * (row(i + step) - row(i - step))
            elif up:
                part = coef * row(i + step)
            elif down:
                part = -coef * row(i - step)
            else:
                continue
            total = part if total is None else total + part
        return total

    def rows_of(ref, c=slice(None)):
        return lambda i: ref[c, i]

    def across(pair, to_first):
        low, high = pair
        upper = (FAR * low, NEAR * low + FAR * high)
        lower = (-(NEAR * high + FAR * low), -FAR * high)
        return tuple(jnp.where(to_first, u, d) for u, d in zip(upper, lower))

    def fold(blocks8):
        level, m = list(blocks8), 1
        while len(level) > 1:
            keep = (lane & m) == 0
            level = [
                jnp.where(keep, a + pltpu.roll(a, cz - m, 2), b + pltpu.roll(b, m, 2))
                for a, b in zip(level[0::2], level[1::2])
            ]
            m *= 2
        return level[0]

    def unfold(block):
        level, m = [block], WIN // 2
        while m >= 1:
            keep = (lane & m) == 0
            wider = []
            for t in level:
                wider.append(jnp.where(keep, t, pltpu.roll(t, m, 2)))
                wider.append(jnp.where(keep, pltpu.roll(t, cz - m, 2), t))
            level = wider
            m //= 2
        return level

    def product(a, b, side):
        return lax.dot_general(
            a, b, (((1,), (side,)), ((), ())), precision=high, preferred_element_type=jnp.float32)

    def parts(a):
        high_part = a.astype(jnp.bfloat16)
        return high_part, (a - high_part.astype(jnp.float32)).astype(jnp.bfloat16)

    def weights(a):
        one, two = parts(a)
        return jnp.concatenate([one, two, one], axis=0)

    def apply(a, stacked):
        one, two = parts(a)
        return jnp.dot(
            jnp.concatenate([one, one, two], axis=1), stacked, preferred_element_type=jnp.float32)

    def build_edges():
        count = inv_ref.shape[2]
        place = lax.broadcasted_iota(jnp.int32, (cz, cz), 0)
        column = lax.broadcasted_iota(jnp.int32, (cz, cz), 1)
        cell = ((place + WIN // 2) // WIN) % cx
        target = cell % WIN + jnp.where(place % WIN < WIN // 2, 0, (count - 1) * WIN)
        total = None
        for g in range(cx // WIN):
            chosen = ((cell // WIN == g) & (column == target)).astype(jnp.float32)
            turned = blocks[g].T
            onto_edge = product(turned, chosen, 1)
            seen_w[g, :, :cz] = weights(turned)
            seen_w[g, :, cz:] = weights(onto_edge)
            fix_rows[g] = weights(product(chosen, turned, 0))
            part = product(chosen, onto_edge, 0)
            total = part if total is None else total + part
        fix_edge[...] = weights(total)

    def observe(src, dst):
        for g in range(cx // WIN):
            sums = fold([src[:, g * WIN + k] for k in range(WIN)])
            total = apply(sums.reshape(comps * cy, cz), seen_w[g, :, :cz]).reshape(comps, cy, cz)
            for k, t in enumerate(unfold(total)):
                dst[:, g * WIN + k] = t

    def build_blocks():
        count = inv_ref.shape[2]
        spread = (
            lax.broadcasted_iota(jnp.int32, (count, cz), 1) // WIN
            == lax.broadcasted_iota(jnp.int32, (count, cz), 0)
        ).astype(jnp.float32)
        for d, source in enumerate((inv_ref, winrecv)):
            lanes_inv[d * owned : (d + 1) * owned] = jnp.dot(
                source[...].reshape(owned * count, count), spread,
                precision=high, preferred_element_type=jnp.float32,
            ).reshape(owned, count, cz) * (1.0 / (WIN * WIN))
        blocks[...] = jnp.zeros(blocks.shape, jnp.float32)
        row = lax.broadcasted_iota(jnp.int32, (WIN, cz), 0)
        col = lax.broadcasted_iota(jnp.int32, (WIN, cz), 1) % WIN

        def add_slot(j, carry):
            owner = jnp.where(j < owned, gx, other)
            cell = plane_s[slot_s[owner * owned + j % owned]] - gx * cx
            for g in range(cx // WIN):
                here = (row == cell - g * WIN) & (col == cell - g * WIN)
                for s in range(count):
                    line = jnp.broadcast_to(lanes_inv[j, s : s + 1, :], (WIN, cz))
                    blocks[g, s * WIN : (s + 1) * WIN, :] += jnp.where(here, line, 0.0)
            return carry

        lax.fori_loop(0, n_gx * owned, add_slot, 0)

    def start(copies):
        for copy in copies:
            copy.start()

    def send_sides(r, c, src):
        xsend[r, c, 0:2] = src[c, pl.ds(near_row, 2)]
        for i in range(cx):
            rhs[c, i] = stencil_inside(rows_of(src, c), i)
        for k in range(2):
            xsend[r, c, 2 + k] = weighted([(in_s[k, j], rhs[c, j]) for j in range(cx)])
        x_copy(r, c).start()

    def build_across():
        def spot(j):
            return jnp.where(cell_of == j, 1.0, 0.0)

        corner = across((spot(their_row), spot(their_row + 1)), first)
        inner = [stencil_inside(spot, j) for j in range(cx)]
        own = [in_s[k, near_row] * corner[0] + in_s[k, near_row + 1] * corner[1] for k in range(2)]
        theirs = [weighted([(near_s[k, j], inner[j]) for j in range(cx)]) for k in range(2)]
        values = [
            weighted([(schur_s[2 * gx + m, 2 * gx + k], own[k]) for k in range(2)]
                     + [(schur_s[2 * gx + m, 2 * other + k], theirs[k]) for k in range(2)])
            for m in range(2)
        ]
        lines = [
            weighted([(local_s[i, near_row], corner[0]), (local_s[i, near_row + 1], corner[1]),
                      (out_s[0, i], values[0]), (out_s[1, i], values[1])])
            for i in range(cx)
        ]
        for i in range(cx):
            line = jnp.where(sub < WIN // 2, lines[i], lines[(i + 1) % cx])
            across_x[i * WIN : (i + 1) * WIN] = jnp.where(in_group == sub, line, 0.0)
        across_w[...] = weights(across_x[...].T)

    def side_fix():
        fix_all.wait_recv()
        along_x = apply(fix_near[2].reshape(comps * cy, cz), across_w[...]).reshape(comps, cy, cz)
        after_y, before_y = fix_near[0] - fix_sent[...], fix_near[1] - fix_sent[...]
        along_y = weighted([
            (coef, pltpu.roll(jnp.where(sub < k, after_y, 0.0), cy - k, 1)
             - pltpu.roll(jnp.where(sub >= cy - k, before_y, 0.0), k, 1))
            for k, coef in ((1, C1), (2, C2), (3, C3))
        ])
        return uxy_pack[0] * along_x + uxy_pack[1] * along_y

    def tangent(r, n, src, edge, before_face, finish_src, shadow, close):
        if not r:
            zsend[r] = edge
            pl.semaphore_wait(barrier, n_gx - 1 + 4)
            start(z_copies(r))
            for c in range(comps):
                send_y(r, c, src)
            loads[2].wait()
            table_copy.start()
            loads[1].wait()
            for c in range(comps):
                send_sides(r, c, src)
            for copy in loads[3:]:
                copy.wait()
            win_copy.start()
            for m in range(2):
                for c in range(comps):
                    for i in range(cx):
                        vel[m, c, i] = time_step * base_ref[m, c, i].astype(jnp.float32)
                uz_pack[m] = packed(lambda i: vel[m, 2, i])
                if not m:
                    start(uz_copies)
            yside[...] = jnp.zeros(yside.shape, jnp.float32)
            for m in range(2):
                for i in range(cx):
                    slope_s[m, i] = stencil_inside(lambda j: in_s[m, j], i)
        else:
            finish_src()
            for i in range(cx):
                rhs[:, i] = stencil_inside(rows_of(src), i)
            for k in range(2):
                own_side[k] = weighted([(in_s[k, j], rhs[:, j]) for j in range(cx)])
        for i in range(cx):
            block = src[:, i]
            solved = weighted([(local_s[i, j], rhs[:, j]) for j in range(cx)])
            acc[:, i] = block - (
                vel[n, 2, i] * circular(block, 2) + vel[n, 1, i] * circular(block, 1) + vel[n, 0, i] * solved)
        shadow()
        face = lateral(edge)
        for c in range(comps):
            away = across([src[c, near_row + k] for k in range(2)], gx != 0)
            sides = [own_side[k, c] if r else xsend[r, c, 2 + k] for k in range(2)]
            x_copy(r, c).wait_recv()
            halo = across((xrecv[r, c, 0], xrecv[r, c, 1]), first)
            own = [
                sides[k] + in_s[k, near_row] * halo[0] + in_s[k, near_row + 1] * halo[1] for k in range(2)
            ]
            theirs = [
                xrecv[r, c, 2 + k] + near_s[k, their_row] * away[0] + near_s[k, their_row + 1] * away[1]
                for k in range(2)
            ]
            values = [
                weighted([(schur_s[2 * gx + m, 2 * gx + k], own[k]) for k in range(2)]
                         + [(schur_s[2 * gx + m, 2 * other + k], theirs[k]) for k in range(2)])
                for m in range(2)
            ]
            y_fix(r, c)
            for i in range(cx):
                acc[c, i] -= vel[n, 1, i] * yside[c, i] + vel[n, 0, i] * weighted([
                    (local_s[i, near_row], halo[0]), (local_s[i, near_row + 1], halo[1]),
                    (out_s[0, i], values[0]), (out_s[1, i], values[1])])
            if not r:
                zsend[1, c] = packed(rows_of(acc, c)) + uz_pack[0] * face[c]
                if c == comps - 1:
                    start(z_copies(1))
                send_y(1, c, acc)
                send_sides(1, c, acc)
        closing = close(face)
        if r:
            uz_both.wait_recv()
            missing = facing(uz_near) * before_face
        z_both(r).wait_recv()
        theirs = facing(zrecv.at[r])
        return closing(lateral(theirs - missing if r else theirs)), face

    def close_state(face):
        before = zsend[1]

        def closing(late):
            fix = uz_pack[0] * (late - face)
            fix_sent[...] = fix
            start(fix_copies)

            def finish():
                for i in range(cx):
                    state_one[:, i] = acc[:, i] - unpacked(fix, i)

            return before - uz_pack[0] * late, finish

        return closing

    def close_observed(face):
        groups = range(cx // WIN)
        before = None
        for g in groups:
            sums = fold([acc[:, g * WIN + k] for k in range(WIN)]).reshape(comps * cy, cz)
            both = apply(sums, seen_w[g])
            mixed[g] = both[:, :cz]
            before = both[:, cz:] if before is None else before + both[:, cz:]

        settle(0)

        def closing(late):
            flat = (uz_pack[1] * (late - face) - side_fix()).reshape(comps * cy, cz)

            edge = (before - apply(flat, fix_edge[...])).reshape(comps, cy, cz)
            for g in groups:
                mixed[g] = mixed[g] - apply(flat, fix_rows[g])

            def finish():
                for g in groups:
                    for k, t in enumerate(unfold(mixed[g].reshape(comps, cy, cz))):
                        force[:, g * WIN + k] = t

            return edge, finish

        return closing

    def adjoint(r, n, src, dst, edge, before_face, finish_src, shadow, extra):
        edge = uz_pack[n] * edge
        if before_face is None:
            zsend[r] = edge
            start(z_copies(r))
        finish_src()
        for c in range(comps):
            for i in range(cx):
                prod[c, i] = vel[n, 1, i] * src[c, i]
            send_y(r, c, prod)
            for i in range(cx):
                rhs[c, i] = vel[n, 0, i] * src[c, i]
            for k in range(2):
                xsend[r, c, k] = weighted([(local_s[j, near_row + k], rhs[c, j]) for j in range(cx)])
                xsend[r, c, 2 + k] = weighted([(out_s[k, j], rhs[c, j]) for j in range(cx)])
            x_copy(r, c).start()
        shadow()
        face = lateral(edge)
        for i in range(cx):
            held[:, i] = weighted([(local_s[j, i], rhs[:, j]) for j in range(cx)])
        for i in range(cx):
            total = src[:, i] + circular(vel[n, 2, i] * src[:, i], 2) + circular(prod[:, i], 1)
            if extra is not None:
                total = total + extra[:, i]
            acc[:, i] = total + stencil_inside(rows_of(held), i)
        for c in range(comps):
            x_copy(r, c).wait_recv()

            def solved(block):
                return [
                    weighted([(schur_s[2 * gx + k, 2 * block + m], xsend[r, c, 2 + k]) for k in range(2)]
                             + [(schur_s[2 * other + k, 2 * block + m], xrecv[r, c, 2 + k]) for k in range(2)])
                    for m in range(2)
                ]

            own, theirs = solved(gx), solved(other)
            halo = across([
                xrecv[r, c, k] + near_s[0, their_row + k] * theirs[0] + near_s[1, their_row + k] * theirs[1]
                for k in range(2)
            ], first)
            for k in range(2):
                acc[c, near_row + k] += halo[k]
            y_fix(r, c)
            for i in range(cx):
                acc[c, i] += yside[c, i] + weighted([(slope_s[m, i], own[m]) for m in range(2)])
            if before_face is None:
                own_side[0, c] = packed(rows_of(acc, c)) - face[c]
                zsend[r + 1, c] = uz_pack[n - 1] * own_side[0, c]
        if before_face is None:
            start(z_copies(r + 1))
        else:
            missing = facing(uz_near) * before_face
        settle(r - 1)
        z_both(r).wait_recv()
        theirs = facing(zrecv.at[r])
        late = lateral(theirs if before_face is None else theirs + missing)
        fix = late - face
        after = own_side[0] + late if before_face is None else None

        def finish():
            for i in range(cx):
                dst[:, i] = acc[:, i] + unpacked(fix, i)

        return after, face, finish

    def table():
        table_copy.wait_recv()
        copy = pltpu.make_async_copy(near_v, near_s, load_sem.at[8])
        copy.start()
        copy.wait()

    def observe_one():
        observe(state_one, obs)

    def tables():
        win_copy.wait_recv()
        build_blocks()
        build_edges()
        build_across()
        for c in range(2):
            uxy_pack[c] = packed(lambda i: vel[1, c, i])

    def nothing():
        pass

    loads[0].wait()
    (edge, finish), face = tangent(
        0, 0, dir_ref, packed(rows_of(dir_ref)), None, nothing, table, close_state)
    (edge, finish), face = tangent(1, 1, state_one, edge, face, finish, tables, close_observed)
    edge, face, finish = adjoint(2, 1, force, costate, edge, None, finish, observe_one, obs)
    edge, face, finish = adjoint(3, 0, costate, res_ref, edge, face, finish, nothing, dir_ref)
    finish()
    settle(3)
    win_copy.wait_send()
    uz_both.wait_send()
    fix_all.wait_send()
    table_copy.wait_send()


def solution(mesh):
    sizes = tuple(mesh.shape[name] for name in ("gx", "gy", "gz"))

    def local(direction, base_flow, local_inv, couple_in, couple_out, schur_inv,
              plane_x, slot_plane, window_inv):
        n_gx = sizes[0]
        comps, cx, cy, cz = direction.shape
        owned, count = window_inv.shape[0], window_inv.shape[3]
        wide = 3
        field = pltpu.VMEM(direction.shape, jnp.float32)

        def held(*shape):
            return pltpu.VMEM(shape, jnp.float32)

        sems = pltpu.SemaphoreType.DMA
        vmem = pl.BlockSpec(memory_space=pltpu.VMEM)
        kept = functools.partial(pltpu.with_memory_space_constraint, memory_space=pltpu.HBM)
        hbm = pl.BlockSpec(memory_space=pltpu.HBM)
        tables = (local_inv, couple_in, couple_out.T, schur_inv, plane_x, slot_plane)
        operands = tuple(map(kept, (direction, base_flow, window_inv.reshape(owned, count, count)) + tables))
        call = functools.partial(
            pl.pallas_call,
            out_shape=jax.ShapeDtypeStruct(direction.shape, jnp.float32),
            in_specs=[hbm] * 9,
            out_specs=vmem,
            compiler_params=pltpu.CompilerParams(collective_id=0, has_side_effects=True, vmem_limit_bytes=16 * 2**20),
        )
        loaded = [
            field, pltpu.VMEM(base_flow.shape, base_flow.dtype), held(owned, count, count),
        ] + [pltpu.SMEM(t.shape, t.dtype) for t in tables]
        if n_gx == 2:
            pulled = call(
                functools.partial(pair_kernel, sizes),
                scratch_shapes=loaded + [
                    held(2, cx), held(2, cx), pltpu.SMEM((2, cx), jnp.float32), pltpu.SMEM((2, cx), jnp.float32),
                ] + [field] * 9 + [
                    held(*base_flow.shape), held(2, cy, cz),
                    held(4, comps, 4, cy, cz), held(4, comps, 4, cy, cz),
                    held(4, comps, 2, wide, cx, cz), held(4, comps, 2, wide, cx, cz),
                    held(4, comps, cy, cz), held(4, 2, comps, cy, cz),
                    held(owned, count, count), held(n_gx * owned, count, cz), held(cx // WIN, count * WIN, cz),
                    pltpu.VMEM((cx // WIN, 3 * cz, 2 * cz), jnp.bfloat16),
                    pltpu.VMEM((cx // WIN, 3 * cz, cz), jnp.bfloat16), pltpu.VMEM((3 * cz, cz), jnp.bfloat16),
                    held(cx // WIN, comps * cy, cz), held(2, cy, cz),
                    held(2, comps, cy, cz), held(comps, cy, cz), held(3, comps, cy, cz),
                    held(cz, cz), pltpu.VMEM((3 * cz, cz), jnp.bfloat16), held(2, cy, cz),
                    sems((10,)), sems((1,)), sems((4,)), sems((2, comps)), sems((2, comps)), sems((4,)),
                ],
            )(*operands)
            return pulled
        pulled = call(
            functools.partial(kernel, sizes),
            scratch_shapes=loaded + [
                held(2, cx), held(2, 2, cx), pltpu.SMEM((2, 2, cx), jnp.float32),
                held(n_gx, 2, comps, cy, cz), held(2, comps, 2, cy, cz),
                sems((10,)), sems((1,)), sems((2,)), sems((2,)),
            ] + [field] * 8 + [
                held(2, comps, cx, cy, cz),
                field,
                held(4, 2, comps, 2, cy, cz),
                held(4, 2, wide, comps, cx, cz),
                held(4, 2, wide, comps, cx, cz),
                held(4, comps, cy, cz),
                held(4, 2, comps, cy, cz),
                held(4, n_gx, 2, comps, cy, cz),
                held(n_gx - 1, owned, count, count),
                held(n_gx * owned, count, cz),
                held(cx // WIN, count * WIN, cz),
                sems((4, 2)), sems((4, 2)), sems((4, 2)), sems((4, 2)), sems((4, 2)), sems((4, 2)),
                sems((4, n_gx)), sems((4, n_gx)), sems((n_gx,)), sems((n_gx,)),
            ],
        )(*operands)
        return pulled + direction

    return jax.shard_map(
        local,
        mesh=mesh,
        in_specs=(
            P(None, "gx", "gy", "gz"),
            P(None, None, "gx", "gy", "gz"),
            P("gx", None),
            P("gx", None),
            P("gx", None),
            P(),
            P(),
            P(),
            P("gx", "gy", "gz", None, None),
        ),
        out_specs=P(None, "gx", "gy", "gz"),
        check_vma=False,
    )
```

```python
import functools

import jax
import jax.numpy as jnp
from jax import lax
from jax.experimental import pallas as pl
from jax.experimental.pallas import tpu as pltpu
from jax.sharding import PartitionSpec as P

WIN = 8
time_step = 0.15
NEAR = 7.0 / 9.0
FAR = 1.0 / 36.0
C1 = 45.0 / 60.0
C2 = -9.0 / 60.0
C3 = 1.0 / 60.0
MESH = pl.DeviceIdType.MESH
high = lax.Precision.HIGHEST


def weighted(terms):
    chains = [None, None]
    for n, (coef, block) in enumerate(terms):
        part = coef * block
        chains[n % 2] = part if chains[n % 2] is None else chains[n % 2] + part
    return chains[0] if chains[1] is None else chains[0] + chains[1]


def kernel(
    sizes,
    dir_hbm, base_hbm, inv_hbm,
    local_h, in_h, out_h, schur_h, plane_h, slot_h,
    res_ref,
    dir_ref, base_ref, inv_ref, local_s, in_s, out_s, schur_s, plane_s, slot_s, in_v, near_v, near_s, esend, halo, load_sem, table_sem, ts_sem, tr_sem,
    state_one, state_two, force, acc, rhs, obs, prod_y, prod_z, hbuf,
    yside, xrecv, ysend, yrecv, zsend, zrecv, edge, winrecv, lanes_inv, blocks,
    xs_sem, xr_sem, ys_sem, yr_sem, zs_sem, zr_sem, es_sem, er_sem, ws_sem, wr_sem,
):
    n_gx, n_gy, n_gz = sizes
    gx, gy, gz = lax.axis_index("gx"), lax.axis_index("gy"), lax.axis_index("gz")
    comps, cx, cy, cz = dir_ref.shape
    wide = ysend.shape[2]
    loads = [
        pltpu.make_async_copy(src, dst, load_sem.at[n])
        for n, (src, dst) in enumerate((
            (dir_hbm, dir_ref), (in_h, in_s), (schur_h, schur_s), (local_h, local_s),
            (out_h, out_s), (plane_h, plane_s), (slot_h, slot_s),
            (base_hbm, base_ref), (inv_hbm, inv_ref), (in_h, in_v),
        ))
    ]
    owned = inv_ref.shape[0]
    y_next, y_prev = lax.rem(gy + 1, n_gy), lax.rem(gy + n_gy - 1, n_gy)
    z_next, z_prev = lax.rem(gz + 1, n_gz), lax.rem(gz + n_gz - 1, n_gz)

    @pl.when(gx == 0)
    def _():
        xrecv[:, 0] = jnp.zeros(xrecv.shape[:1] + xrecv.shape[2:], jnp.float32)

    @pl.when(gx == n_gx - 1)
    def _():
        xrecv[:, 1] = jnp.zeros(xrecv.shape[:1] + xrecv.shape[2:], jnp.float32)

    barrier = pltpu.get_barrier_semaphore()
    for d in range(1, n_gx):
        pl.semaphore_signal(barrier, device_id={"gx": lax.rem(gx + d, n_gx)}, device_id_type=MESH)
    for q in (y_prev, y_next):
        pl.semaphore_signal(barrier, device_id={"gy": q}, device_id_type=MESH)
    for q in (z_prev, z_next):
        pl.semaphore_signal(barrier, device_id={"gz": q}, device_id_type=MESH)

    for copy in loads:
        copy.start()

    def remote(src, dst, send, recv, where):
        return pltpu.make_async_remote_copy(
            src_ref=src, dst_ref=dst, send_sem=send, recv_sem=recv,
            device_id=where, device_id_type=MESH,
        )

    lane = lax.broadcasted_iota(jnp.int32, (comps, cy, cz), 2)
    sub = lax.broadcasted_iota(jnp.int32, (comps, cy, cz), 1)
    in_group = lane % WIN

    def x_copies(r, src):
        right = remote(src.at[:, cx - 2 : cx], xrecv.at[r, 0], xs_sem.at[r, 0], xr_sem.at[r, 0],
                       {"gx": lax.rem(gx + 1, n_gx)})
        left = remote(src.at[:, 0:2], xrecv.at[r, 1], xs_sem.at[r, 1], xr_sem.at[r, 1],
                      {"gx": lax.rem(gx + n_gx - 1, n_gx)})
        return right, left

    def x_start(copies):
        right, left = copies

        @pl.when(gx < n_gx - 1)
        def _():
            right.start()

        @pl.when(gx > 0)
        def _():
            left.start()

    def x_arrived(copies):
        right, left = copies

        @pl.when(gx > 0)
        def _():
            right.wait_recv()

        @pl.when(gx < n_gx - 1)
        def _():
            left.wait_recv()

    def x_sent(copies):
        right, left = copies

        @pl.when(gx < n_gx - 1)
        def _():
            right.wait_send()

        @pl.when(gx > 0)
        def _():
            left.wait_send()

    def y_copies(r):
        return (
            remote(ysend.at[r, 0], yrecv.at[r, 0], ys_sem.at[r, 0], yr_sem.at[r, 0], {"gy": y_prev}),
            remote(ysend.at[r, 1], yrecv.at[r, 1], ys_sem.at[r, 1], yr_sem.at[r, 1], {"gy": y_next}),
        )

    def z_copies(r):
        return (
            remote(zsend.at[r], zrecv.at[r, 0], zs_sem.at[r, 0], zr_sem.at[r, 0], {"gz": z_prev}),
            remote(zsend.at[r], zrecv.at[r, 1], zs_sem.at[r, 1], zr_sem.at[r, 1], {"gz": z_next}),
        )

    def edge_copies(r):
        return tuple(
            remote(edge.at[r, 0], edge.at[r, d], es_sem.at[r, d], er_sem.at[r, d],
                   {"gx": lax.rem(gx + d, n_gx)})
            for d in range(1, n_gx)
        )

    win_copies = tuple(
        remote(inv_ref, winrecv.at[d - 1], ws_sem.at[d], wr_sem.at[d], {"gx": lax.rem(gx + d, n_gx)})
        for d in range(1, n_gx)
    )

    table_copies = (
        remote(in_v, near_v.at[0], ts_sem.at[0], tr_sem.at[0], {"gx": lax.rem(gx + 1, n_gx)}),
        remote(in_v, near_v.at[1], ts_sem.at[1], tr_sem.at[1], {"gx": lax.rem(gx + n_gx - 1, n_gx)}),
    )
    left_one = jnp.where(gx > 0, 1.0, 0.0)
    right_one = jnp.where(gx < n_gx - 1, 1.0, 0.0)
    left_id, right_id = lax.rem(gx + n_gx - 1, n_gx), lax.rem(gx + 1, n_gx)

    def start(copies):
        for copy in copies:
            copy.start()

    def arrived(copies):
        for copy in copies:
            copy.wait_recv()

    def pack_y(r, src):
        lines = src.reshape(comps * cx * cy, cz)
        for c in range(comps):
            for m in range(wide):
                for side, row in ((0, m), (1, cy - wide + m)):
                    ysend[r, side, m, c] = lines[pl.ds(c * cx * cy + row, cx, stride=cy), :]

    def pack_z(r, src):
        packed = None
        for i in range(cx):
            block = src[:, i]
            turned = block if i == 0 else pltpu.roll(block, WIN * i, 2)
            if packed is None:
                packed = turned
            else:
                packed = jnp.where((lane >= WIN * i - 4) & (lane < WIN * i + 4), turned, packed)
        zsend[r] = packed

    def circular_z(block):
        def diff(k):
            return pltpu.roll(block, cz - k, 2) - pltpu.roll(block, k, 2)

        return C1 * diff(1) + C2 * diff(2) + C3 * diff(3)

    def z_fix(r):
        true = jnp.where(in_group < 4, zrecv[r, 0], zrecv[r, 1])
        delta = true - zsend[r]
        low = jnp.where(in_group >= WIN - 3, delta, 0.0)
        top = jnp.where(in_group < 3, delta, 0.0)
        low_fix = -(C1 * pltpu.roll(low, 1, 2) + C2 * pltpu.roll(low, 2, 2) + C3 * pltpu.roll(low, 3, 2))
        top_fix = (C1 * pltpu.roll(top, cz - 1, 2) + C2 * pltpu.roll(top, cz - 2, 2)
                   + C3 * pltpu.roll(top, cz - 3, 2))
        return jnp.where(in_group < 3, low_fix, 0.0) + jnp.where(in_group >= WIN - 3, top_fix, 0.0)

    def z_fix_of(fix, i):
        turned = fix if i == 0 else pltpu.roll(fix, (cz - WIN * i) % cz, 2)
        return jnp.where((lane < 3) | (lane >= cz - 3), turned, 0.0)

    def fill_sides(r):
        lines = yside.reshape(comps * cx * cy, cz)
        for c in range(comps):
            for m in range(wide):
                for side, row in ((0, m), (1, cy - wide + m)):
                    lines[pl.ds(c * cx * cy + row, cx, stride=cy), :] = yrecv[r, side, m, c]

    def along_y(block, side):
        def diff(k):
            ahead = pltpu.roll(jnp.where(sub < k, side, block), cy - k, 1)
            behind = pltpu.roll(jnp.where(sub >= cy - k, side, block), k, 1)
            return ahead - behind

        return C1 * diff(1) + C2 * diff(2) + C3 * diff(3)

    def stencil_x(src, sides, i):
        def row(n):
            if n < 0:
                return sides[0, :, n + 2]
            if n >= cx:
                return sides[1, :, n - cx]
            return src[:, n]

        return NEAR * (row(i + 1) - row(i - 1)) + FAR * (row(i + 2) - row(i - 2))

    def stencil_inside(src, i):
        total = None
        for offset, coef in ((1, NEAR), (-1, -NEAR), (2, FAR), (-2, -FAR)):
            if 0 <= i + offset < cx:
                part = coef * src[:, i + offset]
                total = part if total is None else total + part
        return total

    def velocity(n, c, i):
        return base_ref[n, c, i].astype(jnp.float32)[None]

    def fold(blocks8):
        level, m = list(blocks8), 1
        while len(level) > 1:
            keep = (lane & m) == 0
            level = [
                jnp.where(keep, a + pltpu.roll(a, cz - m, 2), b + pltpu.roll(b, m, 2))
                for a, b in zip(level[0::2], level[1::2])
            ]
            m *= 2
        return level[0]

    def unfold(block):
        level, m = [block], WIN // 2
        while m >= 1:
            keep = (lane & m) == 0
            wider = []
            for t in level:
                wider.append(jnp.where(keep, t, pltpu.roll(t, m, 2)))
                wider.append(jnp.where(keep, pltpu.roll(t, cz - m, 2), t))
            level = wider
            m //= 2
        return level

    def observe(src, dst):
        for g in range(cx // WIN):
            sums = fold([src[:, g * WIN + k] for k in range(WIN)])
            mixed = lax.dot_general(
                sums.reshape(comps * cy, cz), blocks[g], (((1,), (1,)), ((), ())),
                precision=high, preferred_element_type=jnp.float32,
            ).reshape(comps, cy, cz)
            for k, t in enumerate(unfold(mixed)):
                dst[:, g * WIN + k] = t

    def build_blocks():
        count = inv_ref.shape[2]
        spread = (
            lax.broadcasted_iota(jnp.int32, (count, cz), 1) // WIN
            == lax.broadcasted_iota(jnp.int32, (count, cz), 0)
        ).astype(jnp.float32)
        for d in range(n_gx):
            source = inv_ref[...] if d == 0 else winrecv[d - 1]
            lanes_inv[d * owned : (d + 1) * owned] = jnp.dot(
                source.reshape(owned * count, count), spread,
                precision=high, preferred_element_type=jnp.float32,
            ).reshape(owned, count, cz) * (1.0 / (WIN * WIN))
        blocks[...] = jnp.zeros(blocks.shape, jnp.float32)
        row = lax.broadcasted_iota(jnp.int32, (WIN, cz), 0)
        col = lax.broadcasted_iota(jnp.int32, (WIN, cz), 1) % WIN

        def add_slot(j, carry):
            owner = lax.rem(gx + n_gx - j // owned, n_gx)
            cell = plane_s[slot_s[owner * owned + j % owned]] - gx * cx
            for g in range(cx // WIN):
                here = (row == cell - g * WIN) & (col == cell - g * WIN)
                for s in range(count):
                    line = jnp.broadcast_to(lanes_inv[j, s : s + 1, :], (WIN, cz))
                    blocks[g, s * WIN : (s + 1) * WIN, :] += jnp.where(here, line, 0.0)
            return carry

        lax.fori_loop(0, n_gx * owned, add_slot, 0)

    def interface(r, block, m, transposed):
        terms = []
        for d in range(n_gx):
            owner = lax.rem(gx + n_gx - d, n_gx)
            for k in range(2):
                n, own = 2 * owner + k, 2 * block + m
                coef = schur_s[n, own] if transposed else schur_s[own, n]
                terms.append((coef, edge[r, d, k]))
        return weighted(terms)

    def early_copies(r):
        return tuple(
            remote(esend.at[d], edge.at[r, d], es_sem.at[r, d], er_sem.at[r, d],
                   {"gx": lax.rem(gx + d, n_gx)})
            for d in range(1, n_gx)
        )

    def early_shares(r, src):
        for i in range(cx):
            rhs[:, i] = stencil_inside(src, i)
        below = (NEAR * src[:, 0] + FAR * src[:, 1], FAR * src[:, 0])
        above = (-(NEAR * src[:, cx - 1] + FAR * src[:, cx - 2]), -FAR * src[:, cx - 1])
        parts = []
        for k in range(2):
            parts.append((2 * gx + k, weighted([(in_s[k, j], rhs[:, j]) for j in range(cx)])))
            parts.append((2 * right_id + k, right_one * (
                near_s[1, k, 0] * above[0] + near_s[1, k, 1] * above[1])))
            parts.append((2 * left_id + k, left_one * (
                near_s[0, k, cx - 1] * below[0] + near_s[0, k, cx - 2] * below[1])))
        for d in tuple(range(1, n_gx)) + (0,):
            owner = lax.rem(gx + d, n_gx)
            for m in range(2):
                share = weighted([(schur_s[2 * owner + m, n], part) for n, part in parts])
                if d == 0:
                    edge[r, 0, m] = share
                else:
                    esend[d, m] = share

    sent = []

    def tangent(r, n, src, dst, first, shadow):
        xc, yc, zc = x_copies(r, src), y_copies(r), z_copies(r)
        ec = edge_copies(r) if first else early_copies(r)
        if first:
            loads[0].wait()
        else:
            x_start(xc)
        pack_z(r, src)
        if not first:
            start(zc)
        pack_y(r, src)
        if first:
            pl.semaphore_wait(barrier, n_gx - 1 + 4)
            x_start(xc)
            start(zc)
        start(yc)
        if not first:
            early_shares(r, src)
            start(ec)
        sent.append((xc, yc + zc + ec))
        if first:
            for copy in loads[1:]:
                copy.wait()
            start(table_copies)
        for i in range(cx):
            block = src[:, i]
            acc[:, i] = block - time_step * (velocity(n, 2, i) * circular_z(block))
        x_arrived(xc)
        for i in range(cx) if first else (0, 1, cx - 2, cx - 1):
            rhs[:, i] = stencil_x(src, xrecv.at[r], i)
        if first:
            for k in range(2):
                edge[r, 0, k] = weighted([(in_s[k, j], rhs[:, j]) for j in range(cx)])
            start(ec)
            start(win_copies)
        for i in range(cx):
            solved = weighted([(local_s[i, j], rhs[:, j]) for j in range(cx)])
            acc[:, i] -= time_step * (velocity(n, 0, i) * solved)
        if first:
            arrived(table_copies)
            table = pltpu.make_async_copy(near_v, near_s, table_sem.at[0])
            table.start()
            table.wait()
        shadow()
        arrived(yc)
        fill_sides(r)
        for i in range(cx):
            acc[:, i] -= time_step * (velocity(n, 1, i) * along_y(src[:, i], yside[:, i]))
        arrived(zc)
        fix = z_fix(r)
        arrived(ec)
        if first:
            values = [interface(r, gx, m, False) for m in range(2)]
        else:
            values = [weighted([(1.0, edge[r, d, m]) for d in range(n_gx)]) for m in range(2)]
        for i in range(cx):
            pulled = out_s[0, i] * values[0] + out_s[1, i] * values[1]
            dst[:, i] = acc[:, i] - time_step * (
                velocity(n, 0, i) * pulled + velocity(n, 2, i) * z_fix_of(fix, i)
            )

    def adjoint(r, n, src, dst, extra):
        xc, yc, zc, ec = x_copies(r, hbuf.at[r - 2]), y_copies(r), z_copies(r), edge_copies(r)
        sent.append((xc, yc + zc + ec))
        held = hbuf.at[r - 2]
        for i in range(cx):
            prod_z[:, i] = velocity(n, 2, i) * src[:, i]
        pack_z(r, prod_z)
        start(zc)
        for i in range(cx):
            prod_y[:, i] = velocity(n, 1, i) * src[:, i]
        pack_y(r, prod_y)
        start(yc)
        for i in range(cx):
            rhs[:, i] = velocity(n, 0, i) * src[:, i]
        for k in range(2):
            edge[r, 0, k] = weighted([(out_s[k, i], rhs[:, i]) for i in range(cx)])
        start(ec)
        order = (0, 1, cx - 2, cx - 1) + tuple(range(2, cx - 2))
        for place, i in enumerate(order):
            held[:, i] = weighted([(local_s[j, i], rhs[:, j]) for j in range(cx)])
            if place == 3:
                x_start(xc)
        for i in range(cx):
            total = src[:, i] + time_step * circular_z(prod_z[:, i])
            acc[:, i] = total if extra is None else total + extra[:, i]
        arrived(ec)
        values = [interface(r, gx, m, True) for m in range(2)]
        lower = [left_one * interface(r, left_id, m, True) for m in range(2)]
        upper = [right_one * interface(r, right_id, m, True) for m in range(2)]
        for i in range(cx):
            rhs[:, i] = held[:, i] + (in_s[0, i] * values[0] + in_s[1, i] * values[1])
        for i in range(2, cx - 2):
            acc[:, i] += time_step * stencil_x(rhs, halo, i)
        x_arrived(xc)
        for n in range(2):
            halo[0, :, n] = xrecv[r, 0, :, n] + (
                near_s[0, 0, cx - 2 + n] * lower[0] + near_s[0, 1, cx - 2 + n] * lower[1])
            halo[1, :, n] = xrecv[r, 1, :, n] + (
                near_s[1, 0, n] * upper[0] + near_s[1, 1, n] * upper[1])
        for i in (0, 1, cx - 2, cx - 1):
            acc[:, i] += time_step * stencil_x(rhs, halo, i)
        arrived(yc)
        fill_sides(r)
        for i in range(cx):
            acc[:, i] += time_step * along_y(prod_y[:, i], yside[:, i])
        arrived(zc)
        fix = z_fix(r)
        for i in range(cx):
            dst[:, i] = acc[:, i] + time_step * z_fix_of(fix, i)

    def nothing():
        pass

    def observe_one():
        arrived(win_copies)
        build_blocks()
        observe(state_one, obs)

    tangent(0, 0, dir_ref, state_one, True, nothing)
    tangent(1, 1, state_one, state_two, False, observe_one)
    observe(state_two, force)
    adjoint(2, 1, force, state_two, obs)
    adjoint(3, 0, state_two, res_ref, None)
    for xc, rest in sent:
        x_sent(xc)
        for copy in rest:
            copy.wait_send()
    for copy in win_copies + table_copies:
        copy.wait_send()


def pair_kernel(
    sizes,
    dir_hbm, base_hbm, inv_hbm,
    local_h, in_h, out_h, schur_h, plane_h, slot_h,
    res_ref,
    dir_ref, base_ref, inv_ref, local_s, in_s, out_s, schur_s, plane_s, slot_s, in_v, near_v, near_s, slope_s,
    state_one, costate, force, acc, rhs, obs, prod, held, yside, vel, uz_pack,
    xsend, xrecv, ysend, yrecv, zsend, zrecv, winrecv, lanes_inv, blocks, seen_w, fix_rows, fix_edge, mixed, uz_near,
    own_side, fix_sent, fix_near, across_x, across_w, uxy_pack,
    load_sem, sent_sem, side_sem, xr_sem, yr_sem, zr_sem,
):
    n_gx, n_gy, n_gz = sizes
    gx, gy, gz = lax.axis_index("gx"), lax.axis_index("gy"), lax.axis_index("gz")
    comps, cx, cy, cz = dir_ref.shape
    wide = ysend.shape[3]
    owned = inv_ref.shape[0]
    other = 1 - gx
    y_next, y_prev = lax.rem(gy + 1, n_gy), lax.rem(gy + n_gy - 1, n_gy)
    z_next, z_prev = lax.rem(gz + 1, n_gz), lax.rem(gz + n_gz - 1, n_gz)
    first = gx == 0
    near_row = jnp.where(first, cx - 2, 0)
    their_row = jnp.where(first, 0, cx - 2)

    barrier = pltpu.get_barrier_semaphore()
    for q in (z_prev, z_next):
        pl.semaphore_signal(barrier, device_id={"gz": q}, device_id_type=MESH)
    pl.semaphore_signal(barrier, device_id={"gx": other}, device_id_type=MESH)
    for q in (y_prev, y_next):
        pl.semaphore_signal(barrier, device_id={"gy": q}, device_id_type=MESH)

    loads = [
        pltpu.make_async_copy(src, dst, load_sem.at[n])
        for n, (src, dst) in enumerate((
            (dir_hbm, dir_ref), (in_h, in_s), (in_h, in_v), (base_hbm, base_ref), (local_h, local_s),
            (schur_h, schur_s), (out_h, out_s), (plane_h, plane_s), (slot_h, slot_s), (inv_hbm, inv_ref),
        ))
    ]
    for copy in loads:
        copy.start()

    def remote(src, dst, send, recv, where):
        return pltpu.make_async_remote_copy(
            src_ref=src, dst_ref=dst, send_sem=send, recv_sem=recv,
            device_id=where, device_id_type=MESH,
        )

    x_sent = [load_sem.at[n] for n in (1, 7, 1, 7)]
    y_sent = [sent_sem.at[0], load_sem.at[6]] * 2
    z_sent = [load_sem.at[n] for n in (0, 5, 0, 8)]

    def x_copy(r, c):
        return remote(xsend.at[r, c], xrecv.at[r, c], x_sent[r], xr_sem.at[r % 2, c], {"gx": other})

    def x_all(r):
        return remote(xsend.at[r], xrecv.at[r], x_sent[r], xr_sem.at[r % 2, 0], {"gx": other})

    def y_copies(r, c):
        return tuple(
            remote(ysend.at[r, c, d], yrecv.at[r, c, d], y_sent[r], yr_sem.at[r % 2, c], {"gy": q})
            for d, q in enumerate((y_prev, y_next))
        )

    def z_copies(r):
        return tuple(
            remote(zsend.at[r], zrecv.at[r, d], z_sent[r], zr_sem.at[r], {"gz": q})
            for d, q in enumerate((z_prev, z_next))
        )

    uz_copies = tuple(
        remote(uz_pack.at[0], uz_near.at[d], load_sem.at[4], side_sem.at[2], {"gz": q})
        for d, q in enumerate((z_prev, z_next))
    )
    uz_both = remote(uz_near, uz_near, load_sem.at[4], side_sem.at[2], {"gz": z_next})

    fix_copies = tuple(
        remote(fix_sent, fix_near.at[d], load_sem.at[9], side_sem.at[3], where)
        for d, where in enumerate(({"gy": y_prev}, {"gy": y_next}, {"gx": other}))
    )
    fix_all = remote(fix_near, fix_near, load_sem.at[9], side_sem.at[3], {"gx": other})

    def y_both(r, c):
        return remote(yrecv.at[r, c], yrecv.at[r, c], y_sent[r], yr_sem.at[r % 2, c], {"gy": y_next})

    def y_all(r):
        return remote(yrecv.at[r], yrecv.at[r], y_sent[r], yr_sem.at[r % 2, 0], {"gy": y_next})

    def z_both(r):
        return remote(zrecv.at[r], zrecv.at[r], z_sent[r], zr_sem.at[r], {"gz": z_next})

    def settle(r):
        if r >= 0:
            x_all(r).wait_send()
            y_all(r).wait_send()
            z_both(r).wait_send()

    win_copy = remote(inv_ref, winrecv, load_sem.at[3], side_sem.at[0], {"gx": other})
    table_copy = remote(in_v, near_v, load_sem.at[2], side_sem.at[1], {"gx": other})

    lane = lax.broadcasted_iota(jnp.int32, (cy, cz), 1)
    in_group = lane % WIN
    cell_of = ((lane + WIN // 2) // WIN) % cx
    sub = lax.broadcasted_iota(jnp.int32, (cy, cz), 0)
    near_edge = (lane < 3) | (lane >= cz - 3)
    left, right = in_group < 3, in_group >= WIN - 3
    ahead = in_group < WIN // 2

    def packed(block_of):
        total = None
        for i in range(cx):
            block = block_of(i)
            turned = block if i == 0 else pltpu.roll(block, WIN * i, block.ndim - 1)
            total = turned if total is None else jnp.where(cell_of == i, turned, total)
        return total

    def unpacked(block, i):
        turned = block if i == 0 else pltpu.roll(block, (cz - WIN * i) % cz, 2)
        return jnp.where(near_edge, turned, 0.0)

    def send_y(r, c, src):
        lines = src.reshape(comps * cx * cy, cz)
        for side, begin in ((0, 0), (1, cy - wide)):
            for m in range(wide):
                ysend[r, c, side, m] = lines[pl.ds(c * cx * cy + begin + m, cx, stride=cy), :]
        start(y_copies(r, c))

    def circular(block, axis):
        size = block.shape[axis]

        def diff(k):
            return pltpu.roll(block, size - k, axis) - pltpu.roll(block, k, axis)

        return C1 * diff(1) + C2 * diff(2) + C3 * diff(3)

    def lateral(edge):
        low = jnp.where(right, edge, 0.0)
        top = jnp.where(left, edge, 0.0)
        low_fix = -(C1 * pltpu.roll(low, 1, 2) + C2 * pltpu.roll(low, 2, 2) + C3 * pltpu.roll(low, 3, 2))
        top_fix = (C1 * pltpu.roll(top, cz - 1, 2) + C2 * pltpu.roll(top, cz - 2, 2)
                   + C3 * pltpu.roll(top, cz - 3, 2))
        return jnp.where(left, low_fix, jnp.where(right, top_fix, 0.0))

    def facing(pair):
        return jnp.where(ahead, pair[0], pair[1])

    def y_fix(r, c):
        y_both(r, c).wait_recv()
        lines = yside.reshape(comps * cx * cy, cz)

        def put(row, value):
            lines[pl.ds(c * cx * cy + row, cx, stride=cy), :] = value

        d0, d1, d2 = (yrecv[r, c, 0, m] - ysend[r, c, 0, m] for m in range(3))
        put(cy - 1, C1 * d0 + C2 * d1 + C3 * d2)
        put(cy - 2, C2 * d0 + C3 * d1)
        put(cy - 3, C3 * d0)
        d0, d1, d2 = (yrecv[r, c, 1, m] - ysend[r, c, 1, m] for m in range(3))
        put(0, -(C1 * d2 + C2 * d1 + C3 * d0))
        put(1, -(C2 * d2 + C3 * d1))
        put(2, -(C3 * d2))

    def stencil_inside(row, i):
        total = None
        for step, coef in ((1, NEAR), (2, FAR)):
            up, down = i + step < cx, i - step >= 0
            if up and down:
                part = coef * (row(i + step) - row(i - step))
            elif up:
                part = coef * row(i + step)
            elif down:
                part = -coef * row(i - step)
            else:
                continue
            total = part if total is None else total + part
        return total

    def rows_of(ref, c=slice(None)):
        return lambda i: ref[c, i]

    def across(pair, to_first):
        low, high = pair
        upper = (FAR * low, NEAR * low + FAR * high)
        lower = (-(NEAR * high + FAR * low), -FAR * high)
        return tuple(jnp.where(to_first, u, d) for u, d in zip(upper, lower))

    def fold(blocks8):
        level, m = list(blocks8), 1
        while len(level) > 1:
            keep = (lane & m) == 0
            level = [
                jnp.where(keep, a + pltpu.roll(a, cz - m, 2), b + pltpu.roll(b, m, 2))
                for a, b in zip(level[0::2], level[1::2])
            ]
            m *= 2
        return level[0]

    def unfold(block):
        level, m = [block], WIN // 2
        while m >= 1:
            keep = (lane & m) == 0
            wider = []
            for t in level:
                wider.append(jnp.where(keep, t, pltpu.roll(t, m, 2)))
                wider.append(jnp.where(keep, pltpu.roll(t, cz - m, 2), t))
            level = wider
            m //= 2
        return level

    def product(a, b, side):
        return lax.dot_general(
            a, b, (((1,), (side,)), ((), ())), precision=high, preferred_element_type=jnp.float32)

    def parts(a):
        high_part = a.astype(jnp.bfloat16)
        return high_part, (a - high_part.astype(jnp.float32)).astype(jnp.bfloat16)

    def weights(a):
        one, two = parts(a)
        return jnp.concatenate([one, two, one], axis=0)

    def apply(a, stacked):
        one, two = parts(a)
        return jnp.dot(
            jnp.concatenate([one, one, two], axis=1), stacked, preferred_element_type=jnp.float32)

    def build_edges():
        count = inv_ref.shape[2]
        place = lax.broadcasted_iota(jnp.int32, (cz, cz), 0)
        column = lax.broadcasted_iota(jnp.int32, (cz, cz), 1)
        cell = ((place + WIN // 2) // WIN) % cx
        target = cell % WIN + jnp.where(place % WIN < WIN // 2, 0, (count - 1) * WIN)
        total = None
        for g in range(cx // WIN):
            chosen = ((cell // WIN == g) & (column == target)).astype(jnp.float32)
            turned = blocks[g].T
            onto_edge = product(turned, chosen, 1)
            seen_w[g, :, :cz] = weights(turned)
            seen_w[g, :, cz:] = weights(onto_edge)
            fix_rows[g] = weights(product(chosen, turned, 0))
            part = product(chosen, onto_edge, 0)
            total = part if total is None else total + part
        fix_edge[...] = weights(total)

    def observe(src, dst):
        for g in range(cx // WIN):
            sums = fold([src[:, g * WIN + k] for k in range(WIN)])
            total = apply(sums.reshape(comps * cy, cz), seen_w[g, :, :cz]).reshape(comps, cy, cz)
            for k, t in enumerate(unfold(total)):
                dst[:, g * WIN + k] = t

    def build_blocks():
        count = inv_ref.shape[2]
        spread = (
            lax.broadcasted_iota(jnp.int32, (count, cz), 1) // WIN
            == lax.broadcasted_iota(jnp.int32, (count, cz), 0)
        ).astype(jnp.float32)
        for d, source in enumerate((inv_ref, winrecv)):
            lanes_inv[d * owned : (d + 1) * owned] = jnp.dot(
                source[...].reshape(owned * count, count), spread,
                precision=high, preferred_element_type=jnp.float32,
            ).reshape(owned, count, cz) * (1.0 / (WIN * WIN))
        blocks[...] = jnp.zeros(blocks.shape, jnp.float32)
        row = lax.broadcasted_iota(jnp.int32, (WIN, cz), 0)
        col = lax.broadcasted_iota(jnp.int32, (WIN, cz), 1) % WIN

        def add_slot(j, carry):
            owner = jnp.where(j < owned, gx, other)
            cell = plane_s[slot_s[owner * owned + j % owned]] - gx * cx
            for g in range(cx // WIN):
                here = (row == cell - g * WIN) & (col == cell - g * WIN)
                for s in range(count):
                    line = jnp.broadcast_to(lanes_inv[j, s : s + 1, :], (WIN, cz))
                    blocks[g, s * WIN : (s + 1) * WIN, :] += jnp.where(here, line, 0.0)
            return carry

        lax.fori_loop(0, n_gx * owned, add_slot, 0)

    def start(copies):
        for copy in copies:
            copy.start()

    def send_sides(r, c, src):
        xsend[r, c, 0:2] = src[c, pl.ds(near_row, 2)]
        for i in range(cx):
            rhs[c, i] = stencil_inside(rows_of(src, c), i)
        for k in range(2):
            xsend[r, c, 2 + k] = weighted([(in_s[k, j], rhs[c, j]) for j in range(cx)])
        x_copy(r, c).start()

    def build_across():
        def spot(j):
            return jnp.where(cell_of == j, 1.0, 0.0)

        corner = across((spot(their_row), spot(their_row + 1)), first)
        inner = [stencil_inside(spot, j) for j in range(cx)]
        own = [in_s[k, near_row] * corner[0] + in_s[k, near_row + 1] * corner[1] for k in range(2)]
        theirs = [weighted([(near_s[k, j], inner[j]) for j in range(cx)]) for k in range(2)]
        values = [
            weighted([(schur_s[2 * gx + m, 2 * gx + k], own[k]) for k in range(2)]
                     + [(schur_s[2 * gx + m, 2 * other + k], theirs[k]) for k in range(2)])
            for m in range(2)
        ]
        lines = [
            weighted([(local_s[i, near_row], corner[0]), (local_s[i, near_row + 1], corner[1]),
                      (out_s[0, i], values[0]), (out_s[1, i], values[1])])
            for i in range(cx)
        ]
        for i in range(cx):
            line = jnp.where(sub < WIN // 2, lines[i], lines[(i + 1) % cx])
            across_x[i * WIN : (i + 1) * WIN] = jnp.where(in_group == sub, line, 0.0)
        across_w[...] = weights(across_x[...].T)

    def side_fix():
        fix_all.wait_recv()
        along_x = apply(fix_near[2].reshape(comps * cy, cz), across_w[...]).reshape(comps, cy, cz)
        after_y, before_y = fix_near[0] - fix_sent[...], fix_near[1] - fix_sent[...]
        along_y = weighted([
            (coef, pltpu.roll(jnp.where(sub < k, after_y, 0.0), cy - k, 1)
             - pltpu.roll(jnp.where(sub >= cy - k, before_y, 0.0), k, 1))
            for k, coef in ((1, C1), (2, C2), (3, C3))
        ])
        return uxy_pack[0] * along_x + uxy_pack[1] * along_y

    def tangent(r, n, src, edge, before_face, finish_src, shadow, close):
        if not r:
            zsend[r] = edge
            pl.semaphore_wait(barrier, n_gx - 1 + 4)
            start(z_copies(r))
            for c in range(comps):
                send_y(r, c, src)
            loads[2].wait()
            table_copy.start()
            loads[1].wait()
            for c in range(comps):
                send_sides(r, c, src)
            for copy in loads[3:]:
                copy.wait()
            win_copy.start()
            for m in range(2):
                for c in range(comps):
                    for i in range(cx):
                        vel[m, c, i] = time_step * base_ref[m, c, i].astype(jnp.float32)
                uz_pack[m] = packed(lambda i: vel[m, 2, i])
                if not m:
                    start(uz_copies)
            yside[...] = jnp.zeros(yside.shape, jnp.float32)
            for m in range(2):
                for i in range(cx):
                    slope_s[m, i] = stencil_inside(lambda j: in_s[m, j], i)
        else:
            finish_src()
            for i in range(cx):
                rhs[:, i] = stencil_inside(rows_of(src), i)
            for k in range(2):
                own_side[k] = weighted([(in_s[k, j], rhs[:, j]) for j in range(cx)])
        for i in range(cx):
            block = src[:, i]
            solved = weighted([(local_s[i, j], rhs[:, j]) for j in range(cx)])
            acc[:, i] = block - (
                vel[n, 2, i] * circular(block, 2) + vel[n, 1, i] * circular(block, 1) + vel[n, 0, i] * solved)
        shadow()
        face = lateral(edge)
        for c in range(comps):
            away = across([src[c, near_row + k] for k in range(2)], gx != 0)
            sides = [own_side[k, c] if r else xsend[r, c, 2 + k] for k in range(2)]
            x_copy(r, c).wait_recv()
            halo = across((xrecv[r, c, 0], xrecv[r, c, 1]), first)
            own = [
                sides[k] + in_s[k, near_row] * halo[0] + in_s[k, near_row + 1] * halo[1] for k in range(2)
            ]
            theirs = [
                xrecv[r, c, 2 + k] + near_s[k, their_row] * away[0] + near_s[k, their_row + 1] * away[1]
                for k in range(2)
            ]
            values = [
                weighted([(schur_s[2 * gx + m, 2 * gx + k], own[k]) for k in range(2)]
                         + [(schur_s[2 * gx + m, 2 * other + k], theirs[k]) for k in range(2)])
                for m in range(2)
            ]
            y_fix(r, c)
            for i in range(cx):
                acc[c, i] -= vel[n, 1, i] * yside[c, i] + vel[n, 0, i] * weighted([
                    (local_s[i, near_row], halo[0]), (local_s[i, near_row + 1], halo[1]),
                    (out_s[0, i], values[0]), (out_s[1, i], values[1])])
            if not r:
                zsend[1, c] = packed(rows_of(acc, c)) + uz_pack[0] * face[c]
                if c == comps - 1:
                    start(z_copies(1))
                send_sides(1, c, acc)
                send_y(1, c, acc)
        closing = close(face)
        if r:
            uz_both.wait_recv()
            missing = facing(uz_near) * before_face
        z_both(r).wait_recv()
        theirs = facing(zrecv.at[r])
        return closing(lateral(theirs - missing if r else theirs)), face

    def close_state(face):
        before = zsend[1]

        def closing(late):
            fix = uz_pack[0] * (late - face)
            fix_sent[...] = fix
            start(fix_copies)

            def finish():
                for i in range(cx):
                    state_one[:, i] = acc[:, i] - unpacked(fix, i)

            return before - uz_pack[0] * late, finish

        return closing

    def close_observed(face):
        groups = range(cx // WIN)
        before = None
        for g in groups:
            sums = fold([acc[:, g * WIN + k] for k in range(WIN)]).reshape(comps * cy, cz)
            both = apply(sums, seen_w[g])
            mixed[g] = both[:, :cz]
            before = both[:, cz:] if before is None else before + both[:, cz:]

        settle(0)

        def closing(late):
            flat = (uz_pack[1] * (late - face) - side_fix()).reshape(comps * cy, cz)

            edge = (before - apply(flat, fix_edge[...])).reshape(comps, cy, cz)
            for g in groups:
                mixed[g] = mixed[g] - apply(flat, fix_rows[g])

            def finish():
                for g in groups:
                    for k, t in enumerate(unfold(mixed[g].reshape(comps, cy, cz))):
                        force[:, g * WIN + k] = t

            return edge, finish

        return closing

    def adjoint(r, n, src, dst, edge, before_face, finish_src, shadow, extra):
        edge = uz_pack[n] * edge
        if before_face is None:
            zsend[r] = edge
            start(z_copies(r))
        finish_src()
        for c in range(comps):
            for i in range(cx):
                rhs[c, i] = vel[n, 0, i] * src[c, i]
            for k in range(2):
                xsend[r, c, k] = weighted([(local_s[j, near_row + k], rhs[c, j]) for j in range(cx)])
                xsend[r, c, 2 + k] = weighted([(out_s[k, j], rhs[c, j]) for j in range(cx)])
            x_copy(r, c).start()
            for i in range(cx):
                prod[c, i] = vel[n, 1, i] * src[c, i]
            send_y(r, c, prod)
        shadow()
        face = lateral(edge)
        for i in range(cx):
            held[:, i] = weighted([(local_s[j, i], rhs[:, j]) for j in range(cx)])
        for i in range(cx):
            total = src[:, i] + circular(vel[n, 2, i] * src[:, i], 2) + circular(prod[:, i], 1)
            if extra is not None:
                total = total + extra[:, i]
            acc[:, i] = total + stencil_inside(rows_of(held), i)
        for c in range(comps):
            x_copy(r, c).wait_recv()

            def solved(block):
                return [
                    weighted([(schur_s[2 * gx + k, 2 * block + m], xsend[r, c, 2 + k]) for k in range(2)]
                             + [(schur_s[2 * other + k, 2 * block + m], xrecv[r, c, 2 + k]) for k in range(2)])
                    for m in range(2)
                ]

            own, theirs = solved(gx), solved(other)
            halo = across([
                xrecv[r, c, k] + near_s[0, their_row + k] * theirs[0] + near_s[1, their_row + k] * theirs[1]
                for k in range(2)
            ], first)
            for k in range(2):
                acc[c, near_row + k] += halo[k]
            y_fix(r, c)
            for i in range(cx):
                acc[c, i] += yside[c, i] + weighted([(slope_s[m, i], own[m]) for m in range(2)])
            if before_face is None:
                own_side[0, c] = packed(rows_of(acc, c)) - face[c]
                zsend[r + 1, c] = uz_pack[n - 1] * own_side[0, c]
        if before_face is None:
            start(z_copies(r + 1))
        else:
            missing = facing(uz_near) * before_face
        settle(r - 1)
        z_both(r).wait_recv()
        theirs = facing(zrecv.at[r])
        late = lateral(theirs if before_face is None else theirs + missing)
        fix = late - face
        after = own_side[0] + late if before_face is None else None

        def finish():
            for i in range(cx):
                dst[:, i] = acc[:, i] + unpacked(fix, i)

        return after, face, finish

    def table():
        table_copy.wait_recv()
        copy = pltpu.make_async_copy(near_v, near_s, load_sem.at[8])
        copy.start()
        copy.wait()

    def observe_one():
        observe(state_one, obs)

    def tables():
        win_copy.wait_recv()
        build_blocks()
        build_edges()
        build_across()
        for c in range(2):
            uxy_pack[c] = packed(lambda i: vel[1, c, i])

    def nothing():
        pass

    loads[0].wait()
    (edge, finish), face = tangent(
        0, 0, dir_ref, packed(rows_of(dir_ref)), None, nothing, table, close_state)
    (edge, finish), face = tangent(1, 1, state_one, edge, face, finish, tables, close_observed)
    edge, face, finish = adjoint(2, 1, force, costate, edge, None, finish, observe_one, obs)
    edge, face, finish = adjoint(3, 0, costate, res_ref, edge, face, finish, nothing, dir_ref)
    finish()
    settle(3)
    win_copy.wait_send()
    uz_both.wait_send()
    fix_all.wait_send()
    table_copy.wait_send()


def solution(mesh):
    sizes = tuple(mesh.shape[name] for name in ("gx", "gy", "gz"))

    def local(direction, base_flow, local_inv, couple_in, couple_out, schur_inv,
              plane_x, slot_plane, window_inv):
        n_gx = sizes[0]
        comps, cx, cy, cz = direction.shape
        owned, count = window_inv.shape[0], window_inv.shape[3]
        wide = 3
        field = pltpu.VMEM(direction.shape, jnp.float32)

        def held(*shape):
            return pltpu.VMEM(shape, jnp.float32)

        sems = pltpu.SemaphoreType.DMA
        vmem = pl.BlockSpec(memory_space=pltpu.VMEM)
        kept = functools.partial(pltpu.with_memory_space_constraint, memory_space=pltpu.HBM)
        hbm = pl.BlockSpec(memory_space=pltpu.HBM)
        tables = (local_inv, couple_in, couple_out.T, schur_inv, plane_x, slot_plane)
        operands = tuple(map(kept, (direction, base_flow, window_inv.reshape(owned, count, count)) + tables))
        call = functools.partial(
            pl.pallas_call,
            out_shape=jax.ShapeDtypeStruct(direction.shape, jnp.float32),
            in_specs=[hbm] * 9,
            out_specs=vmem,
            compiler_params=pltpu.CompilerParams(collective_id=0, has_side_effects=True, vmem_limit_bytes=16 * 2**20),
        )
        loaded = [
            field, pltpu.VMEM(base_flow.shape, base_flow.dtype), held(owned, count, count),
        ] + [pltpu.SMEM(t.shape, t.dtype) for t in tables]
        if n_gx == 2:
            pulled = call(
                functools.partial(pair_kernel, sizes),
                scratch_shapes=loaded + [
                    held(2, cx), held(2, cx), pltpu.SMEM((2, cx), jnp.float32), pltpu.SMEM((2, cx), jnp.float32),
                ] + [field] * 9 + [
                    held(*base_flow.shape), held(2, cy, cz),
                    held(4, comps, 4, cy, cz), held(4, comps, 4, cy, cz),
                    held(4, comps, 2, wide, cx, cz), held(4, comps, 2, wide, cx, cz),
                    held(4, comps, cy, cz), held(4, 2, comps, cy, cz),
                    held(owned, count, count), held(n_gx * owned, count, cz), held(cx // WIN, count * WIN, cz),
                    pltpu.VMEM((cx // WIN, 3 * cz, 2 * cz), jnp.bfloat16),
                    pltpu.VMEM((cx // WIN, 3 * cz, cz), jnp.bfloat16), pltpu.VMEM((3 * cz, cz), jnp.bfloat16),
                    held(cx // WIN, comps * cy, cz), held(2, cy, cz),
                    held(2, comps, cy, cz), held(comps, cy, cz), held(3, comps, cy, cz),
                    held(cz, cz), pltpu.VMEM((3 * cz, cz), jnp.bfloat16), held(2, cy, cz),
                    sems((10,)), sems((1,)), sems((4,)), sems((2, comps)), sems((2, comps)), sems((4,)),
                ],
            )(*operands)
            return pulled
        pulled = call(
            functools.partial(kernel, sizes),
            scratch_shapes=loaded + [
                held(2, cx), held(2, 2, cx), pltpu.SMEM((2, 2, cx), jnp.float32),
                held(n_gx, 2, comps, cy, cz), held(2, comps, 2, cy, cz),
                sems((10,)), sems((1,)), sems((2,)), sems((2,)),
            ] + [field] * 8 + [
                held(2, comps, cx, cy, cz),
                field,
                held(4, 2, comps, 2, cy, cz),
                held(4, 2, wide, comps, cx, cz),
                held(4, 2, wide, comps, cx, cz),
                held(4, comps, cy, cz),
                held(4, 2, comps, cy, cz),
                held(4, n_gx, 2, comps, cy, cz),
                held(n_gx - 1, owned, count, count),
                held(n_gx * owned, count, cz),
                held(cx // WIN, count * WIN, cz),
                sems((4, 2)), sems((4, 2)), sems((4, 2)), sems((4, 2)), sems((4, 2)), sems((4, 2)),
                sems((4, n_gx)), sems((4, n_gx)), sems((n_gx,)), sems((n_gx,)),
            ],
        )(*operands)
        return pulled + direction

    return jax.shard_map(
        local,
        mesh=mesh,
        in_specs=(
            P(None, "gx", "gy", "gz"),
            P(None, None, "gx", "gy", "gz"),
            P("gx", None),
            P("gx", None),
            P("gx", None),
            P(),
            P(),
            P(),
            P("gx", "gy", "gz", None, None),
        ),
        out_specs=P(None, "gx", "gy", "gz"),
        check_vma=False,
    )
```
